256 devices in a mesh: row: 8 (over x, core), col: 32 (over y, z).
Axes of the slice: x: 4, y: 4, z: 8, core: 2. Of those that a mesh axis runs over, the one named last changes fastest.
Arguments:
- frames: bfloat16 [3072, 4096], P('row', 'col'), may hold values from -6 to 6
- gain: float32 [4096], replicated, may hold values from 0.3 to 10
- w_value: bfloat16 [4096, 4096], P('row', 'col'), may hold values from -0.09375 to 0.09375
- w_gate: bfloat16 [4096, 4096], P('row', 'col'), may hold values from -0.09375 to 0.09375
- kernel: float32 [31, 4096], P(None, 'col'), may hold values from -1.5 to 1.5
- bias: float32 [4096], P('col'), may hold values from -3 to 3
- w_out: bfloat16 [4096, 4096], P('row', 'col'), may hold values from -0.09375 to 0.09375
- grad_out: bfloat16 [3072, 4096], P('row', 'col'), may hold values from -6 to 6
Outputs:
- encoded: bfloat16 [3072, 4096], P('row', 'col')
- input_grad: bfloat16 [3072, 4096], P('row', 'col')
- grad_value: float32 [4096, 4096], P('row', 'col')
- grad_gate: float32 [4096, 4096], P('row', 'col')
- grad_kernel: float32 [31, 4096], P(None, 'col')
- grad_bias: float32 [4096], P('col')
- grad_out_weight: float32 [4096, 4096], P('row', 'col')
- grad_gain: float32 [4096], P('col')
The draws below stay inside these ranges and needn't reach their ends.
All inputs are finite; a program needn't handle non-finite values.
Results may differ from the reference program's by a relative error of at most 0.035.
Values may be sent and summed in bfloat16 or wider, within the bound.
No kernel may reach another device: no remote copies, remote signals or barrier semaphores. Data moves between devices by JAX's collectives and lax.ppermute only.
A program may use at most 128 MiB of HBM per device.

```python
import math
import jax
import jax.numpy as jnp
from jax import lax

D = 4096
F = 4096
K = 31
LEN = 2048
TOTAL = 3072
N_COL = 32


def draw_gain(key, part):
    place = jnp.arange(D, dtype=jnp.float32) / D
    rough = jnp.exp(jax.random.uniform(jax.random.fold_in(key, 11), (D,), jnp.float32, math.log(0.7), math.log(1.5)))
    ramp = jnp.exp(math.log(4.0) * place)
    return (0.5 * ramp * rough).astype(jnp.float32)


def block_scale(own_key, extent, cuts, smallest, high):
    def one(dim, blocks):
        draws = jax.random.uniform(jax.random.fold_in(jax.random.fold_in(own_key, 6), dim), (blocks,), jnp.float32, smallest / len(cuts), high / len(cuts))
        return jnp.repeat(jnp.exp(draws), extent[dim] // blocks).reshape((-1,) + (1,) * (len(extent) - dim - 1))

    loudness = one(*cuts[0])
    for cut in cuts[1:]:
        loudness = loudness * one(*cut)
    return loudness


def gaussian(key, dims, scale, bound, cuts=(), kind=jnp.bfloat16):
    array = scale * jax.random.normal(key, dims, jnp.float32)
    if cuts:
        array = array * block_scale(key, dims, cuts, -0.22, 0.18)
    return jnp.clip(array, -bound, bound).astype(kind)


def setup_inputs(seed: int = 0) -> dict:
    keys = jax.random.split(jax.random.key(seed), 9)
    return {
        "frames": gaussian(keys[0], (TOTAL, D), 1.0, 6.0, ((0, 8), (1, 32))),
        "gain": draw_gain(jax.random.fold_in(keys[8], 71), 0),
        "w_value": gaussian(keys[2], (D, F), D ** -0.5, 0.09375, ((0, 8), (1, 32))),
        "w_gate": gaussian(keys[3], (D, F), D ** -0.5, 0.09375, ((0, 8), (1, 32))),
        "kernel": gaussian(keys[4], (K, F), 0.25, 1.5, ((1, 32),), jnp.float32),
        "bias": gaussian(keys[5], (F,), 0.5, 3.0, ((0, 32),), jnp.float32),
        "w_out": gaussian(keys[6], (F, D), F ** -0.5, 0.09375, ((0, 8), (1, 32))),
        "grad_out": gaussian(keys[7], (TOTAL, D), 1.0, 6.0, ((0, 8), (1, 32))),
    }


epsilon = 1e-05

def tap_masks(positions):
    offsets = jnp.arange(K, dtype=jnp.int32) - K // 2
    placed = (positions % LEN)[None, :] + offsets[:, None]
    return ((placed >= 0) & (placed < LEN)).astype(jnp.float32)

def contract_rows(left, right):
    return lax.dot_general(left, right, (((0,), (0,)), ((), ())), preferred_element_type=jnp.float32)

def contract_cols(left, right):
    return lax.dot_general(left, right, (((1,), (1,)), ((), ())), preferred_element_type=jnp.float32)

def reference(frames, gain, w_value, w_gate, kernel, bias, w_out, grad_out):
    total = frames.shape[0]
    width = frames.shape[1]
    channels = w_value.shape[1]
    half_width = K // 2
    wide = frames.astype(jnp.float32)
    mean_row = lax.optimization_barrier(jnp.sum(wide, axis=1)) / width
    inv_std = lax.rsqrt(lax.optimization_barrier(jnp.sum(wide * wide, axis=1)) / width - mean_row * mean_row + epsilon)
    centred = (wide - mean_row[:, None]) * inv_std[:, None]
    normed = (centred * gain[None, :]).astype(jnp.bfloat16)
    value_pre = jnp.dot(normed, w_value, preferred_element_type=jnp.float32)
    gate_pre = jnp.dot(normed, w_gate, preferred_element_type=jnp.float32)
    gate_sig = jax.nn.sigmoid(gate_pre)
    gated = (value_pre * gate_sig).astype(jnp.bfloat16)
    masks = tap_masks(jnp.arange(total, dtype=jnp.int32))
    padded_glu = jnp.pad(gated.astype(jnp.float32), ((half_width, half_width), (0, 0)))
    conv_pre = jnp.zeros((total, channels), jnp.float32) + bias[None, :]
    for tap_index in range(K):
        conv_pre = conv_pre + kernel[tap_index][None, :] * masks[tap_index][:, None] * padded_glu[tap_index:tap_index + total]
    conv_sig = jax.nn.sigmoid(conv_pre)
    activated = (conv_pre * conv_sig).astype(jnp.bfloat16)
    encoded = (wide + jnp.dot(activated, w_out, preferred_element_type=jnp.float32)).astype(jnp.bfloat16)
    feat_block = width // N_COL

    def act_step(carry, index):
        grad_part = lax.dynamic_slice_in_dim(grad_out, index * feat_block, feat_block, 1)
        weight_part = lax.dynamic_slice_in_dim(w_out, index * feat_block, feat_block, 1)
        part = contract_cols(grad_part, weight_part)
        return (carry + lax.optimization_barrier(part.astype(jnp.bfloat16)).astype(jnp.float32), None)
    act_grad, unused = lax.scan(act_step, jnp.zeros((total, channels), jnp.float32), jnp.arange(N_COL, dtype=jnp.int32))
    grad_out_weight = contract_rows(activated, grad_out)
    conv_grad = (act_grad * conv_sig * (1.0 + conv_pre * (1.0 - conv_sig))).astype(jnp.bfloat16)
    conv_wide = conv_grad.astype(jnp.float32)
    glu_grad = jnp.zeros((total, channels), jnp.float32)
    kernel_rows = []
    for tap_index in range(K):
        masked = jnp.pad(masks[tap_index][:, None] * conv_wide, ((half_width, half_width), (0, 0)))
        begin = 2 * half_width - tap_index
        glu_grad = glu_grad + kernel[tap_index][None, :] * masked[begin:begin + total]
        kernel_rows.append(lax.optimization_barrier(jnp.sum(masks[tap_index][:, None] * conv_wide * padded_glu[tap_index:tap_index + total], axis=0)))
    grad_kernel = jnp.stack(kernel_rows)
    grad_bias = lax.optimization_barrier(jnp.sum(conv_wide, axis=0))
    value_grad = (glu_grad * gate_sig).astype(jnp.bfloat16)
    gate_grad = (glu_grad * value_pre * gate_sig * (1.0 - gate_sig)).astype(jnp.bfloat16)
    grad_value = contract_rows(normed, value_grad)
    grad_gate = contract_rows(normed, gate_grad)
    chan_block = channels // N_COL

    def norm_step(carry, index):
        value_part = lax.dynamic_slice_in_dim(value_grad, index * chan_block, chan_block, 1)
        gate_part = lax.dynamic_slice_in_dim(gate_grad, index * chan_block, chan_block, 1)
        wv_part = lax.dynamic_slice_in_dim(w_value, index * chan_block, chan_block, 1)
        wg_part = lax.dynamic_slice_in_dim(w_gate, index * chan_block, chan_block, 1)
        part = contract_cols(value_part, wv_part) + contract_cols(gate_part, wg_part)
        return (carry + lax.optimization_barrier(part.astype(jnp.bfloat16)).astype(jnp.float32), None)
    normed_grad, unused = lax.scan(norm_step, jnp.zeros((total, width), jnp.float32), jnp.arange(N_COL, dtype=jnp.int32))
    hat_grad = normed_grad * gain[None, :]
    first_sum = lax.optimization_barrier(jnp.sum(hat_grad, axis=1)) / width
    second_sum = lax.optimization_barrier(jnp.sum(hat_grad * centred, axis=1)) / width
    input_grad = (grad_out.astype(jnp.float32) + inv_std[:, None] * (hat_grad - first_sum[:, None] - centred * second_sum[:, None])).astype(jnp.bfloat16)
    grad_gain = lax.optimization_barrier(jnp.sum(normed_grad * centred, axis=0))
    return (encoded, input_grad, grad_value, grad_gate, grad_kernel, grad_bias, grad_out_weight, grad_gain)
```

```python
import jax
import jax.numpy as jnp
from jax import lax
from jax.sharding import Mesh, PartitionSpec as P

K = 31
LEN = 2048
HALF = K // 2
NX, NK, NY, NZ = 4, 2, 4, 8
ROW = ("x", "k")
COL = ("y", "z")


epsilon = 1e-05


def extended(block, width):
    count = NX * NK
    forward = [(i, i + 1) for i in range(count - 1)]
    backward = [(target, source) for source, target in forward]
    low = lax.ppermute(block[-width:], ROW, forward)
    high = lax.ppermute(block[:width], ROW, backward)
    return jnp.concatenate([low, block, high], axis=0)


def tap_masks(positions):
    offsets = jnp.arange(K, dtype=jnp.int32) - HALF
    placed = (positions % LEN)[None, :] + offsets[:, None]
    return ((placed >= 0) & (placed < LEN)).astype(jnp.float32)


def dot(left, right, dims):
    return lax.dot_general(left, right, (dims, ((), ())), preferred_element_type=jnp.float32)


def swap_xy(block):
    return lax.ppermute(
        block, ("x", "y"), [(a * NY + b, b * NY + a) for a in range(NX) for b in range(NY)]
    )


def scatter_sum(parts, axis):
    moved = lax.all_to_all(parts.astype(jnp.bfloat16), axis, 0, 0, tiled=True)
    return jnp.sum(moved.astype(jnp.float32), axis=0)


def shards(frames, gain, w_value, w_gate, kernel, bias, w_out, grad_out):
    bf16 = jnp.bfloat16
    rows, cols = frames.shape
    width = cols * NY * NZ
    quarter = cols * NZ
    row_start = (lax.axis_index("x") * NK + lax.axis_index("k")) * rows
    y_index = lax.axis_index("y")
    col_start = (y_index * NZ + lax.axis_index("z")) * cols
    local_gain = lax.dynamic_slice_in_dim(gain, col_start, cols, 0)
    quarter_gain = lax.dynamic_slice_in_dim(gain, y_index * quarter, quarter, 0)

    vg_own = swap_xy(jnp.concatenate([w_value, w_gate], axis=1))
    out_own = swap_xy(w_out)
    vg_full = lax.all_gather(vg_own, ROW, axis=0, tiled=True).reshape(NY, quarter, 2 * cols)
    out_full = lax.all_gather(out_own, ROW, axis=0, tiled=True).reshape(NY, quarter, cols)

    frames_q = lax.all_gather(frames, "z", axis=1, tiled=True)
    wide_q = frames_q.astype(jnp.float32)
    sums = lax.psum(jnp.stack([jnp.sum(wide_q, axis=1), jnp.sum(wide_q * wide_q, axis=1)]), "y")
    mean_row = sums[0] / width
    inv_std = lax.rsqrt(sums[1] / width - mean_row * mean_row + epsilon)
    centred_q = (wide_q - mean_row[:, None]) * inv_std[:, None]
    normed_q = (centred_q * quarter_gain[None, :]).astype(bf16)
    wide = frames.astype(jnp.float32)
    centred = (wide - mean_row[:, None]) * inv_std[:, None]

    pre_parts = jnp.stack([dot(normed_q, vg_full[i], ((1,), (0,))) for i in range(NY)])
    pre = scatter_sum(pre_parts, "y")
    value_pre = pre[:, :cols]
    gate_pre = pre[:, cols:]
    gate_sig = jax.nn.sigmoid(gate_pre)
    gated = (value_pre * gate_sig).astype(bf16)

    padded_glu = extended(gated, HALF).astype(jnp.float32)
    local_masks = tap_masks(row_start + jnp.arange(rows, dtype=jnp.int32))
    conv_pre = jnp.zeros((rows, cols), jnp.float32) + bias[None, :]
    for tap in range(K):
        conv_pre = (
            conv_pre
            + kernel[tap][None, :] * local_masks[tap][:, None] * padded_glu[tap : tap + rows]
        )
    conv_sig = jax.nn.sigmoid(conv_pre)
    activated = (conv_pre * conv_sig).astype(bf16)

    grad_full = lax.all_gather(grad_out, "y", axis=0, tiled=False)
    act_terms = sum(dot(grad_full[i], out_full[i], ((1,), (1,))) for i in range(NY))
    act_parts = act_terms.reshape(rows, NZ, cols).transpose(1, 0, 2)
    act_grad = scatter_sum(act_parts, "z")

    act_q = lax.all_gather(activated, "z", axis=1, tiled=True)
    enc_parts = jnp.stack([dot(act_q, out_full[i], ((1,), (0,))) for i in range(NY)])
    encoded = (wide + scatter_sum(enc_parts, "y")).astype(bf16)
    out_weight_parts = jnp.stack([dot(act_q, grad_full[i], ((0,), (0,))) for i in range(NY)])
    grad_out_weight = swap_xy(
        lax.psum_scatter(
            out_weight_parts.astype(bf16).reshape(NY * quarter, cols),
            ROW,
            scatter_dimension=0,
            tiled=True,
        )
    ).astype(jnp.float32)

    conv_grad = (act_grad * conv_sig * (1.0 + conv_pre * (1.0 - conv_sig))).astype(bf16)
    conv_wide = conv_grad.astype(jnp.float32)
    padded_grad = extended(conv_grad, HALF).astype(jnp.float32)
    outer_masks = tap_masks(row_start - HALF + jnp.arange(rows + 2 * HALF, dtype=jnp.int32))
    glu_grad = jnp.zeros((rows, cols), jnp.float32)
    kernel_rows = []
    for tap in range(K):
        begin = 2 * HALF - tap
        glu_grad = (
            glu_grad
            + kernel[tap][None, :]
            * outer_masks[tap, begin : begin + rows][:, None]
            * padded_grad[begin : begin + rows]
        )
        kernel_rows.append(
            jnp.sum(
                local_masks[tap][:, None] * conv_wide * padded_glu[tap : tap + rows],
                axis=0,
            )
        )
    kernel_term = jnp.stack(kernel_rows)
    bias_term = jnp.sum(conv_wide, axis=0)

    value_grad = (glu_grad * gate_sig).astype(bf16)
    gate_grad = (glu_grad * value_pre * gate_sig * (1.0 - gate_sig)).astype(bf16)
    vg_grads = lax.all_gather(
        jnp.concatenate([value_grad, gate_grad], axis=1), "y", axis=0, tiled=False
    )
    weight_parts = jnp.stack([dot(normed_q, vg_grads[i], ((0,), (0,))) for i in range(NY)])
    in_weight = swap_xy(
        lax.psum_scatter(
            weight_parts.astype(bf16).reshape(NY * quarter, 2 * cols),
            ROW,
            scatter_dimension=0,
            tiled=True,
        )
    ).astype(jnp.float32)
    grad_value = in_weight[:, :cols]
    grad_gate = in_weight[:, cols:]

    norm_terms = sum(dot(vg_grads[i], vg_full[i], ((1,), (1,))) for i in range(NY))
    hat_terms = norm_terms * quarter_gain[None, :]
    hat_sums = jnp.stack([jnp.sum(hat_terms, axis=1), jnp.sum(hat_terms * centred_q, axis=1)])
    hat_sums = lax.psum(lax.psum(hat_sums, "y"), "z") / width
    norm_parts = norm_terms.reshape(rows, NZ, cols).transpose(1, 0, 2)
    normed_grad = scatter_sum(norm_parts, "z")
    hat_grad = normed_grad * local_gain[None, :]
    input_grad = (
        grad_out.astype(jnp.float32)
        + inv_std[:, None] * (hat_grad - hat_sums[0][:, None] - centred * hat_sums[1][:, None])
    ).astype(bf16)
    gain_term = jnp.sum(normed_grad * centred, axis=0)
    grad_kernel, grad_bias, grad_gain = lax.psum((kernel_term, bias_term, gain_term), ROW)
    return (
        encoded,
        input_grad,
        grad_value,
        grad_gate,
        grad_kernel,
        grad_bias,
        grad_out_weight,
        grad_gain,
    )


def solution(mesh):
    fine = Mesh(mesh.devices.reshape(NX, NK, NY, NZ), ("x", "k", "y", "z"))
    both = P(ROW, COL)
    return jax.shard_map(
        shards,
        mesh=fine,
        in_specs=(both, P(), both, both, P(None, COL), P(COL), both, both),
        out_specs=(both, both, both, both, P(None, COL), P(COL), both, P(COL)),
        check_vma=False,
    )
```

```python
import jax
import jax.numpy as jnp
from jax import lax
from jax.sharding import Mesh, PartitionSpec as P

K = 31
LEN = 2048
HALF = K // 2
NX, NK, NY, NZ = 4, 2, 4, 8
ROW = ("x", "k")
COL = ("y", "z")
TIME = ("y", "k")


epsilon = 1e-05


def extended(block, width):
    place = [k * NY + y for y in range(NY) for k in range(NK)]
    forward = list(zip(place[:-1], place[1:]))
    backward = [(target, source) for source, target in forward]
    low = lax.ppermute(block[-width:], ("k", "y"), forward)
    high = lax.ppermute(block[:width], ("k", "y"), backward)
    return jnp.concatenate([low, block, high], axis=0)


def tap_masks(positions):
    offsets = jnp.arange(K, dtype=jnp.int32) - HALF
    placed = (positions % LEN)[None, :] + offsets[:, None]
    return ((placed >= 0) & (placed < LEN)).astype(jnp.float32)


def dot(left, right, dims):
    return lax.dot_general(left, right, (dims, ((), ())), preferred_element_type=jnp.float32)


def swap_xy(block):
    return lax.ppermute(
        block, ("x", "y"), [(a * NY + b, b * NY + a) for a in range(NX) for b in range(NY)]
    )


def exchange(parts, axis):
    return lax.all_to_all(parts, axis, 0, 0, tiled=True)


def gathered(block, axis, count):
    return exchange(jnp.broadcast_to(block[None], (count,) + block.shape), axis)


def pieces(value):
    out = []
    for _ in range(3):
        piece = lax.reduce_precision(value, 8, 7)
        out.append(piece.astype(jnp.bfloat16))
        value = value - piece
    return jnp.stack(out)


def rows_of(value, lanes, count):
    flat = pieces(value).reshape(-1)
    flat = jnp.pad(flat, (0, count * lanes - flat.shape[0]))
    return flat.reshape(count, lanes)


def from_rows(rows, shape):
    size = 1
    for extent in shape:
        size = size * extent
    total = jnp.sum(rows.astype(jnp.float32), axis=0).reshape(-1)[: 3 * size]
    return jnp.sum(total.reshape((3,) + shape), axis=0)


def shards(frames, gain, w_value, w_gate, kernel, bias, w_out, grad_out):
    bf16 = jnp.bfloat16
    rows, cols = frames.shape
    width = cols * NX * NZ
    quarter = cols * NZ
    x_index = lax.axis_index("x")
    k_index = lax.axis_index("k")
    row_start = (lax.axis_index("y") * NK + k_index) * rows
    col_start = (x_index * NZ + lax.axis_index("z")) * cols
    local_gain = lax.dynamic_slice_in_dim(gain, col_start, cols, 0)
    quarter_gain = lax.dynamic_slice_in_dim(gain, x_index * quarter, quarter, 0)

    swapped = swap_xy(jnp.concatenate([frames, grad_out], axis=1))
    frames = swapped[:, :cols]
    grad_out = swapped[:, cols:]
    taps = swap_xy(jnp.concatenate([kernel, bias[None, :]], axis=0))
    kernel = taps[:K]
    bias = taps[K]

    vg_own = jnp.concatenate([w_value, w_gate], axis=1)
    vg_full = lax.all_gather(vg_own, TIME, axis=0, tiled=True).reshape(NY, quarter, 2 * cols)
    out_full = lax.all_gather(w_out, TIME, axis=0, tiled=True).reshape(NY, quarter, cols)

    frames_q = gathered(frames, "z", NZ).transpose(1, 0, 2).reshape(rows, quarter)
    grad_full = gathered(grad_out, "x", NX)
    wide_q = frames_q.astype(jnp.float32)
    sums = lax.psum(jnp.stack([jnp.sum(wide_q, axis=1), jnp.sum(wide_q * wide_q, axis=1)]), "x")
    mean_row = sums[0] / width
    inv_std = lax.rsqrt(sums[1] / width - mean_row * mean_row + epsilon)
    centred_q = (wide_q - mean_row[:, None]) * inv_std[:, None]
    normed_q = (centred_q * quarter_gain[None, :]).astype(bf16)
    wide = frames.astype(jnp.float32)
    centred = (wide - mean_row[:, None]) * inv_std[:, None]

    unit_terms = jnp.sum(vg_full.astype(jnp.float32) * quarter_gain[None, :, None], axis=1)
    pre_parts = []
    for i in range(NX):
        main = dot(normed_q, vg_full[i], ((1,), (0,))).astype(bf16)
        pre_parts.append(jnp.concatenate([main, rows_of(unit_terms[i], 2 * cols, 16)], axis=0))
    pre_moved = exchange(jnp.stack(pre_parts), "x")
    unit = from_rows(pre_moved[:, rows:], (2 * cols,))
    pre = jnp.sum(pre_moved[:, :rows].astype(jnp.float32), axis=0)
    value_pre = pre[:, :cols]
    gate_pre = pre[:, cols:]
    gate_sig = jax.nn.sigmoid(gate_pre)
    gated = (value_pre * gate_sig).astype(bf16)

    padded_glu = extended(gated, HALF).astype(jnp.float32)
    local_masks = tap_masks(row_start + jnp.arange(rows, dtype=jnp.int32))
    conv_pre = jnp.zeros((rows, cols), jnp.float32) + bias[None, :]
    for tap in range(K):
        conv_pre = (
            conv_pre
            + kernel[tap][None, :] * local_masks[tap][:, None] * padded_glu[tap : tap + rows]
        )
    conv_sig = jax.nn.sigmoid(conv_pre)
    activated = (conv_pre * conv_sig).astype(bf16)

    act_terms = sum(dot(grad_full[i], out_full[i], ((1,), (1,))) for i in range(NX))
    act_parts = act_terms.astype(bf16).reshape(rows, NZ, cols).transpose(1, 0, 2)
    act_grad = jnp.sum(exchange(act_parts, "z").astype(jnp.float32), axis=0)

    conv_grad = (act_grad * conv_sig * (1.0 + conv_pre * (1.0 - conv_sig))).astype(bf16)
    conv_wide = conv_grad.astype(jnp.float32)
    padded_grad = extended(conv_grad, HALF).astype(jnp.float32)
    outer_masks = tap_masks(row_start - HALF + jnp.arange(rows + 2 * HALF, dtype=jnp.int32))
    glu_grad = jnp.zeros((rows, cols), jnp.float32)
    kernel_rows = []
    for tap in range(K):
        begin = 2 * HALF - tap
        glu_grad = (
            glu_grad
            + kernel[tap][None, :]
            * outer_masks[tap, begin : begin + rows][:, None]
            * padded_grad[begin : begin + rows]
        )
        kernel_rows.append(
            jnp.sum(
                local_masks[tap][:, None] * conv_wide * padded_glu[tap : tap + rows],
                axis=0,
            )
        )
    bias_term = jnp.sum(conv_wide, axis=0)

    value_grad = (glu_grad * gate_sig).astype(bf16)
    gate_grad = (glu_grad * value_pre * gate_sig * (1.0 - gate_sig)).astype(bf16)
    vg_grad = jnp.concatenate([value_grad, gate_grad], axis=1)
    vg_wide = vg_grad.astype(jnp.float32)
    hat_terms = jnp.stack(
        [jnp.sum(vg_wide * unit[None, :], axis=1), jnp.sum(vg_wide * pre, axis=1)]
    )
    vg_moved = gathered(
        jnp.concatenate([vg_grad, rows_of(hat_terms, 2 * cols, 16)], axis=0), "x", NX
    )
    vg_grads = vg_moved[:, :rows]
    hat_part = from_rows(vg_moved[:, rows:], (2, rows))

    weight_parts = jnp.stack([dot(normed_q, vg_grads[i], ((0,), (0,))) for i in range(NX)])
    weight_parts = weight_parts.astype(bf16).reshape(NY, NK, quarter // NK, 2 * cols)
    kept = lax.dynamic_index_in_dim(weight_parts, k_index, 1, keepdims=False)
    given = lax.dynamic_index_in_dim(weight_parts, 1 - k_index, 1, keepdims=False)
    taken = lax.ppermute(given, "k", [(0, 1), (1, 0)])
    both = (kept.astype(jnp.float32) + taken.astype(jnp.float32)).astype(bf16)
    in_weight = jnp.sum(exchange(both, "y").astype(jnp.float32), axis=0)
    grad_value = in_weight[:, :cols]
    grad_gate = in_weight[:, cols:]

    norm_terms = sum(dot(vg_grads[i], vg_full[i], ((1,), (1,))) for i in range(NX))
    norm_parts = norm_terms.astype(bf16).reshape(rows, NZ, cols).transpose(1, 0, 2)
    hat_rows = jnp.broadcast_to(rows_of(hat_part, cols, 32)[None], (NZ, 32, cols))
    norm_moved = exchange(jnp.concatenate([norm_parts, hat_rows], axis=1), "z")
    hat_sums = from_rows(norm_moved[:, rows:], (2, rows)) / width
    normed_grad = jnp.sum(norm_moved[:, :rows].astype(jnp.float32), axis=0)
    hat_grad = normed_grad * local_gain[None, :]
    input_grad = (
        grad_out.astype(jnp.float32)
        + inv_std[:, None] * (hat_grad - hat_sums[0][:, None] - centred * hat_sums[1][:, None])
    ).astype(bf16)
    input_grad = swap_xy(input_grad)

    act_q = gathered(activated, "z", NZ).transpose(1, 0, 2).reshape(rows, quarter)
    out_weight_parts = jnp.stack([dot(act_q, grad_full[i], ((0,), (0,))) for i in range(NX)])
    grad_out_weight = lax.psum_scatter(
        out_weight_parts.astype(bf16).reshape(NY * quarter, cols),
        TIME,
        scatter_dimension=0,
        tiled=True,
    ).astype(jnp.float32)
    enc_parts = jnp.stack([dot(act_q, out_full[i], ((1,), (0,))) for i in range(NX)]).astype(bf16)
    enc_sum = jnp.sum(exchange(enc_parts, "x").astype(jnp.float32), axis=0)
    encoded = swap_xy((wide + enc_sum).astype(bf16))

    gain_term = jnp.sum(normed_grad * centred, axis=0)
    small = jnp.stack(kernel_rows + [bias_term, gain_term])
    small = small + lax.ppermute(small, "k", [(0, 1), (1, 0)])
    arrived = []
    for shift in range(NX):
        route = [
            (a * NY + b, ((b + shift) % NX) * NY + a) for a in range(NX) for b in range(NY)
        ]
        arrived.append(lax.ppermute(small, ("x", "y"), route))
    small = sum(arrived)
    return (
        encoded,
        input_grad,
        grad_value,
        grad_gate,
        small[:K],
        small[K],
        grad_out_weight,
        small[K + 1],
    )


def solution(mesh):
    fine = Mesh(mesh.devices.reshape(NX, NK, NY, NZ), ("x", "k", "y", "z"))
    both = P(ROW, COL)
    return jax.shard_map(
        shards,
        mesh=fine,
        in_specs=(both, P(), both, both, P(None, COL), P(COL), both, both),
        out_specs=(both, both, both, both, P(None, COL), P(COL), both, P(COL)),
        check_vma=False,
    )
```

```python
import jax
import jax.numpy as jnp
from jax import lax
from jax.experimental import pallas as pl
from jax.experimental.pallas import tpu as pltpu
from jax.sharding import Mesh, PartitionSpec as P

K = 31
LEN = 2048
HALF = K // 2
NX, NK, NY, NZ = 4, 2, 4, 8
ROW = ("x", "k")
COL = ("y", "z")
TIME = ("y", "k")
ROWS = 384
COLS = 128
QUARTER = COLS * NZ
WIDTH = QUARTER * NX
EDGE = 32

epsilon = 1e-05
f32 = jnp.float32
bf16 = jnp.bfloat16


def dot(left, right, left_dim, right_dim):
    return lax.dot_general(
        left, right, (((left_dim,), (right_dim,)), ((), ())), preferred_element_type=f32
    )


def split3(value):
    high = value.astype(bf16)
    rest = value - high.astype(f32)
    middle = rest.astype(bf16)
    low = (rest - middle.astype(f32)).astype(bf16)
    return high, middle, low


def one_hot():
    lane = lax.broadcasted_iota(jnp.int32, (16, 128), 1)
    row = lax.broadcasted_iota(jnp.int32, (16, 128), 0)
    return jnp.where(lane == row, 1.0, 0.0).astype(bf16)


def columns_to_rows(first, second):
    lane = lax.broadcasted_iota(jnp.int32, (first.shape[0], 128), 1)
    grid = jnp.zeros((first.shape[0], 128), f32)
    for j, piece in enumerate(split3(first) + split3(second)):
        grid = jnp.where(lane == j, piece.astype(f32), grid)
    return dot(one_hot(), grid.astype(bf16), 1, 1)


def rows_to_columns(rows):
    grid = dot(rows, one_hot(), 0, 0)
    first = grid[:, 0:1] + grid[:, 1:2] + grid[:, 2:3]
    second = grid[:, 3:4] + grid[:, 4:5] + grid[:, 5:6]
    return first, second


def stacked_rows(values):
    row = lax.broadcasted_iota(jnp.int32, (16, values[0].shape[1]), 0)
    out = jnp.zeros((16, values[0].shape[1]), f32)
    for j, value in enumerate(values):
        out = jnp.where(row == j, value.astype(f32), out)
    return out


def call(body, out_shape, args, smem=(), scratch=()):
    specs = [
        pl.BlockSpec(memory_space=pltpu.SMEM if i in smem else pltpu.VMEM)
        for i in range(len(args))
    ]
    many = isinstance(out_shape, (list, tuple))
    out_specs = [pl.BlockSpec(memory_space=pltpu.VMEM) for _ in out_shape] if many else (
        pl.BlockSpec(memory_space=pltpu.VMEM)
    )
    return pl.pallas_call(
        body,
        out_shape=out_shape,
        in_specs=specs,
        out_specs=out_specs,
        scratch_shapes=list(scratch),
        compiler_params=pltpu.CompilerParams(vmem_limit_bytes=48 * 1024 * 1024),
    )(*args)


def shape(dims, kind):
    return jax.ShapeDtypeStruct(dims, kind)


def project_kernel(frames_ref, gain_ref, gain_rows_ref, weight_ref, out_ref, left_ref):
    total = jnp.zeros((ROWS, 1), f32)
    square = jnp.zeros((ROWS, 1), f32)
    for i in range(NZ):
        wide = frames_ref[i].astype(f32)
        total = total + jnp.sum(wide, axis=1, keepdims=True)
        square = square + jnp.sum(wide * wide, axis=1, keepdims=True)
    mean = total / QUARTER
    for i in range(NZ):
        cut = pl.ds(i * COLS, COLS)
        scaled = (frames_ref[i].astype(f32) - mean) * gain_ref[0:1, cut]
        left_ref[:, cut] = scaled.astype(bf16)
    sums = columns_to_rows(total, square).astype(bf16)
    for i in range(NX):
        weight = weight_ref[pl.ds(i * QUARTER, QUARTER), 0 : 2 * COLS]
        out_ref[i, 0:ROWS, :] = dot(left_ref[...], weight, 1, 0).astype(bf16)
        unit = jnp.sum(dot(gain_rows_ref[...], weight, 1, 0), axis=0, keepdims=True)
        out_ref[i, ROWS : ROWS + 16, :] = stacked_rows(split3(unit)).astype(bf16)
        out_ref[i, ROWS + 16 : ROWS + 32, :] = sums[:, 0:256]
        out_ref[i, ROWS + 32 : ROWS + 48, 0:128] = sums[:, 256:384]
        out_ref[i, ROWS + 32 : ROWS + 48, 128:256] = jnp.zeros((16, 128), bf16)


def gate_kernel(parts_ref, pre_ref, gated_ref, unit_ref, stat_ref):
    totals, squares, units = [], [], []
    for i in range(NX):
        rows = jnp.concatenate(
            [parts_ref[i, ROWS + 16 : ROWS + 32, :], parts_ref[i, ROWS + 32 : ROWS + 48, 0:128]],
            axis=1,
        )
        first, second = rows_to_columns(rows)
        totals.append(first)
        squares.append(second)
        pieces = parts_ref[i, ROWS : ROWS + 16, :].astype(f32)
        units.append(jnp.sum(pieces, axis=0, keepdims=True))
    mean = sum(totals) / WIDTH
    inv_std = lax.rsqrt(sum(squares) / WIDTH - mean * mean + epsilon)
    pre = jnp.zeros((ROWS, 2 * COLS), f32)
    for i in range(NX):
        pre = pre + parts_ref[i, 0:ROWS, :].astype(f32)
        pre = pre + (totals[i] / QUARTER - mean) * units[i]
    pre = pre * inv_std
    pre_ref[...] = pre
    gated_ref[...] = (pre[:, 0:COLS] * jax.nn.sigmoid(pre[:, COLS:])).astype(bf16)
    unit_ref[...] = jnp.broadcast_to(sum(units), (8, 2 * COLS))
    lane = lax.broadcasted_iota(jnp.int32, (ROWS, 128), 1)
    stat_ref[...] = jnp.where(lane == 0, mean, inv_std)


def act_kernel(place_ref, g0_ref, g1_ref, g2_ref, g3_ref, weight_ref, out_ref):
    total = jnp.zeros((ROWS, QUARTER), f32)
    for j, grad_ref in enumerate((g0_ref, g1_ref, g2_ref, g3_ref)):
        start = pl.multiple_of(place_ref[j] * QUARTER, QUARTER)
        weight = weight_ref[pl.ds(start, QUARTER), 2 * COLS : 3 * COLS]
        total = total + dot(grad_ref[...], weight, 1, 1)
    for i in range(NZ):
        out_ref[pl.ds(i * ROWS, ROWS), :] = total[:, i * COLS : (i + 1) * COLS].astype(bf16)


def conv_kernel(
    place_ref,
    gated_ref,
    low_ref,
    high_ref,
    act_ref,
    act_low_ref,
    act_high_ref,
    taps_ref,
    pre_ref,
    unit_ref,
    activated_ref,
    message_ref,
    small_ref,
    wide_ref,
    grad_ref,
    glu_ref,
    sums_ref,
    masked_ref,
    masked_grad_ref,
):
    border = place_ref[0]
    wide_ref[0:EDGE, :] = low_ref[...].astype(f32)
    wide_ref[EDGE : EDGE + ROWS, :] = gated_ref[...].astype(f32)
    wide_ref[EDGE + ROWS :, :] = high_ref[...].astype(f32)
    sums_ref[...] = jnp.zeros((K + 1, 8, COLS), f32)
    bias = taps_ref[K : K + 1, :]
    chunks = [(-16, 16), (0, 128), (128, 128), (256, 128), (ROWS, 16)]

    def same_clip(start, count):
        row = lax.broadcasted_iota(jnp.int32, (count + 32, COLS), 0) + (start - 16)
        inside = (row < border).astype(jnp.int32)
        own = jnp.where(start < border, 1, 0)
        return inside == own

    for start, count in chunks:
        here = wide_ref[pl.ds(start - 16 + EDGE, count + 32), :]
        masked_ref[0 : count + 32, :] = jnp.where(same_clip(start, count), here, 0.0)
        conv = jnp.broadcast_to(bias, (count, COLS))
        for tap in range(K):
            conv = conv + taps_ref[tap : tap + 1, :] * masked_ref[1 + tap : 1 + tap + count, :]
        sig = jax.nn.sigmoid(conv)
        if start < 0:
            act = act_low_ref[...]
        elif start < ROWS:
            act = act_ref[pl.ds(start, count), :]
        else:
            act = act_high_ref[...]
        grad = (act.astype(f32) * sig * (1.0 + conv * (1.0 - sig))).astype(bf16).astype(f32)
        grad_ref[pl.ds(start + 16, count), :] = grad
        if 0 <= start < ROWS:
            activated_ref[pl.ds(start, count), :] = (conv * sig).astype(bf16)
            for tap in range(K):
                product = grad * masked_ref[1 + tap : 1 + tap + count, :]
                sums_ref[tap] += jnp.sum(product.reshape(count // 8, 8, COLS), axis=0)
            sums_ref[K] += jnp.sum(grad.reshape(count // 8, 8, COLS), axis=0)
    activated_ref[ROWS:, :] = jnp.zeros((activated_ref.shape[0] - ROWS, COLS), bf16)
    small_ref[...] = jnp.sum(sums_ref[...], axis=1)

    for start, count in chunks[1:4]:
        here = grad_ref[pl.ds(start, count + 32), :]
        masked_grad_ref[...] = jnp.where(same_clip(start, count), here, 0.0)
        glu = jnp.zeros((count, COLS), f32)
        for tap in range(K):
            glu = glu + taps_ref[tap : tap + 1, :] * masked_grad_ref[31 - tap : 31 - tap + count, :]
        glu_ref[pl.ds(start, count), :] = glu

    glu = glu_ref[...]
    value_pre = pre_ref[:, 0:COLS]
    gate_pre = pre_ref[:, COLS:]
    gate_sig = jax.nn.sigmoid(gate_pre)
    value_grad = (glu * gate_sig).astype(bf16)
    gate_grad = (glu * value_pre * gate_sig * (1.0 - gate_sig)).astype(bf16)
    message_ref[0:ROWS, 0:COLS] = value_grad
    message_ref[0:ROWS, COLS:] = gate_grad
    value_wide = value_grad.astype(f32)
    gate_wide = gate_grad.astype(f32)
    first = jnp.sum(
        value_wide * unit_ref[0:1, 0:COLS] + gate_wide * unit_ref[0:1, COLS:],
        axis=1,
        keepdims=True,
    )
    second = jnp.sum(value_wide * value_pre + gate_wide * gate_pre, axis=1, keepdims=True)
    rows = columns_to_rows(first, second).astype(bf16)
    message_ref[ROWS : ROWS + 16, :] = rows[:, 0:256]
    message_ref[ROWS + 16 : ROWS + 32, 0:128] = rows[:, 256:384]
    message_ref[ROWS + 16 : ROWS + 32, 128:256] = jnp.zeros((16, 128), bf16)


def norm_kernel(grads_ref, weight_ref, out_ref):
    total = jnp.zeros((ROWS, QUARTER), f32)
    rows = jnp.zeros((16, ROWS), f32)
    for i in range(NX):
        weight = weight_ref[pl.ds(i * QUARTER, QUARTER), 0 : 2 * COLS]
        total = total + dot(grads_ref[i, 0:ROWS, :], weight, 1, 1)
        here = jnp.concatenate(
            [grads_ref[i, ROWS : ROWS + 16, :], grads_ref[i, ROWS + 16 : ROWS + 32, 0:128]], axis=1
        )
        rows = rows + here.astype(f32)
    first = rows[0:1] + rows[1:2] + rows[2:3]
    second = rows[3:4] + rows[4:5] + rows[5:6]
    sums = stacked_rows(split3(first) + split3(second)).astype(bf16)
    for i in range(NZ):
        out_ref[i, 0:ROWS, :] = total[:, i * COLS : (i + 1) * COLS].astype(bf16)
        for j in range(3):
            out_ref[i, ROWS + 16 * j : ROWS + 16 * j + 16, :] = sums[:, j * 128 : (j + 1) * 128]


def weight_kernel(
    place_ref, frames_ref, gain_ref, stat_ref, grads_ref, kept_ref, given_ref, left_ref, right_ref
):
    mean = stat_ref[:, 0:1]
    inv_std = stat_ref[:, 1:2]
    half = QUARTER // NK
    for i in range(NZ):
        scaled = (frames_ref[i].astype(f32) - mean) * inv_std * gain_ref[0:1, pl.ds(i * COLS, COLS)]
        left_ref[i * COLS // half, :, pl.ds(i * COLS % half, COLS)] = scaled.astype(bf16)
    for i in range(NX):
        right_ref[:, pl.ds(i * 2 * COLS, 2 * COLS)] = grads_ref[i, 0:ROWS, :]
    core = place_ref[1]
    for out_ref, which in ((given_ref, 1 - core), (kept_ref, core)):
        out = dot(left_ref[which], right_ref[...], 0, 0).astype(bf16)
        for i in range(NX):
            out_ref[i] = out[:, i * 2 * COLS : (i + 1) * 2 * COLS]


def out_kernel(
    place_ref, act_ref, g0_ref, g1_ref, g2_ref, g3_ref, weight_ref, enc_ref, grad_ref, left_ref
):
    for i in range(NZ):
        left_ref[:, pl.ds(i * COLS, COLS)] = act_ref[i, 0:ROWS, :]
    left = left_ref[...]
    for i in range(NX):
        weight = weight_ref[pl.ds(i * QUARTER, QUARTER), 2 * COLS : 3 * COLS]
        enc_ref[i] = dot(left, weight, 1, 0).astype(bf16)
    for j, right_ref in enumerate((g0_ref, g1_ref, g2_ref, g3_ref)):
        start = pl.multiple_of(place_ref[j] * QUARTER, QUARTER)
        grad_ref[pl.ds(start, QUARTER), :] = dot(left, right_ref[...], 0, 0).astype(bf16)


def input_kernel(parts_ref, frames_ref, grad_ref, stat_ref, gain_ref, out_ref, small_ref):
    normed_grad = jnp.zeros((ROWS, COLS), f32)
    rows = jnp.zeros((16, ROWS), f32)
    for i in range(NZ):
        normed_grad = normed_grad + parts_ref[i, 0:ROWS, :].astype(f32)
        here = [parts_ref[i, ROWS + 16 * j : ROWS + 16 * j + 16, :] for j in range(3)]
        rows = rows + jnp.concatenate(here, axis=1).astype(f32)
    first = rows[0:1] + rows[1:2] + rows[2:3]
    second = rows[3:4] + rows[4:5] + rows[5:6]
    sums = stacked_rows(split3(first) + split3(second)).astype(bf16)
    first, second = rows_to_columns(sums)
    mean = stat_ref[:, 0:1]
    inv_std = stat_ref[:, 1:2]
    centred = (frames_ref[...].astype(f32) - mean) * inv_std
    hat = normed_grad * gain_ref[0:1, :]
    out = grad_ref[...].astype(f32) + inv_std * (hat - first / WIDTH - centred * (second / WIDTH))
    out_ref[...] = out.astype(bf16)
    gain_term = jnp.sum(normed_grad * centred, axis=0, keepdims=True)
    small_ref[...] = jnp.broadcast_to(gain_term, (8, COLS))


def swap_xy(block):
    return lax.ppermute(
        block, ("x", "y"), [(a * NY + b, b * NY + a) for a in range(NX) for b in range(NY)]
    )


def neighbours(block, width):
    place = [k * NY + y for y in range(NY) for k in range(NK)]
    forward = list(zip(place[:-1], place[1:]))
    backward = [(target, source) for source, target in forward]
    low = lax.ppermute(block[-width:], ("k", "y"), forward)
    high = lax.ppermute(block[:width], ("k", "y"), backward)
    return low, high


def exchange(parts, axis):
    return lax.all_to_all(parts, axis, 0, 0, tiled=True)


def gathered(block, axis, count):
    return exchange(jnp.broadcast_to(block[None], (count,) + block.shape), axis)


def shifted(block, axis, count, shift):
    return lax.ppermute(block, axis, [(i, (i + shift) % count) for i in range(count)])


def spread(block, axis, count):
    return [block] + [shifted(block, axis, count, j) for j in range(1, count)]


def taken(parts, axis, count):
    index = lax.axis_index(axis)
    total = lax.dynamic_index_in_dim(parts, index, 0, keepdims=False).astype(f32)
    for j in range(1, count):
        part = lax.dynamic_index_in_dim(parts, (index + j) % count, 0, keepdims=False)
        total = total + shifted(part, axis, count, j).astype(f32)
    return total


def after(value, *others):
    return lax.optimization_barrier((value,) + others)[0]


def shards(frames, gain, w_value, w_gate, kernel, bias, w_out, grad_out):
    x_index = lax.axis_index("x")
    k_index = lax.axis_index("k")
    row_start = (lax.axis_index("y") * NK + k_index) * ROWS
    col_start = (x_index * NZ + lax.axis_index("z")) * COLS
    local_gain = lax.dynamic_slice_in_dim(gain, col_start, COLS, 0)[None]
    quarter_gain = lax.dynamic_slice_in_dim(gain, x_index * QUARTER, QUARTER, 0)[None]
    high = lax.reduce_precision(quarter_gain, 8, 7)
    middle = lax.reduce_precision(quarter_gain - high, 8, 7)
    low = quarter_gain - high - middle
    gain_rows = jnp.pad(jnp.concatenate([high, middle, low], axis=0), ((0, 13), (0, 0)))
    gain_rows = gain_rows.astype(bf16)
    order = (x_index + NX - jnp.arange(NX, dtype=jnp.int32)) % NX
    place = jnp.stack([LEN - row_start, k_index]).astype(jnp.int32)

    weights = lax.all_gather(
        jnp.concatenate([w_value, w_gate, w_out], axis=1), TIME, axis=0, tiled=True
    )

    frames = swap_xy(frames)
    frames_z = gathered(frames, "z", NZ)
    grad_out = swap_xy(after(grad_out, frames))
    grads = spread(grad_out, "x", NX)
    taps = swap_xy(jnp.concatenate([kernel, bias[None, :]], axis=0))

    pre_parts = call(
        project_kernel,
        shape((NX, ROWS + 48, 2 * COLS), bf16),
        (frames_z, quarter_gain, gain_rows, weights),
        scratch=[pltpu.VMEM((ROWS, QUARTER), bf16)],
    )
    pre_moved = exchange(pre_parts, "x")
    act_parts = call(
        act_kernel, shape((NZ * ROWS, COLS), bf16), (order, *grads, weights), smem=(0,)
    )
    act_grad = lax.psum_scatter(act_parts, "z", scatter_dimension=0, tiled=True)
    pre, gated, unit, stat = call(
        gate_kernel,
        [
            shape((ROWS, 2 * COLS), f32),
            shape((ROWS, COLS), bf16),
            shape((8, 2 * COLS), f32),
            shape((ROWS, 128), f32),
        ],
        (pre_moved,),
    )
    gated_low, gated_high = neighbours(gated, EDGE)
    act_low, act_high = neighbours(act_grad, 16)
    activated, message, small = call(
        conv_kernel,
        [
            shape((512, COLS), bf16),
            shape((ROWS + 32, 2 * COLS), bf16),
            shape((K + 1, COLS), f32),
        ],
        (
            place,
            gated,
            gated_low,
            gated_high,
            act_grad,
            act_low,
            act_high,
            taps,
            pre,
            unit,
        ),
        smem=(0,),
        scratch=[
            pltpu.VMEM((ROWS + 2 * EDGE, COLS), f32),
            pltpu.VMEM((ROWS + 32, COLS), f32),
            pltpu.VMEM((ROWS, COLS), f32),
            pltpu.VMEM((K + 1, 8, COLS), f32),
            pltpu.VMEM((160, COLS), f32),
            pltpu.VMEM((160, COLS), f32),
        ],
    )

    vg_grads = gathered(message, "x", NX)
    act_wide = lax.all_gather(activated, "z", axis=0, tiled=False)
    norm_parts = call(norm_kernel, shape((NZ, ROWS + 48, COLS), bf16), (vg_grads, weights))
    norm_moved = exchange(norm_parts, "z")
    kept, given = call(
        weight_kernel,
        [shape((NY, QUARTER // NK, 2 * COLS), bf16) for _ in range(2)],
        (place, frames_z, quarter_gain, stat, vg_grads),
        smem=(0,),
        scratch=[
            pltpu.VMEM((NK, ROWS, QUARTER // NK), bf16),
            pltpu.VMEM((ROWS, NX * 2 * COLS), bf16),
        ],
    )
    other = lax.ppermute(given, "k", [(0, 1), (1, 0)])
    both = (kept.astype(f32) + other.astype(f32)).astype(bf16)
    in_weight = taken(both, "y", NY)

    enc_parts, out_weight_parts = call(
        out_kernel,
        [shape((NX, ROWS, COLS), bf16), shape((NY * QUARTER, COLS), bf16)],
        (order, act_wide, *grads, weights),
        smem=(0,),
        scratch=[pltpu.VMEM((ROWS, QUARTER), bf16)],
    )
    grad_out_weight = lax.psum_scatter(
        out_weight_parts, TIME, scatter_dimension=0, tiled=True
    ).astype(f32)
    enc_sum = taken(enc_parts, "x", NX)
    encoded = swap_xy((frames.astype(f32) + enc_sum).astype(bf16))

    input_grad, gain_term = call(
        input_kernel,
        [shape((ROWS, COLS), bf16), shape((8, COLS), f32)],
        (norm_moved, frames, grad_out, stat, local_gain),
    )
    input_grad = swap_xy(input_grad)

    small = jnp.concatenate([small, gain_term], axis=0)
    small = small + lax.ppermute(small, "k", [(0, 1), (1, 0)])
    arrived = []
    for shift in range(NX):
        route = [
            (a * NY + b, ((b + shift) % NX) * NY + a) for a in range(NX) for b in range(NY)
        ]
        arrived.append(lax.ppermute(small, ("x", "y"), route))
    small = sum(arrived)
    return (
        encoded,
        input_grad,
        in_weight[:, :COLS],
        in_weight[:, COLS:],
        small[:K],
        small[K],
        grad_out_weight,
        small[K + 1],
    )


def solution(mesh):
    fine = Mesh(mesh.devices.reshape(NX, NK, NY, NZ), ("x", "k", "y", "z"))
    both = P(ROW, COL)
    return jax.shard_map(
        shards,
        mesh=fine,
        in_specs=(both, P(), both, both, P(None, COL), P(COL), both, both),
        out_specs=(both, both, both, both, P(None, COL), P(COL), both, P(COL)),
        check_vma=False,
    )
```

```python
import jax
import jax.numpy as jnp
from jax import lax
from jax.experimental import pallas as pl
from jax.experimental.pallas import tpu as pltpu
from jax.sharding import Mesh, PartitionSpec as P

K = 31
LEN = 2048
HALF = K // 2
NX, NK, NY, NZ = 4, 2, 4, 8
ROW = ("x", "k")
COL = ("y", "z")
TIME = ("y", "k")
ROWS = 384
COLS = 128
QUARTER = COLS * NZ
WIDTH = QUARTER * NX
EDGE = 32

epsilon = 1e-05
f32 = jnp.float32
bf16 = jnp.bfloat16


def dot(left, right, left_dim, right_dim):
    return lax.dot_general(
        left, right, (((left_dim,), (right_dim,)), ((), ())), preferred_element_type=f32
    )


def split3(value):
    high = value.astype(bf16)
    rest = value - high.astype(f32)
    middle = rest.astype(bf16)
    low = (rest - middle.astype(f32)).astype(bf16)
    return high, middle, low


def one_hot():
    lane = lax.broadcasted_iota(jnp.int32, (16, 128), 1)
    row = lax.broadcasted_iota(jnp.int32, (16, 128), 0)
    return jnp.where(lane == row, 1.0, 0.0).astype(bf16)


def columns_to_rows(first, second):
    lane = lax.broadcasted_iota(jnp.int32, (first.shape[0], 128), 1)
    grid = jnp.zeros((first.shape[0], 128), f32)
    for j, piece in enumerate(split3(first) + split3(second)):
        grid = jnp.where(lane == j, piece.astype(f32), grid)
    return dot(one_hot(), grid.astype(bf16), 1, 1)


def rows_to_columns(rows):
    grid = dot(rows, one_hot(), 0, 0)
    first = grid[:, 0:1] + grid[:, 1:2] + grid[:, 2:3]
    second = grid[:, 3:4] + grid[:, 4:5] + grid[:, 5:6]
    return first, second


def stacked_rows(values):
    row = lax.broadcasted_iota(jnp.int32, (16, values[0].shape[1]), 0)
    out = jnp.zeros((16, values[0].shape[1]), f32)
    for j, value in enumerate(values):
        out = jnp.where(row == j, value.astype(f32), out)
    return out


def call(body, out_shape, args, smem=(), scratch=()):
    specs = [
        pl.BlockSpec(memory_space=pltpu.SMEM) if i in smem else pl.BlockSpec()
        for i in range(len(args))
    ]
    return pl.pallas_call(
        body,
        out_shape=out_shape,
        in_specs=specs,
        scratch_shapes=list(scratch),
        compiler_params=pltpu.CompilerParams(vmem_limit_bytes=48 * 1024 * 1024),
    )(*args)


def shape(dims, kind):
    return jax.ShapeDtypeStruct(dims, kind)


def project_kernel(place_ref, frames_ref, gain_ref, gain_rows_ref, weight_ref, *refs):
    left_ref = refs[NX]
    total = jnp.zeros((ROWS, 1), f32)
    square = jnp.zeros((ROWS, 1), f32)
    for i in range(NZ):
        wide = frames_ref[i].astype(f32)
        total = total + jnp.sum(wide, axis=1, keepdims=True)
        square = square + jnp.sum(wide * wide, axis=1, keepdims=True)
    mean = total / QUARTER
    for i in range(NZ):
        cut = pl.ds(i * COLS, COLS)
        scaled = (frames_ref[i].astype(f32) - mean) * gain_ref[0:1, cut]
        left_ref[:, cut] = scaled.astype(bf16)
    sums = columns_to_rows(total, square).astype(bf16)
    for j, out_ref in enumerate(refs[:NX]):
        start = pl.multiple_of(place_ref[4 + j] * QUARTER, QUARTER)
        weight = weight_ref[pl.ds(start, QUARTER), 0 : 2 * COLS]
        out_ref[0:ROWS, :] = dot(left_ref[...], weight, 1, 0).astype(bf16)
        unit = jnp.sum(dot(gain_rows_ref[...], weight, 1, 0), axis=0, keepdims=True)
        out_ref[ROWS : ROWS + 16, :] = stacked_rows(split3(unit)).astype(bf16)
        out_ref[ROWS + 16 : ROWS + 32, :] = sums[:, 0:256]
        out_ref[ROWS + 32 : ROWS + 48, 0:128] = sums[:, 256:384]
        out_ref[ROWS + 32 : ROWS + 48, 128:256] = jnp.zeros((16, 128), bf16)


def gate_kernel(p0_ref, p1_ref, p2_ref, p3_ref, pre_ref, gated_ref, unit_ref, stat_ref):
    parts = (p0_ref, p1_ref, p2_ref, p3_ref)
    totals, squares, units = [], [], []
    for part_ref in parts:
        rows = jnp.concatenate(
            [part_ref[ROWS + 16 : ROWS + 32, :], part_ref[ROWS + 32 : ROWS + 48, 0:128]], axis=1
        )
        first, second = rows_to_columns(rows)
        totals.append(first)
        squares.append(second)
        pieces = part_ref[ROWS : ROWS + 16, :].astype(f32)
        units.append(jnp.sum(pieces, axis=0, keepdims=True))
    mean = sum(totals) / WIDTH
    inv_std = lax.rsqrt(sum(squares) / WIDTH - mean * mean + epsilon)
    pre = jnp.zeros((ROWS, 2 * COLS), f32)
    for i, part_ref in enumerate(parts):
        pre = pre + part_ref[0:ROWS, :].astype(f32)
        pre = pre + (totals[i] / QUARTER - mean) * units[i]
    pre = pre * inv_std
    pre_ref[...] = pre
    gated_ref[...] = (pre[:, 0:COLS] * jax.nn.sigmoid(pre[:, COLS:])).astype(bf16)
    unit_ref[...] = jnp.broadcast_to(sum(units), (8, 2 * COLS))
    lane = lax.broadcasted_iota(jnp.int32, (ROWS, 128), 1)
    stat_ref[...] = jnp.where(lane == 0, mean, inv_std)


def act_kernel(place_ref, g0_ref, g1_ref, g2_ref, g3_ref, weight_ref, out_ref):
    total = jnp.zeros((ROWS, QUARTER), f32)
    for j, grad_ref in enumerate((g0_ref, g1_ref, g2_ref, g3_ref)):
        start = pl.multiple_of(place_ref[j] * QUARTER, QUARTER)
        weight = weight_ref[pl.ds(start, QUARTER), 2 * COLS : 3 * COLS]
        total = total + dot(grad_ref[...], weight, 1, 1)
    for i in range(NZ):
        out_ref[i] = total[:, i * COLS : (i + 1) * COLS].astype(bf16)


def sum_kernel(parts_ref, out_ref):
    total = jnp.zeros((ROWS, COLS), f32)
    for i in range(NZ):
        total = total + parts_ref[i].astype(f32)
    out_ref[...] = total.astype(bf16)


CHUNKS = [(-16, 16), (0, 128), (128, 128), (256, 128), (ROWS, 16)]


def same_clip(border, start, count):
    row = lax.broadcasted_iota(jnp.int32, (count + 32, COLS), 0) + (start - 16)
    inside = (row < border).astype(jnp.int32)
    own = jnp.where(start < border, 1, 0)
    return inside == own


def fill_wide(wide_ref, gated_ref, low_ref, high_ref):
    wide_ref[0:EDGE, :] = low_ref[...].astype(f32)
    wide_ref[EDGE : EDGE + ROWS, :] = gated_ref[...].astype(f32)
    wide_ref[EDGE + ROWS :, :] = high_ref[...].astype(f32)


def forward_kernel(
    place_ref,
    gated_ref,
    low_ref,
    high_ref,
    taps_ref,
    activated_ref,
    slope_ref,
    wide_ref,
    masked_ref,
):
    border = place_ref[0]
    fill_wide(wide_ref, gated_ref, low_ref, high_ref)
    bias = taps_ref[K : K + 1, :]
    for start, count in CHUNKS:
        here = wide_ref[pl.ds(start - 16 + EDGE, count + 32), :]
        masked_ref[0 : count + 32, :] = jnp.where(same_clip(border, start, count), here, 0.0)
        conv = jnp.broadcast_to(bias, (count, COLS))
        for tap in range(K):
            conv = conv + taps_ref[tap : tap + 1, :] * masked_ref[1 + tap : 1 + tap + count, :]
        sig = jax.nn.sigmoid(conv)
        slope_ref[pl.ds(start + 16, count), :] = sig * (1.0 + conv * (1.0 - sig))
        if 0 <= start < ROWS:
            activated_ref[pl.ds(start, count), :] = (conv * sig).astype(bf16)


def backward_kernel(
    place_ref,
    gated_ref,
    low_ref,
    high_ref,
    act_ref,
    act_low_ref,
    act_high_ref,
    slope_ref,
    taps_ref,
    pre_ref,
    unit_ref,
    message_ref,
    small_ref,
    wide_ref,
    grad_ref,
    glu_ref,
    sums_ref,
    masked_ref,
    masked_grad_ref,
):
    border = place_ref[0]
    fill_wide(wide_ref, gated_ref, low_ref, high_ref)
    sums_ref[...] = jnp.zeros((K + 1, 8, COLS), f32)
    for start, count in CHUNKS:
        if start < 0:
            act = act_low_ref[...]
        elif start < ROWS:
            act = act_ref[pl.ds(start, count), :]
        else:
            act = act_high_ref[...]
        grad = act.astype(f32) * slope_ref[pl.ds(start + 16, count), :]
        grad = grad.astype(bf16).astype(f32)
        grad_ref[pl.ds(start + 16, count), :] = grad
        if 0 <= start < ROWS:
            here = wide_ref[pl.ds(start - 16 + EDGE, count + 32), :]
            masked_ref[...] = jnp.where(same_clip(border, start, count), here, 0.0)
            for tap in range(K):
                product = grad * masked_ref[1 + tap : 1 + tap + count, :]
                sums_ref[tap] += jnp.sum(product.reshape(count // 8, 8, COLS), axis=0)
            sums_ref[K] += jnp.sum(grad.reshape(count // 8, 8, COLS), axis=0)
    small_ref[...] = jnp.sum(sums_ref[...], axis=1)

    for start, count in CHUNKS[1:4]:
        here = grad_ref[pl.ds(start, count + 32), :]
        masked_grad_ref[...] = jnp.where(same_clip(border, start, count), here, 0.0)
        glu = jnp.zeros((count, COLS), f32)
        for tap in range(K):
            glu = glu + taps_ref[tap : tap + 1, :] * masked_grad_ref[31 - tap : 31 - tap + count, :]
        glu_ref[pl.ds(start, count), :] = glu

    glu = glu_ref[...]
    value_pre = pre_ref[:, 0:COLS]
    gate_pre = pre_ref[:, COLS:]
    gate_sig = jax.nn.sigmoid(gate_pre)
    value_grad = (glu * gate_sig).astype(bf16)
    gate_grad = (glu * value_pre * gate_sig * (1.0 - gate_sig)).astype(bf16)
    message_ref[0:ROWS, 0:COLS] = value_grad
    message_ref[0:ROWS, COLS:] = gate_grad
    value_wide = value_grad.astype(f32)
    gate_wide = gate_grad.astype(f32)
    first = jnp.sum(
        value_wide * unit_ref[0:1, 0:COLS] + gate_wide * unit_ref[0:1, COLS:],
        axis=1,
        keepdims=True,
    )
    second = jnp.sum(value_wide * value_pre + gate_wide * gate_pre, axis=1, keepdims=True)
    rows = columns_to_rows(first, second).astype(bf16)
    message_ref[ROWS : ROWS + 16, :] = rows[:, 0:256]
    message_ref[ROWS + 16 : ROWS + 32, 0:128] = rows[:, 256:384]
    message_ref[ROWS + 16 : ROWS + 32, 128:256] = jnp.zeros((16, 128), bf16)


def norm_kernel(place_ref, g0_ref, g1_ref, g2_ref, g3_ref, weight_ref, out_ref):
    total = jnp.zeros((ROWS, QUARTER), f32)
    rows = jnp.zeros((16, ROWS), f32)
    for j, grad_ref in enumerate((g0_ref, g1_ref, g2_ref, g3_ref)):
        start = pl.multiple_of(place_ref[j] * QUARTER, QUARTER)
        weight = weight_ref[pl.ds(start, QUARTER), 0 : 2 * COLS]
        total = total + dot(grad_ref[0:ROWS, :], weight, 1, 1)
        here = jnp.concatenate(
            [grad_ref[ROWS : ROWS + 16, :], grad_ref[ROWS + 16 : ROWS + 32, 0:128]], axis=1
        )
        rows = rows + here.astype(f32)
    first = rows[0:1] + rows[1:2] + rows[2:3]
    second = rows[3:4] + rows[4:5] + rows[5:6]
    sums = stacked_rows(split3(first) + split3(second)).astype(bf16)
    for i in range(NZ):
        out_ref[i, 0:ROWS, :] = total[:, i * COLS : (i + 1) * COLS].astype(bf16)
        for j in range(3):
            out_ref[i, ROWS + 16 * j : ROWS + 16 * j + 16, :] = sums[:, j * 128 : (j + 1) * 128]


def weight_kernel(
    place_ref,
    frames_ref,
    gain_ref,
    stat_ref,
    g0_ref,
    g1_ref,
    g2_ref,
    g3_ref,
    out_ref,
    left_ref,
):
    mean = stat_ref[:, 0:1]
    inv_std = stat_ref[:, 1:2]
    for i in range(NZ):
        cut = pl.ds(i * COLS, COLS)
        scaled = (frames_ref[i].astype(f32) - mean) * inv_std * gain_ref[0:1, cut]
        left_ref[:, cut] = scaled.astype(bf16)
    for j, grad_ref in enumerate((g0_ref, g1_ref, g2_ref, g3_ref)):
        start = pl.multiple_of(place_ref[j] * QUARTER, QUARTER)
        out = dot(left_ref[...], grad_ref[0:ROWS, :], 0, 0)
        out_ref[pl.ds(start, QUARTER), :] = out.astype(bf16)


def out_kernel(place_ref, act_ref, g0_ref, g1_ref, g2_ref, g3_ref, weight_ref, *refs):
    enc_refs = refs[:NX]
    kept_ref, given_ref, left_ref, grad_ref = refs[NX:]
    half = QUARTER // NK
    for i in range(NZ):
        left_ref[i * COLS // half, :, pl.ds(i * COLS % half, COLS)] = act_ref[i, 0:ROWS, :]
    for j, enc_ref in enumerate(enc_refs):
        total = jnp.zeros((ROWS, COLS), f32)
        for h in range(NK):
            start = pl.multiple_of(place_ref[4 + j] * QUARTER + h * half, half)
            weight = weight_ref[pl.ds(start, half), 2 * COLS : 3 * COLS]
            total = total + dot(left_ref[h], weight, 1, 0)
        enc_ref[...] = total.astype(bf16)
    for i in range(NY):
        source = place_ref[10 + i]
        for j, right_ref in enumerate((g0_ref, g1_ref, g2_ref, g3_ref)):

            @pl.when(source == j)
            def _(right_ref=right_ref, i=i):
                grad_ref[:, i * COLS : (i + 1) * COLS] = right_ref[...]

    core = place_ref[9]
    for out_ref, which in ((given_ref, 1 - core), (kept_ref, core)):
        out = dot(left_ref[which], grad_ref[...], 0, 0).astype(bf16)
        for i in range(NY):
            out_ref[i] = out[:, i * COLS : (i + 1) * COLS]


def input_kernel(parts_ref, frames_ref, grad_ref, stat_ref, gain_ref, out_ref, small_ref):
    normed_grad = jnp.zeros((ROWS, COLS), f32)
    rows = jnp.zeros((16, ROWS), f32)
    for i in range(NZ):
        normed_grad = normed_grad + parts_ref[i, 0:ROWS, :].astype(f32)
        here = [parts_ref[i, ROWS + 16 * j : ROWS + 16 * j + 16, :] for j in range(3)]
        rows = rows + jnp.concatenate(here, axis=1).astype(f32)
    first = rows[0:1] + rows[1:2] + rows[2:3]
    second = rows[3:4] + rows[4:5] + rows[5:6]
    sums = stacked_rows(split3(first) + split3(second)).astype(bf16)
    first, second = rows_to_columns(sums)
    mean = stat_ref[:, 0:1]
    inv_std = stat_ref[:, 1:2]
    centred = (frames_ref[...].astype(f32) - mean) * inv_std
    hat = normed_grad * gain_ref[0:1, :]
    out = grad_ref[...].astype(f32) + inv_std * (hat - first / WIDTH - centred * (second / WIDTH))
    out_ref[...] = out.astype(bf16)
    gain_term = jnp.sum(normed_grad * centred, axis=0, keepdims=True)
    small_ref[...] = jnp.broadcast_to(gain_term, (8, COLS))


def swap_xy(block):
    return lax.ppermute(
        block, ("x", "y"), [(a * NY + b, b * NY + a) for a in range(NX) for b in range(NY)]
    )


def neighbours(block, width):
    place = [k * NY + y for y in range(NY) for k in range(NK)]
    forward = list(zip(place[:-1], place[1:]))
    backward = [(target, source) for source, target in forward]
    low = lax.ppermute(block[-width:], ("k", "y"), forward)
    high = lax.ppermute(block[:width], ("k", "y"), backward)
    return low, high


def exchange(parts, axis):
    return lax.all_to_all(parts, axis, 0, 0, tiled=True)


def gathered(block, axis, count):
    return exchange(jnp.broadcast_to(block[None], (count,) + block.shape), axis)


def shifted(block, axis, count, shift):
    return lax.ppermute(block, axis, [(i, (i + shift) % count) for i in range(count)])


def spread(block, axis, count):
    return [block] + [shifted(block, axis, count, j) for j in range(1, count)]


def after(value, *others):
    return lax.optimization_barrier((value,) + others)[0]


def shards(frames, gain, w_value, w_gate, kernel, bias, w_out, grad_out):
    x_index = lax.axis_index("x")
    k_index = lax.axis_index("k")
    row_start = (lax.axis_index("y") * NK + k_index) * ROWS
    col_start = (x_index * NZ + lax.axis_index("z")) * COLS
    local_gain = lax.dynamic_slice_in_dim(gain, col_start, COLS, 0)[None]
    quarter_gain = lax.dynamic_slice_in_dim(gain, x_index * QUARTER, QUARTER, 0)[None]
    high = lax.reduce_precision(quarter_gain, 8, 7)
    middle = lax.reduce_precision(quarter_gain - high, 8, 7)
    low = quarter_gain - high - middle
    gain_rows = jnp.pad(jnp.concatenate([high, middle, low], axis=0), ((0, 13), (0, 0)))
    gain_rows = gain_rows.astype(bf16)
    y_index = lax.axis_index("y")
    steps = jnp.arange(NX, dtype=jnp.int32)
    below = (x_index + NX - steps) % NX
    above = (x_index + steps) % NX
    distance = (x_index + 2 * NX - (y_index + steps) % NY) % NX
    edges = jnp.stack([LEN - row_start, k_index]).astype(jnp.int32)
    place = jnp.concatenate([below, above, edges, distance]).astype(jnp.int32)
    border = place[8:9]

    weights = lax.all_gather(
        jnp.concatenate([w_value, w_gate, w_out], axis=1), TIME, axis=0, tiled=True
    )

    frames = swap_xy(frames)
    frames_z = gathered(frames, "z", NZ)
    grad_out = swap_xy(after(grad_out, frames))
    grads = spread(grad_out, "x", NX)
    taps = swap_xy(after(jnp.concatenate([kernel, bias[None, :]], axis=0), grads[1]))

    pre_parts = call(
        project_kernel,
        [shape((ROWS + 48, 2 * COLS), bf16) for _ in range(NX)],
        (place, frames_z, quarter_gain, gain_rows, weights),
        smem=(0,),
        scratch=[pltpu.VMEM((ROWS, QUARTER), bf16)],
    )
    pre_moved = [pre_parts[0]] + [shifted(pre_parts[j], "x", NX, j) for j in range(1, NX)]
    held = lax.optimization_barrier((grads, pre_parts[0]))[0]
    act_parts = call(
        act_kernel, shape((NZ, ROWS, COLS), bf16), (place, *held, weights), smem=(0,)
    )
    act_grad = call(sum_kernel, shape((ROWS, COLS), bf16), (exchange(act_parts, "z"),))
    pre, gated, unit, stat = call(
        gate_kernel,
        [
            shape((ROWS, 2 * COLS), f32),
            shape((ROWS, COLS), bf16),
            shape((8, 2 * COLS), f32),
            shape((ROWS, 128), f32),
        ],
        tuple(pre_moved),
    )
    gated_low, gated_high = neighbours(gated, EDGE)
    act_low, act_high = neighbours(act_grad, 16)
    activated, slope = call(
        forward_kernel,
        [shape((ROWS, COLS), bf16), shape((ROWS + 32, COLS), f32)],
        (border, gated, gated_low, gated_high, taps),
        smem=(0,),
        scratch=[
            pltpu.VMEM((ROWS + 2 * EDGE, COLS), f32),
            pltpu.VMEM((160, COLS), f32),
        ],
    )
    act_z = gathered(activated, "z", NZ)
    message, small = call(
        backward_kernel,
        [shape((ROWS + 32, 2 * COLS), bf16), shape((K + 1, COLS), f32)],
        (
            border,
            gated,
            gated_low,
            gated_high,
            act_grad,
            act_low,
            act_high,
            slope,
            taps,
            pre,
            unit,
        ),
        smem=(0,),
        scratch=[
            pltpu.VMEM((ROWS + 2 * EDGE, COLS), f32),
            pltpu.VMEM((ROWS + 32, COLS), f32),
            pltpu.VMEM((ROWS, COLS), f32),
            pltpu.VMEM((K + 1, 8, COLS), f32),
            pltpu.VMEM((160, COLS), f32),
            pltpu.VMEM((160, COLS), f32),
        ],
    )

    vg_grads = spread(message, "x", NX)
    norm_parts = call(
        norm_kernel,
        shape((NZ, ROWS + 48, COLS), bf16),
        (place, *vg_grads, weights),
        smem=(0,),
    )
    norm_moved = exchange(norm_parts, "z")
    held = lax.optimization_barrier((vg_grads, norm_parts))[0]
    weight_parts = call(
        weight_kernel,
        shape((NY * QUARTER, 2 * COLS), bf16),
        (place, frames_z, quarter_gain, stat, *held),
        smem=(0,),
        scratch=[pltpu.VMEM((ROWS, QUARTER), bf16)],
    )
    in_weight = lax.psum_scatter(
        weight_parts, TIME, scatter_dimension=0, tiled=True
    ).astype(f32)

    out_parts = call(
        out_kernel,
        [shape((ROWS, COLS), bf16) for _ in range(NX)]
        + [shape((NY, QUARTER // NK, COLS), bf16) for _ in range(2)],
        (place, after(act_z, norm_parts), *grads, weights),
        smem=(0,),
        scratch=[
            pltpu.VMEM((NK, ROWS, QUARTER // NK), bf16),
            pltpu.VMEM((ROWS, NY * COLS), bf16),
        ],
    )
    kept, given = out_parts[NX:]
    other = lax.ppermute(given, "k", [(0, 1), (1, 0)])
    both = [(kept[i].astype(f32) + other[i].astype(f32)) for i in range(NY)]
    grad_out_weight = both[0]
    for i in range(1, NY):
        grad_out_weight = grad_out_weight + shifted(both[i].astype(bf16), "y", NY, i).astype(f32)
    enc_sum = out_parts[0].astype(f32)
    for j in range(1, NX):
        enc_sum = enc_sum + shifted(out_parts[j], "x", NX, j).astype(f32)
    encoded = swap_xy((frames.astype(f32) + enc_sum).astype(bf16))

    input_grad, gain_term = call(
        input_kernel,
        [shape((ROWS, COLS), bf16), shape((8, COLS), f32)],
        (norm_moved, frames, grad_out, stat, local_gain),
    )
    input_grad = swap_xy(input_grad)

    small = jnp.concatenate([small, gain_term], axis=0)
    small = small + lax.ppermute(small, "k", [(0, 1), (1, 0)])
    arrived = []
    for shift in range(NX):
        route = [
            (a * NY + b, ((b + shift) % NX) * NY + a) for a in range(NX) for b in range(NY)
        ]
        arrived.append(lax.ppermute(small, ("x", "y"), route))
    small = sum(arrived)
    return (
        encoded,
        input_grad,
        in_weight[:, :COLS],
        in_weight[:, COLS:],
        small[:K],
        small[K],
        grad_out_weight,
        small[K + 1],
    )


def solution(mesh):
    fine = Mesh(mesh.devices.reshape(NX, NK, NY, NZ), ("x", "k", "y", "z"))
    both = P(ROW, COL)
    return jax.shard_map(
        shards,
        mesh=fine,
        in_specs=(both, P(), both, both, P(None, COL), P(COL), both, both),
        out_specs=(both, both, both, both, P(None, COL), P(COL), both, P(COL)),
        check_vma=False,
    )
```

```python
import jax
import jax.numpy as jnp
from jax import lax
from jax.experimental import pallas as pl
from jax.experimental.pallas import tpu as pltpu
from jax.sharding import Mesh, PartitionSpec as P

K = 31
LEN = 2048
HALF = K // 2
NX, NK, NY, NZ = 4, 2, 4, 8
ROW = ("x", "k")
COL = ("y", "z")
TIME = ("y", "k")
ROWS = 384
COLS = 128
QUARTER = COLS * NZ
WIDTH = QUARTER * NX
EDGE = 32
IN = (0, 2 * COLS)
OUT = (2 * COLS, COLS)

epsilon = 1e-05
f32 = jnp.float32
bf16 = jnp.bfloat16


def dot(left, right, left_dim, right_dim):
    return lax.dot_general(
        left, right, (((left_dim,), (right_dim,)), ((), ())), preferred_element_type=f32
    )


def split3(value):
    high = value.astype(bf16)
    rest = value - high.astype(f32)
    middle = rest.astype(bf16)
    low = (rest - middle.astype(f32)).astype(bf16)
    return high, middle, low


def one_hot():
    lane = lax.broadcasted_iota(jnp.int32, (16, 128), 1)
    row = lax.broadcasted_iota(jnp.int32, (16, 128), 0)
    return jnp.where(lane == row, 1.0, 0.0).astype(bf16)


def columns_to_rows(first, second):
    lane = lax.broadcasted_iota(jnp.int32, (first.shape[0], 128), 1)
    grid = jnp.zeros((first.shape[0], 128), f32)
    for j, piece in enumerate(split3(first) + split3(second)):
        grid = jnp.where(lane == j, piece.astype(f32), grid)
    return dot(one_hot(), grid.astype(bf16), 1, 1)


def rows_to_columns(rows):
    grid = dot(rows, one_hot(), 0, 0)
    first = grid[:, 0:1] + grid[:, 1:2] + grid[:, 2:3]
    second = grid[:, 3:4] + grid[:, 4:5] + grid[:, 5:6]
    return first, second


def stacked_rows(values):
    row = lax.broadcasted_iota(jnp.int32, (16, values[0].shape[1]), 0)
    out = jnp.zeros((16, values[0].shape[1]), f32)
    for j, value in enumerate(values):
        out = jnp.where(row == j, value.astype(f32), out)
    return out


def call(body, out_shape, args, smem=(), near=(), scratch=(), cuts=()):
    cuts = dict(cuts)
    single = not isinstance(out_shape, (list, tuple))
    outs = [out_shape] if single else list(out_shape)
    count = len(args)
    moved = [i for i in range(count) if i not in smem and i not in near]
    buffers = []
    for i in moved:
        dims = args[i].shape
        if i in cuts:
            dims = (dims[0], cuts[i][1])
        buffers.append(pltpu.VMEM(dims, args[i].dtype))
    for out in outs:
        buffers.append(pltpu.VMEM(out.shape, out.dtype))

    def whole(*refs):
        refs = list(refs)
        inputs, refs = refs[:count], refs[count:]
        results, refs = refs[: len(outs)], refs[len(outs) :]
        held, refs = refs[: len(buffers)], refs[len(buffers) :]
        sems, extra = refs[0], refs[1:]
        copies = []
        for place, i in enumerate(moved):
            source = inputs[i]
            if i in cuts:
                source = source.at[:, pl.ds(cuts[i][0], cuts[i][1])]
            copies.append(pltpu.make_async_copy(source, held[place], sems.at[place]))
            inputs[i] = held[place]
        for copy in copies:
            copy.start()
        for copy in copies:
            copy.wait()
        body(*inputs, *held[len(moved) :], *extra)
        copies = []
        for place, result in enumerate(results, len(moved)):
            copies.append(pltpu.make_async_copy(held[place], result, sems.at[place]))
        for copy in copies:
            copy.start()
        for copy in copies:
            copy.wait()

    hbm = pl.BlockSpec(memory_space=pltpu.MemorySpace.HBM)
    spaces = [
        pltpu.MemorySpace.SMEM
        if i in smem
        else (pltpu.MemorySpace.VMEM if i in near else pltpu.MemorySpace.HBM)
        for i in range(count)
    ]
    made = pl.pallas_call(
        whole,
        out_shape=[pltpu.HBM(out.shape, out.dtype) for out in outs],
        in_specs=[pl.BlockSpec(memory_space=space) for space in spaces],
        out_specs=[hbm] * len(outs),
        scratch_shapes=buffers + [pltpu.SemaphoreType.DMA((len(buffers),))] + list(scratch),
        compiler_params=pltpu.CompilerParams(vmem_limit_bytes=24 * 1024 * 1024),
        name=body.__name__,
    )(
        *[
            pltpu.with_memory_space_constraint(arg, pltpu.HBM) if i in moved else arg
            for i, arg in enumerate(args)
        ]
    )
    return made[0] if single else made


def shape(dims, kind):
    return jax.ShapeDtypeStruct(dims, kind)


def project_kernel(place_ref, frames_ref, gain_ref, gain_rows_ref, weight_ref, *refs):
    left_ref = refs[NX]
    total = jnp.zeros((ROWS, 1), f32)
    square = jnp.zeros((ROWS, 1), f32)
    for i in range(NZ):
        wide = frames_ref[i].astype(f32)
        total = total + jnp.sum(wide, axis=1, keepdims=True)
        square = square + jnp.sum(wide * wide, axis=1, keepdims=True)
    mean = total / QUARTER
    for i in range(NZ):
        cut = pl.ds(i * COLS, COLS)
        scaled = (frames_ref[i].astype(f32) - mean) * gain_ref[0:1, cut]
        left_ref[:, cut] = scaled.astype(bf16)
    sums = columns_to_rows(total, square).astype(bf16)
    for j, out_ref in enumerate(refs[:NX]):
        start = pl.multiple_of(place_ref[4 + j] * QUARTER, QUARTER)
        weight = weight_ref[pl.ds(start, QUARTER), :]
        out_ref[0:ROWS, :] = dot(left_ref[...], weight, 1, 0).astype(bf16)
        unit = jnp.sum(dot(gain_rows_ref[...], weight, 1, 0), axis=0, keepdims=True)
        out_ref[ROWS : ROWS + 16, :] = stacked_rows(split3(unit)).astype(bf16)
        out_ref[ROWS + 16 : ROWS + 32, :] = sums[:, 0:256]
        out_ref[ROWS + 32 : ROWS + 48, 0:128] = sums[:, 256:384]
        out_ref[ROWS + 32 : ROWS + 48, 128:256] = jnp.zeros((16, 128), bf16)


def gate_kernel(p0_ref, p1_ref, p2_ref, p3_ref, pre_ref, gated_ref, unit_ref, stat_ref):
    parts = (p0_ref, p1_ref, p2_ref, p3_ref)
    totals, squares, units = [], [], []
    for part_ref in parts:
        rows = jnp.concatenate(
            [part_ref[ROWS + 16 : ROWS + 32, :], part_ref[ROWS + 32 : ROWS + 48, 0:128]], axis=1
        )
        first, second = rows_to_columns(rows)
        totals.append(first)
        squares.append(second)
        pieces = part_ref[ROWS : ROWS + 16, :].astype(f32)
        units.append(jnp.sum(pieces, axis=0, keepdims=True))
    mean = sum(totals) / WIDTH
    inv_std = lax.rsqrt(sum(squares) / WIDTH - mean * mean + epsilon)
    pre = jnp.zeros((ROWS, 2 * COLS), f32)
    for i, part_ref in enumerate(parts):
        pre = pre + part_ref[0:ROWS, :].astype(f32)
        pre = pre + (totals[i] / QUARTER - mean) * units[i]
    pre = pre * inv_std
    pre_ref[...] = pre
    gated_ref[...] = (pre[:, 0:COLS] * jax.nn.sigmoid(pre[:, COLS:])).astype(bf16)
    unit_ref[...] = jnp.broadcast_to(sum(units), (8, 2 * COLS))
    lane = lax.broadcasted_iota(jnp.int32, (ROWS, 128), 1)
    stat_ref[...] = jnp.where(lane == 0, mean, inv_std)


def act_kernel(place_ref, g0_ref, g1_ref, g2_ref, g3_ref, weight_ref, out_ref):
    total = jnp.zeros((ROWS, QUARTER), f32)
    for j, grad_ref in enumerate((g0_ref, g1_ref, g2_ref, g3_ref)):
        start = pl.multiple_of(place_ref[j] * QUARTER, QUARTER)
        weight = weight_ref[pl.ds(start, QUARTER), :]
        total = total + dot(grad_ref[...], weight, 1, 1)
    for i in range(NZ):
        out_ref[i] = total[:, i * COLS : (i + 1) * COLS].astype(bf16)


def sum_kernel(parts_ref, out_ref):
    total = jnp.zeros((ROWS, COLS), f32)
    for i in range(NZ):
        total = total + parts_ref[i].astype(f32)
    out_ref[...] = total.astype(bf16)


CHUNKS = [(-16, 16), (0, 128), (128, 128), (256, 128), (ROWS, 16)]


def same_clip(border, start, count):
    row = lax.broadcasted_iota(jnp.int32, (count + 32, COLS), 0) + (start - 16)
    inside = (row < border).astype(jnp.int32)
    own = jnp.where(start < border, 1, 0)
    return inside == own


def conv_kernel(
    place_ref,
    gated_ref,
    act_ref,
    low_ref,
    high_ref,
    taps_ref,
    pre_ref,
    unit_ref,
    activated_ref,
    message_ref,
    small_ref,
    wide_ref,
    grad_ref,
    glu_ref,
    sums_ref,
    masked_ref,
    masked_grad_ref,
    kernel_ref,
):
    border = place_ref[0]
    total = jnp.zeros((K + 1, COLS), f32)
    for i in range(3):
        total = total + taps_ref[pl.ds(ROWS + i * (K + 1), K + 1), :].astype(f32)
    kernel_ref[...] = total
    wide_ref[0:EDGE, :] = low_ref[0:EDGE, :].astype(f32)
    wide_ref[EDGE : EDGE + ROWS, :] = gated_ref[...].astype(f32)
    wide_ref[EDGE + ROWS :, :] = high_ref[0:EDGE, :].astype(f32)
    sums_ref[...] = jnp.zeros((K + 1, 8, COLS), f32)
    bias = kernel_ref[K : K + 1, :]
    for start, count in CHUNKS:
        here = wide_ref[pl.ds(start - 16 + EDGE, count + 32), :]
        masked_ref[0 : count + 32, :] = jnp.where(same_clip(border, start, count), here, 0.0)
        conv = jnp.broadcast_to(bias, (count, COLS))
        for tap in range(K):
            conv = conv + kernel_ref[tap : tap + 1, :] * masked_ref[1 + tap : 1 + tap + count, :]
        sig = jax.nn.sigmoid(conv)
        if start < 0:
            act = low_ref[EDGE:, :]
        elif start < ROWS:
            act = act_ref[pl.ds(start, count), :]
        else:
            act = high_ref[EDGE:, :]
        grad = (act.astype(f32) * sig * (1.0 + conv * (1.0 - sig))).astype(bf16).astype(f32)
        grad_ref[pl.ds(start + 16, count), :] = grad
        if 0 <= start < ROWS:
            activated_ref[pl.ds(start, count), :] = (conv * sig).astype(bf16)
            for tap in range(K):
                product = grad * masked_ref[1 + tap : 1 + tap + count, :]
                sums_ref[tap] += jnp.sum(product.reshape(count // 8, 8, COLS), axis=0)
            sums_ref[K] += jnp.sum(grad.reshape(count // 8, 8, COLS), axis=0)
    small_ref[...] = jnp.sum(sums_ref[...], axis=1)

    for start, count in CHUNKS[1:4]:
        here = grad_ref[pl.ds(start, count + 32), :]
        masked_grad_ref[...] = jnp.where(same_clip(border, start, count), here, 0.0)
        glu = jnp.zeros((count, COLS), f32)
        for tap in range(K):
            glu = glu + kernel_ref[tap : tap + 1, :] * masked_grad_ref[31 - tap : 31 - tap + count, :]
        glu_ref[pl.ds(start, count), :] = glu

    glu = glu_ref[...]
    value_pre = pre_ref[:, 0:COLS]
    gate_pre = pre_ref[:, COLS:]
    gate_sig = jax.nn.sigmoid(gate_pre)
    value_grad = (glu * gate_sig).astype(bf16)
    gate_grad = (glu * value_pre * gate_sig * (1.0 - gate_sig)).astype(bf16)
    message_ref[0:ROWS, 0:COLS] = value_grad
    message_ref[0:ROWS, COLS:] = gate_grad
    value_wide = value_grad.astype(f32)
    gate_wide = gate_grad.astype(f32)
    first = jnp.sum(
        value_wide * unit_ref[0:1, 0:COLS] + gate_wide * unit_ref[0:1, COLS:],
        axis=1,
        keepdims=True,
    )
    second = jnp.sum(value_wide * value_pre + gate_wide * gate_pre, axis=1, keepdims=True)
    rows = columns_to_rows(first, second).astype(bf16)
    message_ref[ROWS : ROWS + 16, :] = rows[:, 0:256]
    message_ref[ROWS + 16 : ROWS + 32, 0:128] = rows[:, 256:384]
    message_ref[ROWS + 16 : ROWS + 32, 128:256] = jnp.zeros((16, 128), bf16)


def norm_kernel(place_ref, g0_ref, g1_ref, g2_ref, g3_ref, weight_ref, out_ref):
    total = jnp.zeros((ROWS, QUARTER), f32)
    rows = jnp.zeros((16, ROWS), f32)
    for j, grad_ref in enumerate((g0_ref, g1_ref, g2_ref, g3_ref)):
        start = pl.multiple_of(place_ref[j] * QUARTER, QUARTER)
        weight = weight_ref[pl.ds(start, QUARTER), :]
        total = total + dot(grad_ref[0:ROWS, :], weight, 1, 1)
        here = jnp.concatenate(
            [grad_ref[ROWS : ROWS + 16, :], grad_ref[ROWS + 16 : ROWS + 32, 0:128]], axis=1
        )
        rows = rows + here.astype(f32)
    first = rows[0:1] + rows[1:2] + rows[2:3]
    second = rows[3:4] + rows[4:5] + rows[5:6]
    sums = stacked_rows(split3(first) + split3(second)).astype(bf16)
    for i in range(NZ):
        out_ref[i, 0:ROWS, :] = total[:, i * COLS : (i + 1) * COLS].astype(bf16)
        for j in range(3):
            out_ref[i, ROWS + 16 * j : ROWS + 16 * j + 16, :] = sums[:, j * 128 : (j + 1) * 128]


def weight_kernel(
    place_ref,
    frames_ref,
    gain_ref,
    stat_ref,
    g0_ref,
    g1_ref,
    g2_ref,
    g3_ref,
    out_ref,
    left_ref,
):
    mean = stat_ref[:, 0:1]
    inv_std = stat_ref[:, 1:2]
    for i in range(NZ):
        cut = pl.ds(i * COLS, COLS)
        scaled = (frames_ref[i].astype(f32) - mean) * inv_std * gain_ref[0:1, cut]
        left_ref[:, cut] = scaled.astype(bf16)
    for j, grad_ref in enumerate((g0_ref, g1_ref, g2_ref, g3_ref)):
        start = pl.multiple_of(place_ref[j] * QUARTER, QUARTER)
        out = dot(left_ref[...], grad_ref[0:ROWS, :], 0, 0)
        out_ref[pl.ds(start, QUARTER), :] = out.astype(bf16)


def out_kernel(place_ref, act_ref, g0_ref, g1_ref, g2_ref, g3_ref, weight_ref, *refs):
    enc_refs = refs[:NX]
    kept_ref, given_ref, left_ref, grad_ref = refs[NX:]
    half = QUARTER // NK
    for i in range(NZ):
        left_ref[i * COLS // half, :, pl.ds(i * COLS % half, COLS)] = act_ref[i, 0:ROWS, :]
    for j, enc_ref in enumerate(enc_refs):
        total = jnp.zeros((ROWS, COLS), f32)
        for h in range(NK):
            start = pl.multiple_of(place_ref[4 + j] * QUARTER + h * half, half)
            weight = weight_ref[pl.ds(start, half), :]
            total = total + dot(left_ref[h], weight, 1, 0)
        enc_ref[...] = total.astype(bf16)
    for i in range(NY):
        source = place_ref[10 + i]
        for j, right_ref in enumerate((g0_ref, g1_ref, g2_ref, g3_ref)):

            @pl.when(source == j)
            def _(right_ref=right_ref, i=i):
                grad_ref[:, i * COLS : (i + 1) * COLS] = right_ref[...]

    core = place_ref[9]
    for out_ref, which in ((given_ref, 1 - core), (kept_ref, core)):
        out = dot(left_ref[which], grad_ref[...], 0, 0).astype(bf16)
        for i in range(NY):
            out_ref[i] = out[:, i * COLS : (i + 1) * COLS]


def input_kernel(parts_ref, frames_ref, grad_ref, stat_ref, gain_ref, out_ref, small_ref):
    normed_grad = jnp.zeros((ROWS, COLS), f32)
    rows = jnp.zeros((16, ROWS), f32)
    for i in range(NZ):
        normed_grad = normed_grad + parts_ref[i, 0:ROWS, :].astype(f32)
        here = [parts_ref[i, ROWS + 16 * j : ROWS + 16 * j + 16, :] for j in range(3)]
        rows = rows + jnp.concatenate(here, axis=1).astype(f32)
    first = rows[0:1] + rows[1:2] + rows[2:3]
    second = rows[3:4] + rows[4:5] + rows[5:6]
    sums = stacked_rows(split3(first) + split3(second)).astype(bf16)
    first, second = rows_to_columns(sums)
    mean = stat_ref[:, 0:1]
    inv_std = stat_ref[:, 1:2]
    centred = (frames_ref[...].astype(f32) - mean) * inv_std
    hat = normed_grad * gain_ref[0:1, :]
    out = grad_ref[...].astype(f32) + inv_std * (hat - first / WIDTH - centred * (second / WIDTH))
    out_ref[...] = out.astype(bf16)
    gain_term = jnp.sum(normed_grad * centred, axis=0, keepdims=True)
    small_ref[...] = jnp.broadcast_to(gain_term, (8, COLS))


def swap_xy(block):
    return lax.ppermute(
        block, ("x", "y"), [(a * NY + b, b * NY + a) for a in range(NX) for b in range(NY)]
    )


def neighbours(upper, lower):
    place = [k * NY + y for y in range(NY) for k in range(NK)]
    forward = list(zip(place[:-1], place[1:]))
    backward = [(target, source) for source, target in forward]
    low = lax.ppermute(upper, ("k", "y"), forward)
    high = lax.ppermute(lower, ("k", "y"), backward)
    return low, high


def exchange(parts, axis):
    return lax.all_to_all(parts, axis, 0, 0, tiled=True)


def gathered(block, axis, count):
    return exchange(jnp.broadcast_to(block[None], (count,) + block.shape), axis)


def shifted(block, axis, count, shift):
    return lax.ppermute(block, axis, [(i, (i + shift) % count) for i in range(count)])


def spread(block, axis, count):
    return [block] + [shifted(block, axis, count, j) for j in range(1, count)]


def pieces(value):
    out = []
    for _ in range(3):
        piece = lax.reduce_precision(value, 8, 7)
        out.append(piece.astype(bf16))
        value = value - piece
    return jnp.stack(out)


def after(value, *others):
    return lax.optimization_barrier((value,) + others)[0]


def shards(frames, gain, w_value, w_gate, kernel, bias, w_out, grad_out):
    x_index = lax.axis_index("x")
    k_index = lax.axis_index("k")
    row_start = (lax.axis_index("y") * NK + k_index) * ROWS
    col_start = (x_index * NZ + lax.axis_index("z")) * COLS
    local_gain = lax.dynamic_slice_in_dim(gain, col_start, COLS, 0)[None]
    quarter_gain = lax.dynamic_slice_in_dim(gain, x_index * QUARTER, QUARTER, 0)[None]
    gain_rows = jnp.pad(pieces(quarter_gain)[:, 0], ((0, 13), (0, 0)))
    y_index = lax.axis_index("y")
    steps = jnp.arange(NX, dtype=jnp.int32)
    below = (x_index + NX - steps) % NX
    above = (x_index + steps) % NX
    distance = (x_index + 2 * NX - (y_index + steps) % NY) % NX
    edges = jnp.stack([LEN - row_start, k_index]).astype(jnp.int32)
    place = jnp.concatenate([below, above, edges, distance]).astype(jnp.int32)
    border = place[8:9]

    weights = lax.all_gather(
        jnp.concatenate([w_value, w_gate, w_out], axis=1), TIME, axis=0, tiled=True
    )

    frames = swap_xy(frames)
    frames_z = gathered(frames, "z", NZ)
    taps = jnp.concatenate([kernel, bias[None, :]], axis=0)
    packed = jnp.concatenate([grad_out, pieces(taps).reshape(3 * (K + 1), COLS)], axis=0)
    packed = swap_xy(after(packed, frames))
    grad_out = packed[:ROWS]
    grads = spread(grad_out, "x", NX)

    act_parts = call(
        act_kernel, shape((NZ, ROWS, COLS), bf16), (place, *grads, weights), smem=(0,), near=(1, 2, 3, 4), cuts={5: OUT}
    )
    act_moved = exchange(act_parts, "z")
    pre_parts = call(
        project_kernel,
        [shape((ROWS + 48, 2 * COLS), bf16) for _ in range(NX)],
        (place, after(frames_z, act_parts), quarter_gain, gain_rows, weights),
        smem=(0,),
        near=(1,),
        cuts={4: IN},
        scratch=[pltpu.VMEM((ROWS, QUARTER), bf16)],
    )
    pre_moved = [pre_parts[0]] + [shifted(pre_parts[j], "x", NX, j) for j in range(1, NX)]
    pre, gated, unit, stat = call(
        gate_kernel,
        [
            shape((ROWS, 2 * COLS), f32),
            shape((ROWS, COLS), bf16),
            shape((8, 2 * COLS), f32),
            shape((ROWS, 128), f32),
        ],
        tuple(pre_moved),
        near=(1, 2, 3),
    )
    act_grad = call(sum_kernel, shape((ROWS, COLS), bf16), (act_moved,), near=(0,))
    low, high = neighbours(
        jnp.concatenate([gated[-EDGE:], act_grad[-16:]], axis=0),
        jnp.concatenate([gated[:EDGE], act_grad[:16]], axis=0),
    )
    activated, message, small = call(
        conv_kernel,
        [
            shape((ROWS, COLS), bf16),
            shape((ROWS + 32, 2 * COLS), bf16),
            shape((K + 1, COLS), f32),
        ],
        (border, gated, act_grad, low, high, packed, pre, unit),
        smem=(0,),
        near=(3, 4),
        scratch=[
            pltpu.VMEM((ROWS + 2 * EDGE, COLS), f32),
            pltpu.VMEM((ROWS + 32, COLS), f32),
            pltpu.VMEM((ROWS, COLS), f32),
            pltpu.VMEM((K + 1, 8, COLS), f32),
            pltpu.VMEM((160, COLS), f32),
            pltpu.VMEM((160, COLS), f32),
            pltpu.VMEM((K + 1, COLS), f32),
        ],
    )
    act_z = gathered(activated, "z", NZ)

    vg_grads = spread(message, "x", NX)
    norm_parts = call(
        norm_kernel,
        shape((NZ, ROWS + 48, COLS), bf16),
        (place, *vg_grads, after(weights, act_z)),
        smem=(0,),
        near=(2, 3, 4),
        cuts={5: IN},
    )
    norm_moved = exchange(norm_parts, "z")
    held = lax.optimization_barrier((vg_grads, norm_parts))[0]
    weight_parts = call(
        weight_kernel,
        shape((NY * QUARTER, 2 * COLS), bf16),
        (place, frames_z, quarter_gain, stat, *held),
        smem=(0,),
        near=(5, 6, 7),
        scratch=[pltpu.VMEM((ROWS, QUARTER), bf16)],
    )
    in_weight = lax.psum_scatter(
        weight_parts, TIME, scatter_dimension=0, tiled=True
    ).astype(f32)

    out_parts = call(
        out_kernel,
        [shape((ROWS, COLS), bf16) for _ in range(NX)]
        + [shape((NY, QUARTER // NK, COLS), bf16) for _ in range(2)],
        (place, act_z, *after(grads, norm_parts), weights),
        smem=(0,),
        near=(1,),
        cuts={6: OUT},
        scratch=[
            pltpu.VMEM((NK, ROWS, QUARTER // NK), bf16),
            pltpu.VMEM((ROWS, NY * COLS), bf16),
        ],
    )
    kept, given = out_parts[NX:]
    other = lax.ppermute(given, "k", [(0, 1), (1, 0)])
    both = [(kept[i].astype(f32) + other[i].astype(f32)) for i in range(NY)]
    grad_out_weight = both[0]
    for i in range(1, NY):
        grad_out_weight = grad_out_weight + shifted(both[i].astype(bf16), "y", NY, i).astype(f32)
    enc_sum = out_parts[0].astype(f32)
    for j in range(1, NX):
        enc_sum = enc_sum + shifted(out_parts[j], "x", NX, j).astype(f32)
    encoded = swap_xy((frames.astype(f32) + enc_sum).astype(bf16))

    input_grad, gain_term = call(
        input_kernel,
        [shape((ROWS, COLS), bf16), shape((8, COLS), f32)],
        (norm_moved, frames, grad_out, stat, local_gain),
        near=(0,),
    )
    input_grad = swap_xy(input_grad)

    small = jnp.concatenate([small, gain_term], axis=0)
    small = small + lax.ppermute(small, "k", [(0, 1), (1, 0)])
    arrived = []
    for shift in range(NX):
        route = [
            (a * NY + b, ((b + shift) % NX) * NY + a) for a in range(NX) for b in range(NY)
        ]
        arrived.append(lax.ppermute(small, ("x", "y"), route))
    small, input_grad = lax.optimization_barrier((sum(arrived), input_grad))
    return (
        encoded,
        input_grad,
        in_weight[:, :COLS],
        in_weight[:, COLS:],
        small[:K],
        small[K],
        grad_out_weight,
        small[K + 1],
    )


def solution(mesh):
    fine = Mesh(mesh.devices.reshape(NX, NK, NY, NZ), ("x", "k", "y", "z"))
    both = P(ROW, COL)
    return jax.shard_map(
        shards,
        mesh=fine,
        in_specs=(both, P(), both, both, P(None, COL), P(COL), both, both),
        out_specs=(both, both, both, both, P(None, COL), P(COL), both, P(COL)),
        check_vma=False,
    )
```

```python
import jax
import jax.numpy as jnp
from jax import lax
from jax.experimental import pallas as pl
from jax.experimental.pallas import tpu as pltpu
from jax.sharding import Mesh, PartitionSpec as P

K = 31
LEN = 2048
HALF = K // 2
NX, NK, NY, NZ = 4, 2, 4, 8
ROW = ("x", "k")
COL = ("y", "z")
TIME = ("y", "k")
ROWS = 384
COLS = 128
QUARTER = COLS * NZ
WIDTH = QUARTER * NX
EDGE = 32
GATHER_ROWS = 512
IN = (0, 2 * COLS)
OUT = (2 * COLS, COLS)

epsilon = 1e-05
f32 = jnp.float32
bf16 = jnp.bfloat16


def dot(left, right, left_dim, right_dim):
    return lax.dot_general(
        left, right, (((left_dim,), (right_dim,)), ((), ())), preferred_element_type=f32
    )


def split3(value):
    high = value.astype(bf16)
    rest = value - high.astype(f32)
    middle = rest.astype(bf16)
    low = (rest - middle.astype(f32)).astype(bf16)
    return high, middle, low


def one_hot():
    lane = lax.broadcasted_iota(jnp.int32, (16, 128), 1)
    row = lax.broadcasted_iota(jnp.int32, (16, 128), 0)
    return jnp.where(lane == row, 1.0, 0.0).astype(bf16)


def columns_to_rows(first, second):
    lane = lax.broadcasted_iota(jnp.int32, (first.shape[0], 128), 1)
    grid = jnp.zeros((first.shape[0], 128), f32)
    for j, piece in enumerate(split3(first) + split3(second)):
        grid = jnp.where(lane == j, piece.astype(f32), grid)
    return dot(one_hot(), grid.astype(bf16), 1, 1)


def rows_to_columns(rows):
    grid = dot(rows, one_hot(), 0, 0)
    first = grid[:, 0:1] + grid[:, 1:2] + grid[:, 2:3]
    second = grid[:, 3:4] + grid[:, 4:5] + grid[:, 5:6]
    return first, second


def stacked_rows(values):
    row = lax.broadcasted_iota(jnp.int32, (16, values[0].shape[1]), 0)
    out = jnp.zeros((16, values[0].shape[1]), f32)
    for j, value in enumerate(values):
        out = jnp.where(row == j, value.astype(f32), out)
    return out


def call(body, out_shape, args, smem=(), near=(), late=(), scratch=(), cuts=()):
    cuts = dict(cuts)
    single = not isinstance(out_shape, (list, tuple))
    outs = [out_shape] if single else list(out_shape)
    count = len(args)
    moved = [i for i in range(count) if i not in smem and i not in near]
    buffers = []
    for i in moved:
        dims = args[i].shape
        if i in cuts:
            dims = (dims[0], cuts[i][1])
        buffers.append(pltpu.VMEM(dims, args[i].dtype))
    for out in outs:
        buffers.append(pltpu.VMEM(out.shape, out.dtype))

    def whole(*refs):
        refs = list(refs)
        inputs, refs = refs[:count], refs[count:]
        results, refs = refs[: len(outs)], refs[len(outs) :]
        held, refs = refs[: len(buffers)], refs[len(buffers) :]
        sems, extra = refs[0], refs[1:]
        copies = {}
        for place, i in enumerate(moved):
            source = inputs[i]
            if i in cuts:
                source = source.at[:, pl.ds(cuts[i][0], cuts[i][1])]
            copies[i] = pltpu.make_async_copy(source, held[place], sems.at[place])
            inputs[i] = held[place]
        for copy in copies.values():
            copy.start()
        for i, copy in copies.items():
            if i not in late:
                copy.wait()
        sent = []

        def send(j, part=None):
            source, target = held[len(moved) + j], results[j]
            if part is not None:
                source, target = source.at[part], target.at[part]
            copy = pltpu.make_async_copy(source, target, sems.at[len(moved) + len(sent)])
            copy.start()
            sent.append((j, copy))

        hooks = (lambda i: copies[i].wait(), send) if late else ()
        body(*hooks, *inputs, *held[len(moved) :], *extra)
        already = {j for j, _ in sent}
        for j in range(len(outs)):
            if j not in already:
                send(j)
        for _, copy in sent:
            copy.wait()

    hbm = pl.BlockSpec(memory_space=pltpu.MemorySpace.HBM)
    spaces = [
        pltpu.MemorySpace.SMEM
        if i in smem
        else (pltpu.MemorySpace.VMEM if i in near else pltpu.MemorySpace.HBM)
        for i in range(count)
    ]
    made = pl.pallas_call(
        whole,
        out_shape=[pltpu.HBM(out.shape, out.dtype) for out in outs],
        in_specs=[pl.BlockSpec(memory_space=space) for space in spaces],
        out_specs=[hbm] * len(outs),
        scratch_shapes=buffers + [pltpu.SemaphoreType.DMA((len(moved) + max(len(outs), NZ),))] + list(scratch),
        compiler_params=pltpu.CompilerParams(vmem_limit_bytes=24 * 1024 * 1024),
        name=body.__name__,
    )(
        *[
            pltpu.with_memory_space_constraint(arg, pltpu.HBM) if i in moved else arg
            for i, arg in enumerate(args)
        ]
    )
    return made[0] if single else made


def shape(dims, kind):
    return jax.ShapeDtypeStruct(dims, kind)


def project_kernel(arrive, send, place_ref, frames_ref, gain_ref, gain_rows_ref, weight_ref, *refs):
    left_ref = refs[NX]
    total = jnp.zeros((ROWS, 1), f32)
    square = jnp.zeros((ROWS, 1), f32)
    for i in range(NZ):
        wide = frames_ref[i].astype(f32)
        total = total + jnp.sum(wide, axis=1, keepdims=True)
        square = square + jnp.sum(wide * wide, axis=1, keepdims=True)
    mean = total / QUARTER
    for i in range(NZ):
        cut = pl.ds(i * COLS, COLS)
        scaled = (frames_ref[i].astype(f32) - mean) * gain_ref[0:1, cut]
        left_ref[:, cut] = scaled.astype(bf16)
    sums = columns_to_rows(total, square).astype(bf16)
    arrive(4)
    for j, out_ref in enumerate(refs[:NX]):
        start = pl.multiple_of(place_ref[4 + j] * QUARTER, QUARTER)
        weight = weight_ref[pl.ds(start, QUARTER), :]
        out_ref[0:ROWS, :] = dot(left_ref[...], weight, 1, 0).astype(bf16)
        unit = jnp.sum(dot(gain_rows_ref[...], weight, 1, 0), axis=0, keepdims=True)
        out_ref[ROWS : ROWS + 16, :] = stacked_rows(split3(unit)).astype(bf16)
        out_ref[ROWS + 16 : ROWS + 32, :] = sums[:, 0:256]
        out_ref[ROWS + 32 : ROWS + 48, 0:128] = sums[:, 256:384]
        out_ref[ROWS + 32 : ROWS + 48, 128:256] = jnp.zeros((16, 128), bf16)
        send(j)


def gate_kernel(p0_ref, p1_ref, p2_ref, p3_ref, pre_ref, gated_ref, unit_ref, stat_ref):
    parts = (p0_ref, p1_ref, p2_ref, p3_ref)
    totals, squares, units = [], [], []
    for part_ref in parts:
        rows = jnp.concatenate(
            [part_ref[ROWS + 16 : ROWS + 32, :], part_ref[ROWS + 32 : ROWS + 48, 0:128]], axis=1
        )
        first, second = rows_to_columns(rows)
        totals.append(first)
        squares.append(second)
        pieces = part_ref[ROWS : ROWS + 16, :].astype(f32)
        units.append(jnp.sum(pieces, axis=0, keepdims=True))
    mean = sum(totals) / WIDTH
    inv_std = lax.rsqrt(sum(squares) / WIDTH - mean * mean + epsilon)
    pre = jnp.zeros((ROWS, 2 * COLS), f32)
    for i, part_ref in enumerate(parts):
        pre = pre + part_ref[0:ROWS, :].astype(f32)
        pre = pre + (totals[i] / QUARTER - mean) * units[i]
    pre = pre * inv_std
    pre_ref[...] = pre
    gated_ref[...] = (pre[:, 0:COLS] * jax.nn.sigmoid(pre[:, COLS:])).astype(bf16)
    unit_ref[...] = jnp.broadcast_to(sum(units), (8, 2 * COLS))
    lane = lax.broadcasted_iota(jnp.int32, (ROWS, 128), 1)
    stat_ref[...] = jnp.where(lane == 0, mean, inv_std)


def act_kernel(place_ref, g0_ref, g1_ref, g2_ref, g3_ref, weight_ref, out_ref):
    total = jnp.zeros((ROWS, QUARTER), f32)
    for j, grad_ref in enumerate((g0_ref, g1_ref, g2_ref, g3_ref)):
        start = pl.multiple_of(place_ref[j] * QUARTER, QUARTER)
        weight = weight_ref[pl.ds(start, QUARTER), :]
        total = total + dot(grad_ref[...], weight, 1, 1)
    for i in range(NZ):
        out_ref[i] = total[:, i * COLS : (i + 1) * COLS].astype(bf16)


def sum_kernel(parts_ref, out_ref):
    total = jnp.zeros((ROWS, COLS), f32)
    for i in range(NZ):
        total = total + parts_ref[i].astype(f32)
    out_ref[...] = total.astype(bf16)


CHUNKS = [(-16, 16), (0, 128), (128, 128), (256, 128), (ROWS, 16)]


def same_clip(border, start, count):
    row = lax.broadcasted_iota(jnp.int32, (count + 32, COLS), 0) + (start - 16)
    inside = (row < border).astype(jnp.int32)
    own = jnp.where(start < border, 1, 0)
    return inside == own


def conv_kernel(
    place_ref,
    gated_ref,
    act_ref,
    low_ref,
    high_ref,
    taps_ref,
    pre_ref,
    unit_ref,
    activated_ref,
    message_ref,
    small_ref,
    wide_ref,
    grad_ref,
    glu_ref,
    sums_ref,
    masked_ref,
    masked_grad_ref,
    kernel_ref,
):
    border = place_ref[0]
    total = jnp.zeros((K + 1, COLS), f32)
    for i in range(3):
        total = total + taps_ref[pl.ds(ROWS + i * (K + 1), K + 1), :].astype(f32)
    kernel_ref[...] = total
    wide_ref[0:EDGE, :] = low_ref[0:EDGE, :].astype(f32)
    wide_ref[EDGE : EDGE + ROWS, :] = gated_ref[...].astype(f32)
    wide_ref[EDGE + ROWS :, :] = high_ref[0:EDGE, :].astype(f32)
    sums_ref[...] = jnp.zeros((K + 1, 8, COLS), f32)
    bias = kernel_ref[K : K + 1, :]
    for start, count in CHUNKS:
        here = wide_ref[pl.ds(start - 16 + EDGE, count + 32), :]
        masked_ref[0 : count + 32, :] = jnp.where(same_clip(border, start, count), here, 0.0)
        conv = jnp.broadcast_to(bias, (count, COLS))
        for tap in range(K):
            conv = conv + kernel_ref[tap : tap + 1, :] * masked_ref[1 + tap : 1 + tap + count, :]
        sig = jax.nn.sigmoid(conv)
        if start < 0:
            act = low_ref[EDGE:, :]
        elif start < ROWS:
            act = act_ref[pl.ds(start, count), :]
        else:
            act = high_ref[EDGE:, :]
        grad = (act.astype(f32) * sig * (1.0 + conv * (1.0 - sig))).astype(bf16).astype(f32)
        grad_ref[pl.ds(start + 16, count), :] = grad
        if 0 <= start < ROWS:
            activated_ref[pl.ds(start, count), :] = (conv * sig).astype(bf16)
            for tap in range(K):
                product = grad * masked_ref[1 + tap : 1 + tap + count, :]
                sums_ref[tap] += jnp.sum(product.reshape(count // 8, 8, COLS), axis=0)
            sums_ref[K] += jnp.sum(grad.reshape(count // 8, 8, COLS), axis=0)
    activated_ref[ROWS:, :] = jnp.zeros((GATHER_ROWS - ROWS, COLS), bf16)
    small_ref[...] = jnp.sum(sums_ref[...], axis=1)

    for start, count in CHUNKS[1:4]:
        here = grad_ref[pl.ds(start, count + 32), :]
        masked_grad_ref[...] = jnp.where(same_clip(border, start, count), here, 0.0)
        glu = jnp.zeros((count, COLS), f32)
        for tap in range(K):
            glu = glu + kernel_ref[tap : tap + 1, :] * masked_grad_ref[31 - tap : 31 - tap + count, :]
        glu_ref[pl.ds(start, count), :] = glu

    glu = glu_ref[...]
    value_pre = pre_ref[:, 0:COLS]
    gate_pre = pre_ref[:, COLS:]
    gate_sig = jax.nn.sigmoid(gate_pre)
    value_grad = (glu * gate_sig).astype(bf16)
    gate_grad = (glu * value_pre * gate_sig * (1.0 - gate_sig)).astype(bf16)
    message_ref[0:ROWS, 0:COLS] = value_grad
    message_ref[0:ROWS, COLS:] = gate_grad
    value_wide = value_grad.astype(f32)
    gate_wide = gate_grad.astype(f32)
    first = jnp.sum(
        value_wide * unit_ref[0:1, 0:COLS] + gate_wide * unit_ref[0:1, COLS:],
        axis=1,
        keepdims=True,
    )
    second = jnp.sum(value_wide * value_pre + gate_wide * gate_pre, axis=1, keepdims=True)
    rows = columns_to_rows(first, second).astype(bf16)
    message_ref[ROWS : ROWS + 16, :] = rows[:, 0:256]
    message_ref[ROWS + 16 : ROWS + 32, 0:128] = rows[:, 256:384]
    message_ref[ROWS + 16 : ROWS + 32, 128:256] = jnp.zeros((16, 128), bf16)


def norm_kernel(arrive, send, place_ref, g0_ref, g1_ref, g2_ref, g3_ref, weight_ref, out_ref):
    rows = jnp.zeros((16, ROWS), f32)
    arrive(1)
    grads = (g0_ref, g1_ref, g2_ref, g3_ref)
    for grad_ref in grads:
        here = jnp.concatenate(
            [grad_ref[ROWS : ROWS + 16, :], grad_ref[ROWS + 16 : ROWS + 32, 0:128]], axis=1
        )
        rows = rows + here.astype(f32)
    first = rows[0:1] + rows[1:2] + rows[2:3]
    second = rows[3:4] + rows[4:5] + rows[5:6]
    sums = stacked_rows(split3(first) + split3(second)).astype(bf16)
    arrive(5)
    step = 2 * COLS
    for part in range(QUARTER // step):
        total = jnp.zeros((ROWS, step), f32)
        for j, grad_ref in enumerate(grads):
            start = pl.multiple_of(place_ref[j] * QUARTER + part * step, step)
            total = total + dot(grad_ref[0:ROWS, :], weight_ref[pl.ds(start, step), :], 1, 1)
        for i in (2 * part, 2 * part + 1):
            cut = (i - 2 * part) * COLS
            out_ref[i, 0:ROWS, :] = total[:, cut : cut + COLS].astype(bf16)
            for j in range(3):
                rows_here = sums[:, j * 128 : (j + 1) * 128]
                out_ref[i, ROWS + 16 * j : ROWS + 16 * j + 16, :] = rows_here
            send(0, i)


def weight_kernel(
    place_ref,
    frames_ref,
    gain_ref,
    stat_ref,
    g0_ref,
    g1_ref,
    g2_ref,
    g3_ref,
    kept_ref,
    given_ref,
    left_ref,
    right_ref,
):
    mean = stat_ref[:, 0:1]
    inv_std = stat_ref[:, 1:2]
    half = QUARTER // NK
    for i in range(NZ):
        cut = pl.ds(i * COLS, COLS)
        scaled = (frames_ref[i].astype(f32) - mean) * inv_std * gain_ref[0:1, cut]
        left_ref[i * COLS // half, :, pl.ds(i * COLS % half, COLS)] = scaled.astype(bf16)
    order_blocks(place_ref, 10, (g0_ref, g1_ref, g2_ref, g3_ref), right_ref, 2 * COLS)
    core = place_ref[9]
    for out_ref, which in ((given_ref, 1 - core), (kept_ref, core)):
        out = dot(left_ref[which], right_ref[...], 0, 0).astype(bf16)
        for i in range(NY):
            out_ref[i] = out[:, i * 2 * COLS : (i + 1) * 2 * COLS]


def order_blocks(place_ref, base, sources, out_ref, lanes):
    for i in range(NY):
        source = place_ref[base + i]
        for j, block_ref in enumerate(sources):

            @pl.when(source == j)
            def _(block_ref=block_ref, i=i):
                out_ref[:, i * lanes : (i + 1) * lanes] = block_ref[0:ROWS, :]


def out_kernel(place_ref, act_ref, g0_ref, g1_ref, g2_ref, g3_ref, weight_ref, *refs):
    enc_refs = refs[:NX]
    kept_ref, given_ref, left_ref, grad_ref = refs[NX:]
    half = QUARTER // NK
    for i in range(NZ):
        left_ref[i * COLS // half, :, pl.ds(i * COLS % half, COLS)] = act_ref[i, 0:ROWS, :]
    for j, enc_ref in enumerate(enc_refs):
        total = jnp.zeros((ROWS, COLS), f32)
        for h in range(NK):
            start = pl.multiple_of(place_ref[4 + j] * QUARTER + h * half, half)
            weight = weight_ref[pl.ds(start, half), :]
            total = total + dot(left_ref[h], weight, 1, 0)
        enc_ref[...] = total.astype(bf16)
    order_blocks(place_ref, 0, (g0_ref, g1_ref, g2_ref, g3_ref), grad_ref, COLS)
    core = place_ref[9]
    for out_ref, which in ((given_ref, 1 - core), (kept_ref, core)):
        out = dot(left_ref[which], grad_ref[...], 0, 0).astype(bf16)
        for i in range(NY):
            out_ref[i] = out[:, i * COLS : (i + 1) * COLS]


def input_kernel(parts_ref, frames_ref, grad_ref, stat_ref, gain_ref, out_ref, small_ref):
    normed_grad = jnp.zeros((ROWS, COLS), f32)
    rows = jnp.zeros((16, ROWS), f32)
    for i in range(NZ):
        normed_grad = normed_grad + parts_ref[i, 0:ROWS, :].astype(f32)
        here = [parts_ref[i, ROWS + 16 * j : ROWS + 16 * j + 16, :] for j in range(3)]
        rows = rows + jnp.concatenate(here, axis=1).astype(f32)
    first = rows[0:1] + rows[1:2] + rows[2:3]
    second = rows[3:4] + rows[4:5] + rows[5:6]
    sums = stacked_rows(split3(first) + split3(second)).astype(bf16)
    first, second = rows_to_columns(sums)
    mean = stat_ref[:, 0:1]
    inv_std = stat_ref[:, 1:2]
    centred = (frames_ref[...].astype(f32) - mean) * inv_std
    hat = normed_grad * gain_ref[0:1, :]
    out = grad_ref[...].astype(f32) + inv_std * (hat - first / WIDTH - centred * (second / WIDTH))
    out_ref[...] = out.astype(bf16)
    gain_term = jnp.sum(normed_grad * centred, axis=0, keepdims=True)
    small_ref[...] = jnp.broadcast_to(gain_term, (8, COLS))


def swap_xy(block):
    return lax.ppermute(
        block, ("x", "y"), [(a * NY + b, b * NY + a) for a in range(NX) for b in range(NY)]
    )


def neighbours(upper, lower):
    place = [k * NY + y for y in range(NY) for k in range(NK)]
    forward = list(zip(place[:-1], place[1:]))
    backward = [(target, source) for source, target in forward]
    low = lax.ppermute(upper, ("k", "y"), forward)
    high = lax.ppermute(lower, ("k", "y"), backward)
    return low, high


def exchange(parts, axis):
    return lax.all_to_all(parts, axis, 0, 0, tiled=True)


def gathered(block, axis, count):
    return exchange(jnp.broadcast_to(block[None], (count,) + block.shape), axis)


def shifted(block, axis, count, shift):
    return lax.ppermute(block, axis, [(i, (i + shift) % count) for i in range(count)])


def spread(block, axis, count):
    return [block] + [shifted(block, axis, count, j) for j in range(1, count)]


def reduced(kept, given):
    other = lax.ppermute(given, "k", [(0, 1), (1, 0)])
    both = [(kept[i].astype(f32) + other[i].astype(f32)) for i in range(NY)]
    total = both[0]
    for i in range(1, NY):
        total = total + shifted(both[i].astype(bf16), "y", NY, i).astype(f32)
    return total


def pieces(value):
    out = []
    for _ in range(3):
        piece = lax.reduce_precision(value, 8, 7)
        out.append(piece.astype(bf16))
        value = value - piece
    return jnp.stack(out)


def after(value, *others):
    return lax.optimization_barrier((value,) + others)[0]


def shards(frames, gain, w_value, w_gate, kernel, bias, w_out, grad_out):
    x_index = lax.axis_index("x")
    k_index = lax.axis_index("k")
    row_start = (lax.axis_index("y") * NK + k_index) * ROWS
    col_start = (x_index * NZ + lax.axis_index("z")) * COLS
    local_gain = lax.dynamic_slice_in_dim(gain, col_start, COLS, 0)[None]
    quarter_gain = lax.dynamic_slice_in_dim(gain, x_index * QUARTER, QUARTER, 0)[None]
    gain_rows = jnp.pad(pieces(quarter_gain)[:, 0], ((0, 13), (0, 0)))
    y_index = lax.axis_index("y")
    steps = jnp.arange(NX, dtype=jnp.int32)
    below = (x_index + NX - steps) % NX
    above = (x_index + steps) % NX
    distance = (x_index + 2 * NX - (y_index + steps) % NY) % NX
    edges = jnp.stack([LEN - row_start, k_index]).astype(jnp.int32)
    place = jnp.concatenate([below, above, edges, distance]).astype(jnp.int32)
    border = place[8:9]

    weights = lax.all_gather(
        jnp.concatenate([w_value, w_gate, w_out], axis=1), TIME, axis=0, tiled=True
    )

    frames = swap_xy(frames)
    frames_z = gathered(frames, "z", NZ)
    taps = jnp.concatenate([kernel, bias[None, :]], axis=0)
    packed = jnp.concatenate([grad_out, pieces(taps).reshape(3 * (K + 1), COLS)], axis=0)
    packed = swap_xy(packed)
    grad_out = packed[:ROWS]
    grads = spread(grad_out, "x", NX)

    act_parts = call(
        act_kernel, shape((NZ, ROWS, COLS), bf16), (place, *grads, weights), smem=(0,), near=(1, 2, 3, 4), cuts={5: OUT}
    )
    act_moved = exchange(act_parts, "z")
    pre_parts = call(
        project_kernel,
        [shape((ROWS + 48, 2 * COLS), bf16) for _ in range(NX)],
        (place, after(frames_z, act_parts), quarter_gain, gain_rows, weights),
        smem=(0,),
        near=(1,),
        late=(4,),
        cuts={4: IN},
        scratch=[pltpu.VMEM((ROWS, QUARTER), bf16)],
    )
    pre_moved = [pre_parts[0]] + [shifted(pre_parts[j], "x", NX, j) for j in range(1, NX)]
    pre, gated, unit, stat = call(
        gate_kernel,
        [
            shape((ROWS, 2 * COLS), f32),
            shape((ROWS, COLS), bf16),
            shape((8, 2 * COLS), f32),
            shape((ROWS, 128), f32),
        ],
        tuple(pre_moved),
        near=(1, 2, 3),
    )
    act_grad = call(sum_kernel, shape((ROWS, COLS), bf16), (act_moved,), near=(0,))
    low, high = neighbours(
        jnp.concatenate([gated[-EDGE:], act_grad[-16:]], axis=0),
        jnp.concatenate([gated[:EDGE], act_grad[:16]], axis=0),
    )
    activated, message, small = call(
        conv_kernel,
        [
            shape((GATHER_ROWS, COLS), bf16),
            shape((ROWS + 32, 2 * COLS), bf16),
            shape((K + 1, COLS), f32),
        ],
        (border, gated, act_grad, low, high, packed, pre, unit),
        smem=(0,),
        near=(3, 4),
        scratch=[
            pltpu.VMEM((ROWS + 2 * EDGE, COLS), f32),
            pltpu.VMEM((ROWS + 32, COLS), f32),
            pltpu.VMEM((ROWS, COLS), f32),
            pltpu.VMEM((K + 1, 8, COLS), f32),
            pltpu.VMEM((160, COLS), f32),
            pltpu.VMEM((160, COLS), f32),
            pltpu.VMEM((K + 1, COLS), f32),
        ],
    )
    act_z = lax.all_gather(activated, "z", axis=0, tiled=False)

    vg_grads = spread(message, "x", NX)
    norm_parts = call(
        norm_kernel,
        shape((NZ, ROWS + 48, COLS), bf16),
        (place, *vg_grads, weights),
        smem=(0,),
        near=(2, 3, 4),
        late=(1, 5),
        cuts={5: IN},
    )
    norm_moved = exchange(norm_parts, "z")
    held = lax.optimization_barrier((vg_grads, norm_parts))[0]
    kept, given = call(
        weight_kernel,
        [shape((NY, QUARTER // NK, 2 * COLS), bf16) for _ in range(2)],
        (place, frames_z, quarter_gain, stat, *held),
        smem=(0,),
        near=(5, 6, 7),
        scratch=[
            pltpu.VMEM((NK, ROWS, QUARTER // NK), bf16),
            pltpu.VMEM((ROWS, NY * 2 * COLS), bf16),
        ],
    )
    in_weight = reduced(kept, given)

    out_parts = call(
        out_kernel,
        [shape((ROWS, COLS), bf16) for _ in range(NX)]
        + [shape((NY, QUARTER // NK, COLS), bf16) for _ in range(2)],
        (place, act_z, *after(grads, norm_parts), weights),
        smem=(0,),
        cuts={6: OUT},
        scratch=[
            pltpu.VMEM((NK, ROWS, QUARTER // NK), bf16),
            pltpu.VMEM((ROWS, NY * COLS), bf16),
        ],
    )
    kept, given = out_parts[NX:]
    other = lax.ppermute(given, "k", [(0, 1), (1, 0)])
    both = (kept.astype(f32) + other.astype(f32)).astype(bf16)
    grad_out_weight = lax.psum_scatter(
        both.reshape(NY * QUARTER // NK, COLS), "y", scatter_dimension=0, tiled=True
    ).astype(f32)
    enc_sum = out_parts[0].astype(f32)
    for j in range(1, NX):
        enc_sum = enc_sum + shifted(out_parts[j], "x", NX, j).astype(f32)
    encoded = swap_xy((frames.astype(f32) + enc_sum).astype(bf16))

    input_grad, gain_term = call(
        input_kernel,
        [shape((ROWS, COLS), bf16), shape((8, COLS), f32)],
        (after(norm_moved, *out_parts), frames, grad_out, stat, local_gain),
        near=(0,),
    )
    input_grad = swap_xy(input_grad)

    small = jnp.concatenate([small, gain_term], axis=0)
    small = small + lax.ppermute(small, "k", [(0, 1), (1, 0)])
    arrived = []
    for shift in range(NX):
        route = [
            (a * NY + b, ((b + shift) % NX) * NY + a) for a in range(NX) for b in range(NY)
        ]
        arrived.append(lax.ppermute(small, ("x", "y"), route))
    small, input_grad = lax.optimization_barrier((sum(arrived), input_grad))
    return (
        encoded,
        input_grad,
        in_weight[:, :COLS],
        in_weight[:, COLS:],
        small[:K],
        small[K],
        grad_out_weight,
        small[K + 1],
    )


def solution(mesh):
    fine = Mesh(mesh.devices.reshape(NX, NK, NY, NZ), ("x", "k", "y", "z"))
    both = P(ROW, COL)
    return jax.shard_map(
        shards,
        mesh=fine,
        in_specs=(both, P(), both, both, P(None, COL), P(COL), both, both),
        out_specs=(both, both, both, both, P(None, COL), P(COL), both, P(COL)),
        check_vma=False,
    )
```

```python
import jax
import jax.numpy as jnp
from jax import lax
from jax.experimental import pallas as pl
from jax.experimental.pallas import tpu as pltpu
from jax.sharding import Mesh, PartitionSpec as P

K = 31
LEN = 2048
HALF = K // 2
NX, NK, NY, NZ = 4, 2, 4, 8
ROW = ("x", "k")
COL = ("y", "z")
TIME = ("y", "k")
ROWS = 384
COLS = 128
QUARTER = COLS * NZ
WIDTH = QUARTER * NX
EDGE = 32
IN = (0, 2 * COLS)
OUT = (2 * COLS, COLS)

epsilon = 1e-05
f32 = jnp.float32
bf16 = jnp.bfloat16


def dot(left, right, left_dim, right_dim):
    return lax.dot_general(
        left, right, (((left_dim,), (right_dim,)), ((), ())), preferred_element_type=f32
    )


def split3(value):
    high = value.astype(bf16)
    rest = value - high.astype(f32)
    middle = rest.astype(bf16)
    low = (rest - middle.astype(f32)).astype(bf16)
    return high, middle, low


def one_hot():
    lane = lax.broadcasted_iota(jnp.int32, (16, 128), 1)
    row = lax.broadcasted_iota(jnp.int32, (16, 128), 0)
    return jnp.where(lane == row, 1.0, 0.0).astype(bf16)


def columns_to_rows(first, second):
    lane = lax.broadcasted_iota(jnp.int32, (first.shape[0], 128), 1)
    grid = jnp.zeros((first.shape[0], 128), f32)
    for j, piece in enumerate(split3(first) + split3(second)):
        grid = jnp.where(lane == j, piece.astype(f32), grid)
    return dot(one_hot(), grid.astype(bf16), 1, 1)


def rows_to_columns(rows):
    grid = dot(rows, one_hot(), 0, 0)
    first = grid[:, 0:1] + grid[:, 1:2] + grid[:, 2:3]
    second = grid[:, 3:4] + grid[:, 4:5] + grid[:, 5:6]
    return first, second


def stacked_rows(values):
    row = lax.broadcasted_iota(jnp.int32, (16, values[0].shape[1]), 0)
    out = jnp.zeros((16, values[0].shape[1]), f32)
    for j, value in enumerate(values):
        out = jnp.where(row == j, value.astype(f32), out)
    return out


def call(body, out_shape, args, smem=(), near=(), late=(), scratch=(), cuts=()):
    cuts = dict(cuts)
    single = not isinstance(out_shape, (list, tuple))
    outs = [out_shape] if single else list(out_shape)
    count = len(args)
    moved = [i for i in range(count) if i not in smem and i not in near]
    buffers = []
    for i in moved:
        dims = args[i].shape
        if i in cuts:
            dims = (dims[0], cuts[i][1])
        buffers.append(pltpu.VMEM(dims, args[i].dtype))
    for out in outs:
        buffers.append(pltpu.VMEM(out.shape, out.dtype))

    def whole(*refs):
        refs = list(refs)
        inputs, refs = refs[:count], refs[count:]
        results, refs = refs[: len(outs)], refs[len(outs) :]
        held, refs = refs[: len(buffers)], refs[len(buffers) :]
        sems, extra = refs[0], refs[1:]
        copies = {}
        for place, i in enumerate(moved):
            source = inputs[i]
            if i in cuts:
                source = source.at[:, pl.ds(cuts[i][0], cuts[i][1])]
            copies[i] = pltpu.make_async_copy(source, held[place], sems.at[place])
            inputs[i] = held[place]
        for copy in copies.values():
            copy.start()
        for i, copy in copies.items():
            if i not in late:
                copy.wait()
        sent = []

        def send(j, part=None):
            source, target = held[len(moved) + j], results[j]
            if part is not None:
                source, target = source.at[part], target.at[part]
            copy = pltpu.make_async_copy(source, target, sems.at[len(moved) + len(sent)])
            copy.start()
            sent.append((j, copy))

        hooks = (lambda i: copies[i].wait(), send) if late else ()
        body(*hooks, *inputs, *held[len(moved) :], *extra)
        already = {j for j, _ in sent}
        for j in range(len(outs)):
            if j not in already:
                send(j)
        for _, copy in sent:
            copy.wait()

    hbm = pl.BlockSpec(memory_space=pltpu.MemorySpace.HBM)
    spaces = [
        pltpu.MemorySpace.SMEM
        if i in smem
        else (pltpu.MemorySpace.VMEM if i in near else pltpu.MemorySpace.HBM)
        for i in range(count)
    ]
    made = pl.pallas_call(
        whole,
        out_shape=[pltpu.HBM(out.shape, out.dtype) for out in outs],
        in_specs=[pl.BlockSpec(memory_space=space) for space in spaces],
        out_specs=[hbm] * len(outs),
        scratch_shapes=buffers + [pltpu.SemaphoreType.DMA((len(moved) + max(len(outs), NZ),))] + list(scratch),
        compiler_params=pltpu.CompilerParams(vmem_limit_bytes=24 * 1024 * 1024),
        name=body.__name__,
    )(
        *[
            pltpu.with_memory_space_constraint(arg, pltpu.HBM) if i in moved else arg
            for i, arg in enumerate(args)
        ]
    )
    return made[0] if single else made


def shape(dims, kind):
    return jax.ShapeDtypeStruct(dims, kind)


def project_kernel(arrive, send, place_ref, frames_ref, gain_ref, gain_rows_ref, weight_ref, *refs):
    left_ref = refs[NX]
    total = jnp.zeros((ROWS, 1), f32)
    square = jnp.zeros((ROWS, 1), f32)
    for i in range(NZ):
        wide = frames_ref[i].astype(f32)
        total = total + jnp.sum(wide, axis=1, keepdims=True)
        square = square + jnp.sum(wide * wide, axis=1, keepdims=True)
    mean = total / QUARTER
    arrive(2)
    arrive(3)
    for i in range(NZ):
        cut = pl.ds(i * COLS, COLS)
        scaled = (frames_ref[i].astype(f32) - mean) * gain_ref[0:1, cut]
        left_ref[:, cut] = scaled.astype(bf16)
    sums = columns_to_rows(total, square).astype(bf16)
    for j, out_ref in enumerate(refs[:NX]):
        start = pl.multiple_of(place_ref[4 + j] * QUARTER, QUARTER)
        weight = weight_ref[pl.ds(start, QUARTER), 0 : 2 * COLS]
        out_ref[0:ROWS, :] = dot(left_ref[...], weight, 1, 0).astype(bf16)
        unit = jnp.sum(dot(gain_rows_ref[...], weight, 1, 0), axis=0, keepdims=True)
        out_ref[ROWS : ROWS + 16, :] = stacked_rows(split3(unit)).astype(bf16)
        out_ref[ROWS + 16 : ROWS + 32, :] = sums[:, 0:256]
        out_ref[ROWS + 32 : ROWS + 48, 0:128] = sums[:, 256:384]
        out_ref[ROWS + 32 : ROWS + 48, 128:256] = jnp.zeros((16, 128), bf16)
        send(j)


def gate_kernel(p0_ref, p1_ref, p2_ref, p3_ref, pre_ref, gated_ref, unit_ref, stat_ref):
    parts = (p0_ref, p1_ref, p2_ref, p3_ref)
    totals, squares, units = [], [], []
    for part_ref in parts:
        rows = jnp.concatenate(
            [part_ref[ROWS + 16 : ROWS + 32, :], part_ref[ROWS + 32 : ROWS + 48, 0:128]], axis=1
        )
        first, second = rows_to_columns(rows)
        totals.append(first)
        squares.append(second)
        pieces = part_ref[ROWS : ROWS + 16, :].astype(f32)
        units.append(jnp.sum(pieces, axis=0, keepdims=True))
    mean = sum(totals) / WIDTH
    inv_std = lax.rsqrt(sum(squares) / WIDTH - mean * mean + epsilon)
    pre = jnp.zeros((ROWS, 2 * COLS), f32)
    for i, part_ref in enumerate(parts):
        pre = pre + part_ref[0:ROWS, :].astype(f32)
        pre = pre + (totals[i] / QUARTER - mean) * units[i]
    pre = pre * inv_std
    pre_ref[...] = pre
    gated_ref[...] = (pre[:, 0:COLS] * jax.nn.sigmoid(pre[:, COLS:])).astype(bf16)
    unit_ref[...] = jnp.broadcast_to(sum(units), (8, 2 * COLS))
    lane = lax.broadcasted_iota(jnp.int32, (ROWS, 128), 1)
    stat_ref[...] = jnp.where(lane == 0, mean, inv_std)


def act_kernel(place_ref, g0_ref, g1_ref, g2_ref, g3_ref, weight_ref, out_ref):
    total = jnp.zeros((ROWS, QUARTER), f32)
    for j, grad_ref in enumerate((g0_ref, g1_ref, g2_ref, g3_ref)):
        start = pl.multiple_of(place_ref[j] * QUARTER, QUARTER)
        weight = weight_ref[pl.ds(start, QUARTER), 2 * COLS : 3 * COLS]
        total = total + dot(grad_ref[...], weight, 1, 1)
    for i in range(NZ):
        out_ref[i] = total[:, i * COLS : (i + 1) * COLS].astype(bf16)


def sum_kernel(parts_ref, out_ref):
    total = jnp.zeros((ROWS, COLS), f32)
    for i in range(NZ):
        total = total + parts_ref[i].astype(f32)
    out_ref[...] = total.astype(bf16)


CHUNKS = [(-16, 16), (0, 128), (128, 128), (256, 128), (ROWS, 16)]


def same_clip(border, start, count):
    row = lax.broadcasted_iota(jnp.int32, (count + 32, COLS), 0) + (start - 16)
    inside = (row < border).astype(jnp.int32)
    own = jnp.where(start < border, 1, 0)
    return inside == own


def fill_wide(wide_ref, gated_ref, low_ref, high_ref):
    wide_ref[0:EDGE, :] = low_ref[...].astype(f32)
    wide_ref[EDGE : EDGE + ROWS, :] = gated_ref[...].astype(f32)
    wide_ref[EDGE + ROWS :, :] = high_ref[...].astype(f32)


def forward_kernel(
    place_ref,
    gated_ref,
    low_ref,
    high_ref,
    taps_ref,
    activated_ref,
    slope_ref,
    kernel_ref,
    wide_ref,
    masked_ref,
):
    border = place_ref[0]
    total = jnp.zeros((K + 1, COLS), f32)
    for i in range(3):
        total = total + taps_ref[pl.ds(ROWS + i * (K + 1), K + 1), :].astype(f32)
    kernel_ref[...] = total
    fill_wide(wide_ref, gated_ref, low_ref, high_ref)
    bias = kernel_ref[K : K + 1, :]
    for start, count in CHUNKS:
        here = wide_ref[pl.ds(start - 16 + EDGE, count + 32), :]
        masked_ref[0 : count + 32, :] = jnp.where(same_clip(border, start, count), here, 0.0)
        conv = jnp.broadcast_to(bias, (count, COLS))
        for tap in range(K):
            conv = conv + kernel_ref[tap : tap + 1, :] * masked_ref[1 + tap : 1 + tap + count, :]
        sig = jax.nn.sigmoid(conv)
        slope_ref[pl.ds(start + 16, count), :] = sig * (1.0 + conv * (1.0 - sig))
        if 0 <= start < ROWS:
            activated = (conv * sig).astype(bf16)
            for i in range(NZ):
                activated_ref[i, pl.ds(start, count), :] = activated


def backward_kernel(
    place_ref,
    gated_ref,
    low_ref,
    high_ref,
    act_ref,
    act_low_ref,
    act_high_ref,
    slope_ref,
    taps_ref,
    pre_ref,
    unit_ref,
    message_ref,
    small_ref,
    wide_ref,
    grad_ref,
    glu_ref,
    sums_ref,
    masked_ref,
    masked_grad_ref,
):
    border = place_ref[0]
    fill_wide(wide_ref, gated_ref, low_ref, high_ref)
    sums_ref[...] = jnp.zeros((K + 1, 8, COLS), f32)
    for start, count in CHUNKS:
        if start < 0:
            act = act_low_ref[...]
        elif start < ROWS:
            act = act_ref[pl.ds(start, count), :]
        else:
            act = act_high_ref[...]
        grad = act.astype(f32) * slope_ref[pl.ds(start + 16, count), :]
        grad = grad.astype(bf16).astype(f32)
        grad_ref[pl.ds(start + 16, count), :] = grad
        if 0 <= start < ROWS:
            here = wide_ref[pl.ds(start - 16 + EDGE, count + 32), :]
            masked_ref[...] = jnp.where(same_clip(border, start, count), here, 0.0)
            for tap in range(K):
                product = grad * masked_ref[1 + tap : 1 + tap + count, :]
                sums_ref[tap] += jnp.sum(product.reshape(count // 8, 8, COLS), axis=0)
            sums_ref[K] += jnp.sum(grad.reshape(count // 8, 8, COLS), axis=0)
    small_ref[...] = jnp.sum(sums_ref[...], axis=1)

    for start, count in CHUNKS[1:4]:
        here = grad_ref[pl.ds(start, count + 32), :]
        masked_grad_ref[...] = jnp.where(same_clip(border, start, count), here, 0.0)
        glu = jnp.zeros((count, COLS), f32)
        for tap in range(K):
            glu = glu + taps_ref[tap : tap + 1, :] * masked_grad_ref[31 - tap : 31 - tap + count, :]
        glu_ref[pl.ds(start, count), :] = glu

    glu = glu_ref[...]
    value_pre = pre_ref[:, 0:COLS]
    gate_pre = pre_ref[:, COLS:]
    gate_sig = jax.nn.sigmoid(gate_pre)
    value_grad = (glu * gate_sig).astype(bf16)
    gate_grad = (glu * value_pre * gate_sig * (1.0 - gate_sig)).astype(bf16)
    message_ref[0:ROWS, 0:COLS] = value_grad
    message_ref[0:ROWS, COLS:] = gate_grad
    value_wide = value_grad.astype(f32)
    gate_wide = gate_grad.astype(f32)
    first = jnp.sum(
        value_wide * unit_ref[0:1, 0:COLS] + gate_wide * unit_ref[0:1, COLS:],
        axis=1,
        keepdims=True,
    )
    second = jnp.sum(value_wide * value_pre + gate_wide * gate_pre, axis=1, keepdims=True)
    rows = columns_to_rows(first, second).astype(bf16)
    message_ref[ROWS : ROWS + 16, :] = rows[:, 0:256]
    message_ref[ROWS + 16 : ROWS + 32, 0:128] = rows[:, 256:384]
    message_ref[ROWS + 16 : ROWS + 32, 128:256] = jnp.zeros((16, 128), bf16)


def norm_kernel(arrive, send, place_ref, g0_ref, g1_ref, g2_ref, g3_ref, weight_ref, out_ref):
    rows = jnp.zeros((16, ROWS), f32)
    arrive(1)
    grads = (g0_ref, g1_ref, g2_ref, g3_ref)
    for grad_ref in grads:
        here = jnp.concatenate(
            [grad_ref[ROWS : ROWS + 16, :], grad_ref[ROWS + 16 : ROWS + 32, 0:128]], axis=1
        )
        rows = rows + here.astype(f32)
    first = rows[0:1] + rows[1:2] + rows[2:3]
    second = rows[3:4] + rows[4:5] + rows[5:6]
    sums = stacked_rows(split3(first) + split3(second)).astype(bf16)
    step = 2 * COLS
    for part in range(QUARTER // step):
        total = jnp.zeros((ROWS, step), f32)
        for j, grad_ref in enumerate(grads):
            start = pl.multiple_of(place_ref[j] * QUARTER + part * step, step)
            weight = weight_ref[pl.ds(start, step), 0 : 2 * COLS]
            total = total + dot(grad_ref[0:ROWS, :], weight, 1, 1)
        for i in (2 * part, 2 * part + 1):
            cut = (i - 2 * part) * COLS
            out_ref[i, 0:ROWS, :] = total[:, cut : cut + COLS].astype(bf16)
            for j in range(3):
                rows_here = sums[:, j * 128 : (j + 1) * 128]
                out_ref[i, ROWS + 16 * j : ROWS + 16 * j + 16, :] = rows_here
            send(0, i)


def weight_kernel(
    place_ref,
    frames_ref,
    gain_ref,
    stat_ref,
    g0_ref,
    g1_ref,
    g2_ref,
    g3_ref,
    out_ref,
    left_ref,
):
    mean = stat_ref[:, 0:1]
    inv_std = stat_ref[:, 1:2]
    for i in range(NZ):
        cut = pl.ds(i * COLS, COLS)
        scaled = (frames_ref[i].astype(f32) - mean) * inv_std * gain_ref[0:1, cut]
        left_ref[:, cut] = scaled.astype(bf16)
    for j, grad_ref in enumerate((g0_ref, g1_ref, g2_ref, g3_ref)):
        start = pl.multiple_of(place_ref[j] * QUARTER, QUARTER)
        out = dot(left_ref[...], grad_ref[0:ROWS, :], 0, 0)
        out_ref[pl.ds(start, QUARTER), :] = out.astype(bf16)


def order_blocks(place_ref, base, sources, out_ref, lanes):
    for i in range(NY):
        source = place_ref[base + i]
        for j, block_ref in enumerate(sources):

            @pl.when(source == j)
            def _(block_ref=block_ref, i=i):
                out_ref[:, i * lanes : (i + 1) * lanes] = block_ref[0:ROWS, :]


def out_kernel(place_ref, act_ref, g0_ref, g1_ref, g2_ref, g3_ref, weight_ref, *refs):
    enc_refs = refs[:NX]
    kept_ref, given_ref, left_ref, grad_ref = refs[NX:]
    half = QUARTER // NK
    for i in range(NZ):
        left_ref[i * COLS // half, :, pl.ds(i * COLS % half, COLS)] = act_ref[i, 0:ROWS, :]
    for j, enc_ref in enumerate(enc_refs):
        total = jnp.zeros((ROWS, COLS), f32)
        for h in range(NK):
            start = pl.multiple_of(place_ref[4 + j] * QUARTER + h * half, half)
            weight = weight_ref[pl.ds(start, half), 2 * COLS : 3 * COLS]
            total = total + dot(left_ref[h], weight, 1, 0)
        enc_ref[...] = total.astype(bf16)
    order_blocks(place_ref, 10, (g0_ref, g1_ref, g2_ref, g3_ref), grad_ref, COLS)
    core = place_ref[9]
    for out_ref, which in ((given_ref, 1 - core), (kept_ref, core)):
        out = dot(left_ref[which], grad_ref[...], 0, 0).astype(bf16)
        for i in range(NY):
            out_ref[i] = out[:, i * COLS : (i + 1) * COLS]


def input_kernel(
    parts_ref,
    frames_ref,
    grad_ref,
    stat_ref,
    gain_ref,
    e0_ref,
    e1_ref,
    e2_ref,
    e3_ref,
    out_ref,
    small_ref,
):
    normed_grad = jnp.zeros((ROWS, COLS), f32)
    rows = jnp.zeros((16, ROWS), f32)
    for i in range(NZ):
        normed_grad = normed_grad + parts_ref[i, 0:ROWS, :].astype(f32)
        here = [parts_ref[i, ROWS + 16 * j : ROWS + 16 * j + 16, :] for j in range(3)]
        rows = rows + jnp.concatenate(here, axis=1).astype(f32)
    first = rows[0:1] + rows[1:2] + rows[2:3]
    second = rows[3:4] + rows[4:5] + rows[5:6]
    sums = stacked_rows(split3(first) + split3(second)).astype(bf16)
    first, second = rows_to_columns(sums)
    mean = stat_ref[:, 0:1]
    inv_std = stat_ref[:, 1:2]
    centred = (frames_ref[...].astype(f32) - mean) * inv_std
    hat = normed_grad * gain_ref[0:1, :]
    out = grad_ref[...].astype(f32) + inv_std * (hat - first / WIDTH - centred * (second / WIDTH))
    out_ref[:, COLS:] = out.astype(bf16)
    encoded = frames_ref[...].astype(f32)
    for part_ref in (e0_ref, e1_ref, e2_ref, e3_ref):
        encoded = encoded + part_ref[...].astype(f32)
    out_ref[:, 0:COLS] = encoded.astype(bf16)
    gain_term = jnp.sum(normed_grad * centred, axis=0, keepdims=True)
    small_ref[...] = jnp.broadcast_to(gain_term, (8, COLS))


def swap_xy(block):
    return lax.ppermute(
        block, ("x", "y"), [(a * NY + b, b * NY + a) for a in range(NX) for b in range(NY)]
    )


def neighbours(upper, lower):
    place = [k * NY + y for y in range(NY) for k in range(NK)]
    forward = list(zip(place[:-1], place[1:]))
    backward = [(target, source) for source, target in forward]
    low = lax.ppermute(upper, ("k", "y"), forward)
    high = lax.ppermute(lower, ("k", "y"), backward)
    return low, high


def exchange(parts, axis):
    return lax.all_to_all(parts, axis, 0, 0, tiled=True)


def gathered(block, axis, count):
    return exchange(jnp.broadcast_to(block[None], (count,) + block.shape), axis)


def shifted(block, axis, count, shift):
    return lax.ppermute(block, axis, [(i, (i + shift) % count) for i in range(count)])


def spread(block, axis, count):
    return [block] + [shifted(block, axis, count, j) for j in range(1, count)]


def reduced(kept, given):
    other = lax.ppermute(given, "k", [(0, 1), (1, 0)])
    both = [(kept[i].astype(f32) + other[i].astype(f32)) for i in range(NY)]
    total = both[0]
    for i in range(1, NY):
        total = total + shifted(both[i].astype(bf16), "y", NY, i).astype(f32)
    return total


def pieces(value):
    out = []
    for _ in range(3):
        piece = lax.reduce_precision(value, 8, 7)
        out.append(piece.astype(bf16))
        value = value - piece
    return jnp.stack(out)


def after(value, *others):
    return lax.optimization_barrier((value,) + others)[0]


def shards(frames, gain, w_value, w_gate, kernel, bias, w_out, grad_out):
    x_index = lax.axis_index("x")
    k_index = lax.axis_index("k")
    row_start = (lax.axis_index("y") * NK + k_index) * ROWS
    col_start = (x_index * NZ + lax.axis_index("z")) * COLS
    local_gain = lax.dynamic_slice_in_dim(gain, col_start, COLS, 0)[None]
    quarter_gain = lax.dynamic_slice_in_dim(gain, x_index * QUARTER, QUARTER, 0)[None]
    gain_rows = jnp.pad(pieces(quarter_gain)[:, 0], ((0, 13), (0, 0)))
    y_index = lax.axis_index("y")
    steps = jnp.arange(NX, dtype=jnp.int32)
    below = (x_index + NX - steps) % NX
    above = (x_index + steps) % NX
    distance = (x_index + 2 * NX - (y_index + steps) % NY) % NX
    edges = jnp.stack([LEN - row_start, k_index]).astype(jnp.int32)
    place = jnp.concatenate([below, above, edges, distance]).astype(jnp.int32)
    border = place[8:9]

    weights = lax.all_gather(
        jnp.concatenate([w_value, w_gate, w_out], axis=1), TIME, axis=0, tiled=True
    )

    frames = swap_xy(frames)
    frames_z = gathered(frames, "z", NZ)
    taps = jnp.concatenate([kernel, bias[None, :]], axis=0)
    packed = jnp.concatenate([grad_out, pieces(taps).reshape(3 * (K + 1), COLS)], axis=0)
    packed = swap_xy(packed)
    grad_out = packed[:ROWS]
    grads = spread(grad_out, "x", NX)

    act_parts = call(
        act_kernel, shape((NZ, ROWS, COLS), bf16), (place, *grads, weights), smem=(0,), near=(1, 2, 3, 4, 5)
    )
    act_moved = exchange(act_parts, "z")
    pre_parts = call(
        project_kernel,
        [shape((ROWS + 48, 2 * COLS), bf16) for _ in range(NX)],
        (place, after(frames_z, act_parts), quarter_gain, gain_rows, weights),
        smem=(0,),
        near=(1, 4),
        late=(2, 3),
        scratch=[pltpu.VMEM((ROWS, QUARTER), bf16)],
    )
    pre_moved = [pre_parts[0]] + [shifted(pre_parts[j], "x", NX, j) for j in range(1, NX)]
    pre, gated, unit, stat = call(
        gate_kernel,
        [
            shape((ROWS, 2 * COLS), f32),
            shape((ROWS, COLS), bf16),
            shape((8, 2 * COLS), f32),
            shape((ROWS, 128), f32),
        ],
        tuple(pre_moved),
        near=(1, 2, 3),
    )
    act_grad = call(sum_kernel, shape((ROWS, COLS), bf16), (act_moved,), near=(0,))
    gated_low, gated_high = neighbours(gated[-EDGE:], gated[:EDGE])
    act_low, act_high = neighbours(act_grad[-16:], act_grad[:16])
    activated, slope, taps = call(
        forward_kernel,
        [
            shape((NZ, ROWS, COLS), bf16),
            shape((ROWS + 32, COLS), f32),
            shape((K + 1, COLS), f32),
        ],
        (border, gated, gated_low, gated_high, packed),
        smem=(0,),
        near=(2, 3),
        scratch=[
            pltpu.VMEM((ROWS + 2 * EDGE, COLS), f32),
            pltpu.VMEM((160, COLS), f32),
        ],
    )
    act_z = exchange(activated, "z")
    message, small = call(
        backward_kernel,
        [shape((ROWS + 32, 2 * COLS), bf16), shape((K + 1, COLS), f32)],
        (
            border,
            gated,
            gated_low,
            gated_high,
            act_grad,
            act_low,
            act_high,
            slope,
            taps,
            pre,
            unit,
        ),
        smem=(0,),
        near=(2, 3, 5, 6),
        scratch=[
            pltpu.VMEM((ROWS + 2 * EDGE, COLS), f32),
            pltpu.VMEM((ROWS + 32, COLS), f32),
            pltpu.VMEM((ROWS, COLS), f32),
            pltpu.VMEM((K + 1, 8, COLS), f32),
            pltpu.VMEM((160, COLS), f32),
            pltpu.VMEM((160, COLS), f32),
        ],
    )

    vg_grads = spread(message, "x", NX)
    norm_parts = call(
        norm_kernel,
        shape((NZ, ROWS + 48, COLS), bf16),
        (place, *vg_grads, after(weights, act_z)),
        smem=(0,),
        near=(2, 3, 4, 5),
        late=(1,),
    )
    norm_moved = exchange(norm_parts, "z")
    held = lax.optimization_barrier((vg_grads, norm_parts))[0]
    weight_parts = call(
        weight_kernel,
        shape((NY * QUARTER, 2 * COLS), bf16),
        (place, frames_z, quarter_gain, stat, *held),
        smem=(0,),
        near=(5, 6, 7),
        scratch=[pltpu.VMEM((ROWS, QUARTER), bf16)],
    )
    in_weight = lax.psum_scatter(
        weight_parts, TIME, scatter_dimension=0, tiled=True
    ).astype(f32)

    out_parts = call(
        out_kernel,
        [shape((ROWS, COLS), bf16) for _ in range(NX)]
        + [shape((NY, QUARTER // NK, COLS), bf16) for _ in range(2)],
        (place, act_z, *after(grads, norm_parts), weights),
        smem=(0,),
        near=(1, 6),
        scratch=[
            pltpu.VMEM((NK, ROWS, QUARTER // NK), bf16),
            pltpu.VMEM((ROWS, NY * COLS), bf16),
        ],
    )
    grad_out_weight = reduced(*out_parts[NX:])
    enc = [out_parts[0]] + [shifted(out_parts[j], "x", NX, j) for j in range(1, NX)]

    results, gain_term = call(
        input_kernel,
        [shape((ROWS, 2 * COLS), bf16), shape((8, COLS), f32)],
        (norm_moved, frames, grad_out, stat, local_gain, *enc),
        near=(0, 6, 7, 8),
    )
    results = swap_xy(results)
    encoded = results[:, :COLS]
    input_grad = results[:, COLS:]

    small = jnp.concatenate([small, gain_term], axis=0)
    small = small + lax.ppermute(small, "k", [(0, 1), (1, 0)])
    arrived = []
    for shift in range(NX):
        route = [
            (a * NY + b, ((b + shift) % NX) * NY + a) for a in range(NX) for b in range(NY)
        ]
        arrived.append(lax.ppermute(small, ("x", "y"), route))
    small = sum(after(arrived, results))
    return (
        encoded,
        input_grad,
        in_weight[:, :COLS],
        in_weight[:, COLS:],
        small[:K],
        small[K],
        grad_out_weight,
        small[K + 1],
    )


def solution(mesh):
    fine = Mesh(mesh.devices.reshape(NX, NK, NY, NZ), ("x", "k", "y", "z"))
    both = P(ROW, COL)
    return jax.shard_map(
        shards,
        mesh=fine,
        in_specs=(both, P(), both, both, P(None, COL), P(COL), both, both),
        out_specs=(both, both, both, both, P(None, COL), P(COL), both, P(COL)),
        check_vma=False,
    )
```

```python
import jax
import jax.numpy as jnp
from jax import lax
from jax.experimental import pallas as pl
from jax.experimental.pallas import tpu as pltpu
from jax.sharding import Mesh, PartitionSpec as P

K = 31
LEN = 2048
HALF = K // 2
NX, NK, NY, NZ = 4, 2, 4, 8
ROW = ("x", "k")
COL = ("y", "z")
TIME = ("y", "k")
ROWS = 384
COLS = 128
QUARTER = COLS * NZ
WIDTH = QUARTER * NX
EDGE = 32
GATHER_ROWS = 512
IN = (0, 2 * COLS)
OUT = (2 * COLS, COLS)

epsilon = 1e-05
f32 = jnp.float32
bf16 = jnp.bfloat16


def dot(left, right, left_dim, right_dim):
    return lax.dot_general(
        left, right, (((left_dim,), (right_dim,)), ((), ())), preferred_element_type=f32
    )


def split3(value):
    high = value.astype(bf16)
    rest = value - high.astype(f32)
    middle = rest.astype(bf16)
    low = (rest - middle.astype(f32)).astype(bf16)
    return high, middle, low


def one_hot():
    lane = lax.broadcasted_iota(jnp.int32, (16, 128), 1)
    row = lax.broadcasted_iota(jnp.int32, (16, 128), 0)
    return jnp.where(lane == row, 1.0, 0.0).astype(bf16)


def columns_to_rows(first, second):
    lane = lax.broadcasted_iota(jnp.int32, (first.shape[0], 128), 1)
    grid = jnp.zeros((first.shape[0], 128), f32)
    for j, piece in enumerate(split3(first) + split3(second)):
        grid = jnp.where(lane == j, piece.astype(f32), grid)
    return dot(one_hot(), grid.astype(bf16), 1, 1)


def rows_to_columns(rows):
    grid = dot(rows, one_hot(), 0, 0)
    first = grid[:, 0:1] + grid[:, 1:2] + grid[:, 2:3]
    second = grid[:, 3:4] + grid[:, 4:5] + grid[:, 5:6]
    return first, second


def stacked_rows(values):
    row = lax.broadcasted_iota(jnp.int32, (16, values[0].shape[1]), 0)
    out = jnp.zeros((16, values[0].shape[1]), f32)
    for j, value in enumerate(values):
        out = jnp.where(row == j, value.astype(f32), out)
    return out


def call(body, out_shape, args, smem=(), near=(), late=(), scratch=(), cuts=()):
    cuts = dict(cuts)
    single = not isinstance(out_shape, (list, tuple))
    outs = [out_shape] if single else list(out_shape)
    count = len(args)
    moved = [i for i in range(count) if i not in smem and i not in near]
    buffers = []
    for i in moved:
        dims = args[i].shape
        if i in cuts:
            dims = (dims[0], cuts[i][1])
        buffers.append(pltpu.VMEM(dims, args[i].dtype))
    for out in outs:
        buffers.append(pltpu.VMEM(out.shape, out.dtype))

    def whole(*refs):
        refs = list(refs)
        inputs, refs = refs[:count], refs[count:]
        results, refs = refs[: len(outs)], refs[len(outs) :]
        held, refs = refs[: len(buffers)], refs[len(buffers) :]
        sems, extra = refs[0], refs[1:]
        copies = {}
        for place, i in enumerate(moved):
            source = inputs[i]
            if i in cuts:
                source = source.at[:, pl.ds(cuts[i][0], cuts[i][1])]
            copies[i] = pltpu.make_async_copy(source, held[place], sems.at[place])
            inputs[i] = held[place]
        for copy in copies.values():
            copy.start()
        for i, copy in copies.items():
            if i not in late:
                copy.wait()
        sent = []

        def send(j, part=None):
            source, target = held[len(moved) + j], results[j]
            if part is not None:
                source, target = source.at[part], target.at[part]
            copy = pltpu.make_async_copy(source, target, sems.at[len(moved) + len(sent)])
            copy.start()
            sent.append((j, copy))

        hooks = (lambda i: copies[i].wait(), send) if late else ()
        body(*hooks, *inputs, *held[len(moved) :], *extra)
        already = {j for j, _ in sent}
        for j in range(len(outs)):
            if j not in already:
                send(j)
        for _, copy in sent:
            copy.wait()

    hbm = pl.BlockSpec(memory_space=pltpu.MemorySpace.HBM)
    spaces = [
        pltpu.MemorySpace.SMEM
        if i in smem
        else (pltpu.MemorySpace.VMEM if i in near else pltpu.MemorySpace.HBM)
        for i in range(count)
    ]
    made = pl.pallas_call(
        whole,
        out_shape=[pltpu.HBM(out.shape, out.dtype) for out in outs],
        in_specs=[pl.BlockSpec(memory_space=space) for space in spaces],
        out_specs=[hbm] * len(outs),
        scratch_shapes=buffers + [pltpu.SemaphoreType.DMA((len(moved) + max(len(outs), NZ),))] + list(scratch),
        compiler_params=pltpu.CompilerParams(vmem_limit_bytes=24 * 1024 * 1024),
        name=body.__name__,
    )(
        *[
            pltpu.with_memory_space_constraint(arg, pltpu.HBM) if i in moved else arg
            for i, arg in enumerate(args)
        ]
    )
    return made[0] if single else made


def shape(dims, kind):
    return jax.ShapeDtypeStruct(dims, kind)


def project_kernel(arrive, send, place_ref, frames_ref, gain_ref, weight_ref, *refs):
    left_ref = refs[NX]
    total = jnp.zeros((ROWS, 1), f32)
    square = jnp.zeros((ROWS, 1), f32)
    for i in range(NZ):
        wide = frames_ref[i].astype(f32)
        total = total + jnp.sum(wide, axis=1, keepdims=True)
        square = square + jnp.sum(wide * wide, axis=1, keepdims=True)
    mean = total / QUARTER
    arrive(2)
    gain = gain_ref[...]
    gain_rows = stacked_rows(split3(gain)).astype(bf16)
    for i in range(NZ):
        cut = pl.ds(i * COLS, COLS)
        scaled = (frames_ref[i].astype(f32) - mean) * gain_ref[0:1, cut]
        left_ref[:, cut] = scaled.astype(bf16)
    sums = columns_to_rows(total, square).astype(bf16)
    for j, out_ref in enumerate(refs[:NX]):
        start = pl.multiple_of(place_ref[4 + j] * QUARTER, QUARTER)
        weight = weight_ref[pl.ds(start, QUARTER), 0 : 2 * COLS]
        out_ref[0:ROWS, :] = dot(left_ref[...], weight, 1, 0).astype(bf16)
        unit = jnp.sum(dot(gain_rows, weight, 1, 0), axis=0, keepdims=True)
        out_ref[ROWS : ROWS + 16, :] = stacked_rows(split3(unit)).astype(bf16)
        out_ref[ROWS + 16 : ROWS + 32, :] = sums[:, 0:256]
        out_ref[ROWS + 32 : ROWS + 48, 0:128] = sums[:, 256:384]
        out_ref[ROWS + 32 : ROWS + 48, 128:256] = jnp.zeros((16, 128), bf16)
        send(j)


def gate_kernel(p0_ref, p1_ref, p2_ref, p3_ref, pre_ref, gated_ref, unit_ref, stat_ref):
    parts = (p0_ref, p1_ref, p2_ref, p3_ref)
    totals, squares, units = [], [], []
    for part_ref in parts:
        rows = jnp.concatenate(
            [part_ref[ROWS + 16 : ROWS + 32, :], part_ref[ROWS + 32 : ROWS + 48, 0:128]], axis=1
        )
        first, second = rows_to_columns(rows)
        totals.append(first)
        squares.append(second)
        pieces = part_ref[ROWS : ROWS + 16, :].astype(f32)
        units.append(jnp.sum(pieces, axis=0, keepdims=True))
    mean = sum(totals) / WIDTH
    inv_std = lax.rsqrt(sum(squares) / WIDTH - mean * mean + epsilon)
    pre = jnp.zeros((ROWS, 2 * COLS), f32)
    for i, part_ref in enumerate(parts):
        pre = pre + part_ref[0:ROWS, :].astype(f32)
        pre = pre + (totals[i] / QUARTER - mean) * units[i]
    pre = pre * inv_std
    pre_ref[...] = pre
    gated_ref[...] = (pre[:, 0:COLS] * jax.nn.sigmoid(pre[:, COLS:])).astype(bf16)
    unit_ref[...] = jnp.broadcast_to(sum(units), (8, 2 * COLS))
    lane = lax.broadcasted_iota(jnp.int32, (ROWS, 128), 1)
    stat_ref[...] = jnp.where(lane == 0, mean, inv_std)


def act_kernel(place_ref, g0_ref, g1_ref, g2_ref, g3_ref, weight_ref, out_ref):
    total = jnp.zeros((ROWS, QUARTER), f32)
    for j, grad_ref in enumerate((g0_ref, g1_ref, g2_ref, g3_ref)):
        start = pl.multiple_of(place_ref[j] * QUARTER, QUARTER)
        weight = weight_ref[pl.ds(start, QUARTER), 2 * COLS : 3 * COLS]
        total = total + dot(grad_ref[...], weight, 1, 1)
    for i in range(NZ):
        out_ref[i] = total[:, i * COLS : (i + 1) * COLS].astype(bf16)


def sum_kernel(parts_ref, out_ref):
    total = jnp.zeros((ROWS, COLS), f32)
    for i in range(NZ):
        total = total + parts_ref[i].astype(f32)
    out_ref[...] = total.astype(bf16)


CHUNKS = [(-16, 16), (0, 128), (128, 128), (256, 128), (ROWS, 16)]


def same_clip(border, start, count):
    row = lax.broadcasted_iota(jnp.int32, (count + 32, COLS), 0) + (start - 16)
    inside = (row < border).astype(jnp.int32)
    own = jnp.where(start < border, 1, 0)
    return inside == own


def conv_kernel(
    place_ref,
    gated_ref,
    act_ref,
    low_ref,
    high_ref,
    taps_ref,
    pre_ref,
    unit_ref,
    activated_ref,
    message_ref,
    small_ref,
    wide_ref,
    grad_ref,
    glu_ref,
    sums_ref,
    masked_ref,
    masked_grad_ref,
    kernel_ref,
):
    border = place_ref[0]
    total = jnp.zeros((K + 1, COLS), f32)
    for i in range(3):
        total = total + taps_ref[pl.ds(ROWS + i * (K + 1), K + 1), :].astype(f32)
    kernel_ref[...] = total
    wide_ref[0:EDGE, :] = low_ref[0:EDGE, :].astype(f32)
    wide_ref[EDGE : EDGE + ROWS, :] = gated_ref[...].astype(f32)
    wide_ref[EDGE + ROWS :, :] = high_ref[0:EDGE, :].astype(f32)
    sums_ref[...] = jnp.zeros((K + 1, 8, COLS), f32)
    bias = kernel_ref[K : K + 1, :]
    for start, count in CHUNKS:
        here = wide_ref[pl.ds(start - 16 + EDGE, count + 32), :]
        masked_ref[0 : count + 32, :] = jnp.where(same_clip(border, start, count), here, 0.0)
        conv = jnp.broadcast_to(bias, (count, COLS))
        for tap in range(K):
            conv = conv + kernel_ref[tap : tap + 1, :] * masked_ref[1 + tap : 1 + tap + count, :]
        sig = jax.nn.sigmoid(conv)
        if start < 0:
            act = low_ref[EDGE:, :]
        elif start < ROWS:
            act = act_ref[pl.ds(start, count), :]
        else:
            act = high_ref[EDGE:, :]
        grad = (act.astype(f32) * sig * (1.0 + conv * (1.0 - sig))).astype(bf16).astype(f32)
        grad_ref[pl.ds(start + 16, count), :] = grad
        if 0 <= start < ROWS:
            activated_ref[pl.ds(start, count), :] = (conv * sig).astype(bf16)
            for tap in range(K):
                product = grad * masked_ref[1 + tap : 1 + tap + count, :]
                sums_ref[tap] += jnp.sum(product.reshape(count // 8, 8, COLS), axis=0)
            sums_ref[K] += jnp.sum(grad.reshape(count // 8, 8, COLS), axis=0)
    activated_ref[ROWS:, :] = jnp.zeros((GATHER_ROWS - ROWS, COLS), bf16)
    small_ref[...] = jnp.sum(sums_ref[...], axis=1)

    for start, count in CHUNKS[1:4]:
        here = grad_ref[pl.ds(start, count + 32), :]
        masked_grad_ref[...] = jnp.where(same_clip(border, start, count), here, 0.0)
        glu = jnp.zeros((count, COLS), f32)
        for tap in range(K):
            glu = glu + kernel_ref[tap : tap + 1, :] * masked_grad_ref[31 - tap : 31 - tap + count, :]
        glu_ref[pl.ds(start, count), :] = glu

    glu = glu_ref[...]
    value_pre = pre_ref[:, 0:COLS]
    gate_pre = pre_ref[:, COLS:]
    gate_sig = jax.nn.sigmoid(gate_pre)
    value_grad = (glu * gate_sig).astype(bf16)
    gate_grad = (glu * value_pre * gate_sig * (1.0 - gate_sig)).astype(bf16)
    message_ref[0:ROWS, 0:COLS] = value_grad
    message_ref[0:ROWS, COLS:] = gate_grad
    value_wide = value_grad.astype(f32)
    gate_wide = gate_grad.astype(f32)
    first = jnp.sum(
        value_wide * unit_ref[0:1, 0:COLS] + gate_wide * unit_ref[0:1, COLS:],
        axis=1,
        keepdims=True,
    )
    second = jnp.sum(value_wide * value_pre + gate_wide * gate_pre, axis=1, keepdims=True)
    rows = columns_to_rows(first, second).astype(bf16)
    message_ref[ROWS : ROWS + 16, :] = rows[:, 0:256]
    message_ref[ROWS + 16 : ROWS + 32, 0:128] = rows[:, 256:384]
    message_ref[ROWS + 16 : ROWS + 32, 128:256] = jnp.zeros((16, 128), bf16)


def norm_kernel(arrive, send, place_ref, g0_ref, g1_ref, g2_ref, g3_ref, weight_ref, out_ref):
    rows = jnp.zeros((16, ROWS), f32)
    arrive(1)
    grads = (g0_ref, g1_ref, g2_ref, g3_ref)
    for grad_ref in grads:
        here = jnp.concatenate(
            [grad_ref[ROWS : ROWS + 16, :], grad_ref[ROWS + 16 : ROWS + 32, 0:128]], axis=1
        )
        rows = rows + here.astype(f32)
    first = rows[0:1] + rows[1:2] + rows[2:3]
    second = rows[3:4] + rows[4:5] + rows[5:6]
    sums = stacked_rows(split3(first) + split3(second)).astype(bf16)
    step = 2 * COLS
    for part in range(QUARTER // step):
        total = jnp.zeros((ROWS, step), f32)
        for j, grad_ref in enumerate(grads):
            start = pl.multiple_of(place_ref[j] * QUARTER + part * step, step)
            weight = weight_ref[pl.ds(start, step), 0 : 2 * COLS]
            total = total + dot(grad_ref[0:ROWS, :], weight, 1, 1)
        for i in (2 * part, 2 * part + 1):
            cut = (i - 2 * part) * COLS
            out_ref[i, 0:ROWS, :] = total[:, cut : cut + COLS].astype(bf16)
            for j in range(3):
                rows_here = sums[:, j * 128 : (j + 1) * 128]
                out_ref[i, ROWS + 16 * j : ROWS + 16 * j + 16, :] = rows_here
            send(0, i)


def weight_kernel(
    place_ref,
    frames_ref,
    gain_ref,
    stat_ref,
    g0_ref,
    g1_ref,
    g2_ref,
    g3_ref,
    kept_ref,
    given_ref,
    left_ref,
    right_ref,
):
    mean = stat_ref[:, 0:1]
    inv_std = stat_ref[:, 1:2]
    half = QUARTER // NK
    for i in range(NZ):
        cut = pl.ds(i * COLS, COLS)
        scaled = (frames_ref[i].astype(f32) - mean) * inv_std * gain_ref[0:1, cut]
        left_ref[i * COLS // half, :, pl.ds(i * COLS % half, COLS)] = scaled.astype(bf16)
    order_blocks(place_ref, 10, (g0_ref, g1_ref, g2_ref, g3_ref), right_ref, 2 * COLS)
    core = place_ref[9]
    for out_ref, which in ((given_ref, 1 - core), (kept_ref, core)):
        out = dot(left_ref[which], right_ref[...], 0, 0).astype(bf16)
        for i in range(NY):
            out_ref[i] = out[:, i * 2 * COLS : (i + 1) * 2 * COLS]


def order_blocks(place_ref, base, sources, out_ref, lanes):
    for i in range(NY):
        source = place_ref[base + i]
        for j, block_ref in enumerate(sources):

            @pl.when(source == j)
            def _(block_ref=block_ref, i=i):
                out_ref[:, i * lanes : (i + 1) * lanes] = block_ref[0:ROWS, :]


def encode_kernel(arrive, send, place_ref, act_ref, weight_ref, *refs):
    left_ref = refs[NX]
    arrive(1)
    for i in range(NZ):
        left_ref[:, pl.ds(i * COLS, COLS)] = act_ref[i, 0:ROWS, :]
    for j, enc_ref in enumerate(refs[:NX]):
        start = pl.multiple_of(place_ref[4 + j] * QUARTER, QUARTER)
        weight = weight_ref[pl.ds(start, QUARTER), 2 * COLS : 3 * COLS]
        enc_ref[...] = dot(left_ref[...], weight, 1, 0).astype(bf16)
        send(j)


def out_kernel(
    place_ref, act_ref, g0_ref, g1_ref, g2_ref, g3_ref, kept_ref, given_ref, left_ref, grad_ref
):
    half = QUARTER // NK
    for i in range(NZ):
        left_ref[i * COLS // half, :, pl.ds(i * COLS % half, COLS)] = act_ref[i, 0:ROWS, :]
    order_blocks(place_ref, 0, (g0_ref, g1_ref, g2_ref, g3_ref), grad_ref, COLS)
    core = place_ref[9]
    for out_ref, which in ((given_ref, 1 - core), (kept_ref, core)):
        out = dot(left_ref[which], grad_ref[...], 0, 0).astype(bf16)
        for i in range(NY):
            out_ref[i] = out[:, i * COLS : (i + 1) * COLS]


def input_kernel(
    parts_ref,
    frames_ref,
    grad_ref,
    stat_ref,
    gain_ref,
    e0_ref,
    e1_ref,
    e2_ref,
    e3_ref,
    out_ref,
    small_ref,
):
    normed_grad = jnp.zeros((ROWS, COLS), f32)
    rows = jnp.zeros((16, ROWS), f32)
    for i in range(NZ):
        normed_grad = normed_grad + parts_ref[i, 0:ROWS, :].astype(f32)
        here = [parts_ref[i, ROWS + 16 * j : ROWS + 16 * j + 16, :] for j in range(3)]
        rows = rows + jnp.concatenate(here, axis=1).astype(f32)
    first = rows[0:1] + rows[1:2] + rows[2:3]
    second = rows[3:4] + rows[4:5] + rows[5:6]
    sums = stacked_rows(split3(first) + split3(second)).astype(bf16)
    first, second = rows_to_columns(sums)
    mean = stat_ref[:, 0:1]
    inv_std = stat_ref[:, 1:2]
    centred = (frames_ref[...].astype(f32) - mean) * inv_std
    hat = normed_grad * gain_ref[0:1, :]
    out = grad_ref[...].astype(f32) + inv_std * (hat - first / WIDTH - centred * (second / WIDTH))
    out_ref[:, COLS:] = out.astype(bf16)
    encoded = frames_ref[...].astype(f32)
    for part_ref in (e0_ref, e1_ref, e2_ref, e3_ref):
        encoded = encoded + part_ref[...].astype(f32)
    out_ref[:, 0:COLS] = encoded.astype(bf16)
    gain_term = jnp.sum(normed_grad * centred, axis=0, keepdims=True)
    small_ref[...] = jnp.broadcast_to(gain_term, (8, COLS))


def swap_xy(block):
    return lax.ppermute(
        block, ("x", "y"), [(a * NY + b, b * NY + a) for a in range(NX) for b in range(NY)]
    )


def neighbours(upper, lower):
    place = [k * NY + y for y in range(NY) for k in range(NK)]
    forward = list(zip(place[:-1], place[1:]))
    backward = [(target, source) for source, target in forward]
    low = lax.ppermute(upper, ("k", "y"), forward)
    high = lax.ppermute(lower, ("k", "y"), backward)
    return low, high


def exchange(parts, axis):
    return lax.all_to_all(parts, axis, 0, 0, tiled=True)


def gathered(block, axis, count):
    return exchange(jnp.broadcast_to(block[None], (count,) + block.shape), axis)


def shifted(block, axis, count, shift):
    return lax.ppermute(block, axis, [(i, (i + shift) % count) for i in range(count)])


def spread(block, axis, count):
    return [block] + [shifted(block, axis, count, j) for j in range(1, count)]


def reduced(kept, given):
    other = lax.ppermute(given, "k", [(0, 1), (1, 0)])
    both = [(kept[i].astype(f32) + other[i].astype(f32)) for i in range(NY)]
    sent = [part.astype(bf16) for part in both[1:]]
    total = both[0]
    for i in range(1, NY):
        total = total + shifted(sent[i - 1], "y", NY, i).astype(f32)
    return total, sent


def pieces(value):
    out = []
    for _ in range(3):
        piece = lax.reduce_precision(value, 8, 7)
        out.append(piece.astype(bf16))
        value = value - piece
    return jnp.stack(out)


def after(value, *others):
    return lax.optimization_barrier((value,) + others)[0]


def shards(frames, gain, w_value, w_gate, kernel, bias, w_out, grad_out):
    x_index = lax.axis_index("x")
    k_index = lax.axis_index("k")
    row_start = (lax.axis_index("y") * NK + k_index) * ROWS
    col_start = (x_index * NZ + lax.axis_index("z")) * COLS
    local_gain = lax.dynamic_slice_in_dim(gain, col_start, COLS, 0)[None]
    quarter_gain = lax.dynamic_slice_in_dim(gain, x_index * QUARTER, QUARTER, 0)[None]
    y_index = lax.axis_index("y")
    steps = jnp.arange(NX, dtype=jnp.int32)
    below = (x_index + NX - steps) % NX
    above = (x_index + steps) % NX
    distance = (x_index + 2 * NX - (y_index + steps) % NY) % NX
    edges = jnp.stack([LEN - row_start, k_index]).astype(jnp.int32)
    place = jnp.concatenate([below, above, edges, distance]).astype(jnp.int32)
    border = place[8:9]

    weights = lax.all_gather(
        jnp.concatenate([w_value, w_gate, w_out], axis=1), TIME, axis=0, tiled=True
    )

    frames = swap_xy(frames)
    frames_z = gathered(frames, "z", NZ)
    taps = jnp.concatenate([kernel, bias[None, :]], axis=0)
    packed = jnp.concatenate([grad_out, pieces(taps).reshape(3 * (K + 1), COLS)], axis=0)
    packed = swap_xy(packed)
    grad_out = packed[:ROWS]
    grads = spread(grad_out, "x", NX)

    act_parts = call(
        act_kernel, shape((NZ, ROWS, COLS), bf16), (place, *grads, weights), smem=(0,), near=(1, 2, 3, 4, 5)
    )
    act_moved = exchange(act_parts, "z")
    pre_parts = call(
        project_kernel,
        [shape((ROWS + 48, 2 * COLS), bf16) for _ in range(NX)],
        (place, after(frames_z, act_parts), quarter_gain, weights),
        smem=(0,),
        near=(1, 3),
        late=(2,),
        scratch=[pltpu.VMEM((ROWS, QUARTER), bf16)],
    )
    pre_moved = [pre_parts[0]] + [shifted(pre_parts[j], "x", NX, j) for j in range(1, NX)]
    pre, gated, unit, stat = call(
        gate_kernel,
        [
            shape((ROWS, 2 * COLS), f32),
            shape((ROWS, COLS), bf16),
            shape((8, 2 * COLS), f32),
            shape((ROWS, 128), f32),
        ],
        tuple(pre_moved),
        near=(1, 2, 3),
    )
    act_grad = call(sum_kernel, shape((ROWS, COLS), bf16), (act_moved,), near=(0,))
    low, high = neighbours(
        jnp.concatenate([gated[-EDGE:], act_grad[-16:]], axis=0),
        jnp.concatenate([gated[:EDGE], act_grad[:16]], axis=0),
    )
    activated, message, small = call(
        conv_kernel,
        [
            shape((GATHER_ROWS, COLS), bf16),
            shape((ROWS + 32, 2 * COLS), bf16),
            shape((K + 1, COLS), f32),
        ],
        (border, gated, act_grad, low, high, packed, pre, unit),
        smem=(0,),
        near=(3, 4),
        scratch=[
            pltpu.VMEM((ROWS + 2 * EDGE, COLS), f32),
            pltpu.VMEM((ROWS + 32, COLS), f32),
            pltpu.VMEM((ROWS, COLS), f32),
            pltpu.VMEM((K + 1, 8, COLS), f32),
            pltpu.VMEM((160, COLS), f32),
            pltpu.VMEM((160, COLS), f32),
            pltpu.VMEM((K + 1, COLS), f32),
        ],
    )
    act_z = lax.all_gather(activated, "z", axis=0, tiled=False)

    vg_grads = spread(message, "x", NX)
    norm_parts = call(
        norm_kernel,
        shape((NZ, ROWS + 48, COLS), bf16),
        (place, *vg_grads, weights),
        smem=(0,),
        near=(2, 3, 4, 5),
        late=(1,),
    )
    norm_moved = exchange(norm_parts, "z")
    held = lax.optimization_barrier((vg_grads, norm_parts))[0]
    kept, given = call(
        weight_kernel,
        [shape((NY, QUARTER // NK, 2 * COLS), bf16) for _ in range(2)],
        (place, frames_z, quarter_gain, stat, *held),
        smem=(0,),
        near=(5, 6, 7),
        scratch=[
            pltpu.VMEM((NK, ROWS, QUARTER // NK), bf16),
            pltpu.VMEM((ROWS, NY * 2 * COLS), bf16),
        ],
    )
    in_weight, in_sent = reduced(kept, given)

    enc_parts = call(
        encode_kernel,
        [shape((ROWS, COLS), bf16) for _ in range(NX)],
        (place, act_z, after(weights, in_sent)),
        smem=(0,),
        near=(2,),
        late=(1,),
        scratch=[pltpu.VMEM((ROWS, QUARTER), bf16)],
    )
    enc = [enc_parts[0]] + [shifted(enc_parts[j], "x", NX, j) for j in range(1, NX)]
    kept, given = call(
        out_kernel,
        [shape((NY, QUARTER // NK, COLS), bf16) for _ in range(2)],
        (place, after(act_z, enc_parts), *grads),
        smem=(0,),
        scratch=[
            pltpu.VMEM((NK, ROWS, QUARTER // NK), bf16),
            pltpu.VMEM((ROWS, NY * COLS), bf16),
        ],
    )
    other = lax.ppermute(given, "k", [(0, 1), (1, 0)])
    both = (kept.astype(f32) + other.astype(f32)).astype(bf16)
    grad_out_weight = lax.psum_scatter(
        both.reshape(NY * QUARTER // NK, COLS), "y", scatter_dimension=0, tiled=True
    ).astype(f32)

    results, gain_term = call(
        input_kernel,
        [shape((ROWS, 2 * COLS), bf16), shape((8, COLS), f32)],
        (after(norm_moved, both), frames, grad_out, stat, local_gain, *enc),
        near=(0, 6, 7, 8),
    )
    results = swap_xy(results)
    encoded = results[:, :COLS]
    input_grad = results[:, COLS:]

    small = jnp.concatenate([small, gain_term], axis=0)
    small = small + lax.ppermute(small, "k", [(0, 1), (1, 0)])
    arrived = []
    for shift in range(NX):
        route = [
            (a * NY + b, ((b + shift) % NX) * NY + a) for a in range(NX) for b in range(NY)
        ]
        arrived.append(lax.ppermute(small, ("x", "y"), route))
    small = sum(after(arrived, results))
    return (
        encoded,
        input_grad,
        in_weight[:, :COLS],
        in_weight[:, COLS:],
        small[:K],
        small[K],
        grad_out_weight,
        small[K + 1],
    )


def solution(mesh):
    fine = Mesh(mesh.devices.reshape(NX, NK, NY, NZ), ("x", "k", "y", "z"))
    both = P(ROW, COL)
    return jax.shard_map(
        shards,
        mesh=fine,
        in_specs=(both, P(), both, both, P(None, COL), P(COL), both, both),
        out_specs=(both, both, both, both, P(None, COL), P(COL), both, P(COL)),
        check_vma=False,
    )
```

```python
import jax
import jax.numpy as jnp
from jax import lax
from jax.experimental import pallas as pl
from jax.experimental.pallas import tpu as pltpu
from jax.sharding import Mesh, PartitionSpec as P

K = 31
LEN = 2048
HALF = K // 2
NX, NK, NY, NZ = 4, 2, 4, 8
ROW = ("x", "k")
COL = ("y", "z")
TIME = ("y", "k")
ROWS = 384
COLS = 128
QUARTER = COLS * NZ
WIDTH = QUARTER * NX
EDGE = 32
IN = (0, 2 * COLS)
OUT = (2 * COLS, COLS)

epsilon = 1e-05
f32 = jnp.float32
bf16 = jnp.bfloat16


def dot(left, right, left_dim, right_dim):
    return lax.dot_general(
        left, right, (((left_dim,), (right_dim,)), ((), ())), preferred_element_type=f32
    )


def split3(value):
    high = value.astype(bf16)
    rest = value - high.astype(f32)
    middle = rest.astype(bf16)
    low = (rest - middle.astype(f32)).astype(bf16)
    return high, middle, low


def one_hot():
    lane = lax.broadcasted_iota(jnp.int32, (16, 128), 1)
    row = lax.broadcasted_iota(jnp.int32, (16, 128), 0)
    return jnp.where(lane == row, 1.0, 0.0).astype(bf16)


def columns_to_rows(first, second):
    lane = lax.broadcasted_iota(jnp.int32, (first.shape[0], 128), 1)
    grid = jnp.zeros((first.shape[0], 128), f32)
    for j, piece in enumerate(split3(first) + split3(second)):
        grid = jnp.where(lane == j, piece.astype(f32), grid)
    return dot(one_hot(), grid.astype(bf16), 1, 1)


def rows_to_columns(rows):
    grid = dot(rows, one_hot(), 0, 0)
    first = grid[:, 0:1] + grid[:, 1:2] + grid[:, 2:3]
    second = grid[:, 3:4] + grid[:, 4:5] + grid[:, 5:6]
    return first, second


def stacked_rows(values):
    row = lax.broadcasted_iota(jnp.int32, (16, values[0].shape[1]), 0)
    out = jnp.zeros((16, values[0].shape[1]), f32)
    for j, value in enumerate(values):
        out = jnp.where(row == j, value.astype(f32), out)
    return out


def call(body, out_shape, args, smem=(), near=(), late=(), scratch=(), cuts=()):
    cuts = dict(cuts)
    single = not isinstance(out_shape, (list, tuple))
    outs = [out_shape] if single else list(out_shape)
    count = len(args)
    moved = [i for i in range(count) if i not in smem and i not in near]
    buffers = []
    for i in moved:
        dims = args[i].shape
        if i in cuts:
            dims = (dims[0], cuts[i][1])
        buffers.append(pltpu.VMEM(dims, args[i].dtype))
    for out in outs:
        buffers.append(pltpu.VMEM(out.shape, out.dtype))

    def whole(*refs):
        refs = list(refs)
        inputs, refs = refs[:count], refs[count:]
        results, refs = refs[: len(outs)], refs[len(outs) :]
        held, refs = refs[: len(buffers)], refs[len(buffers) :]
        sems, extra = refs[0], refs[1:]
        copies = {}
        for place, i in enumerate(moved):
            source = inputs[i]
            if i in cuts:
                source = source.at[:, pl.ds(cuts[i][0], cuts[i][1])]
            copies[i] = pltpu.make_async_copy(source, held[place], sems.at[place])
            inputs[i] = held[place]
        for copy in copies.values():
            copy.start()
        for i, copy in copies.items():
            if i not in late:
                copy.wait()
        sent = []

        def send(j, part=None):
            source, target = held[len(moved) + j], results[j]
            if part is not None:
                source, target = source.at[part], target.at[part]
            copy = pltpu.make_async_copy(source, target, sems.at[len(moved) + len(sent)])
            copy.start()
            sent.append((j, copy))

        hooks = (lambda i: copies[i].wait(), send) if late else ()
        body(*hooks, *inputs, *held[len(moved) :], *extra)
        already = {j for j, _ in sent}
        for j in range(len(outs)):
            if j not in already:
                send(j)
        for _, copy in sent:
            copy.wait()

    hbm = pl.BlockSpec(memory_space=pltpu.MemorySpace.HBM)
    spaces = [
        pltpu.MemorySpace.SMEM
        if i in smem
        else (pltpu.MemorySpace.VMEM if i in near else pltpu.MemorySpace.HBM)
        for i in range(count)
    ]
    made = pl.pallas_call(
        whole,
        out_shape=[pltpu.HBM(out.shape, out.dtype) for out in outs],
        in_specs=[pl.BlockSpec(memory_space=space) for space in spaces],
        out_specs=[hbm] * len(outs),
        scratch_shapes=buffers + [pltpu.SemaphoreType.DMA((len(moved) + max(len(outs), NZ),))] + list(scratch),
        compiler_params=pltpu.CompilerParams(vmem_limit_bytes=24 * 1024 * 1024),
        name=body.__name__,
    )(
        *[
            pltpu.with_memory_space_constraint(arg, pltpu.HBM) if i in moved else arg
            for i, arg in enumerate(args)
        ]
    )
    return made[0] if single else made


def shape(dims, kind):
    return jax.ShapeDtypeStruct(dims, kind)


def project_kernel(arrive, send, place_ref, frames_ref, gain_ref, weight_ref, *refs):
    left_ref = refs[NX]
    total = jnp.zeros((ROWS, 1), f32)
    square = jnp.zeros((ROWS, 1), f32)
    for i in range(NZ):
        wide = frames_ref[i].astype(f32)
        total = total + jnp.sum(wide, axis=1, keepdims=True)
        square = square + jnp.sum(wide * wide, axis=1, keepdims=True)
    mean = total / QUARTER
    arrive(2)
    gain = gain_ref[...]
    gain_rows = stacked_rows(split3(gain)).astype(bf16)
    for i in range(NZ):
        cut = pl.ds(i * COLS, COLS)
        scaled = (frames_ref[i].astype(f32) - mean) * gain_ref[0:1, cut]
        left_ref[:, cut] = scaled.astype(bf16)
    sums = columns_to_rows(total, square).astype(bf16)
    for j, out_ref in enumerate(refs[:NX]):
        start = pl.multiple_of(place_ref[4 + j] * QUARTER, QUARTER)
        weight = weight_ref[pl.ds(start, QUARTER), 0 : 2 * COLS]
        out_ref[0:ROWS, :] = dot(left_ref[...], weight, 1, 0).astype(bf16)
        unit = jnp.sum(dot(gain_rows, weight, 1, 0), axis=0, keepdims=True)
        out_ref[ROWS : ROWS + 16, :] = stacked_rows(split3(unit)).astype(bf16)
        out_ref[ROWS + 16 : ROWS + 32, :] = sums[:, 0:256]
        out_ref[ROWS + 32 : ROWS + 48, 0:128] = sums[:, 256:384]
        out_ref[ROWS + 32 : ROWS + 48, 128:256] = jnp.zeros((16, 128), bf16)
        send(j)


def gate_kernel(p0_ref, p1_ref, p2_ref, p3_ref, pre_ref, gated_ref, unit_ref, stat_ref):
    parts = (p0_ref, p1_ref, p2_ref, p3_ref)
    totals, squares, units = [], [], []
    for part_ref in parts:
        rows = jnp.concatenate(
            [part_ref[ROWS + 16 : ROWS + 32, :], part_ref[ROWS + 32 : ROWS + 48, 0:128]], axis=1
        )
        first, second = rows_to_columns(rows)
        totals.append(first)
        squares.append(second)
        pieces = part_ref[ROWS : ROWS + 16, :].astype(f32)
        units.append(jnp.sum(pieces, axis=0, keepdims=True))
    mean = sum(totals) / WIDTH
    inv_std = lax.rsqrt(sum(squares) / WIDTH - mean * mean + epsilon)
    pre = jnp.zeros((ROWS, 2 * COLS), f32)
    for i, part_ref in enumerate(parts):
        pre = pre + part_ref[0:ROWS, :].astype(f32)
        pre = pre + (totals[i] / QUARTER - mean) * units[i]
    pre = pre * inv_std
    pre_ref[...] = pre
    gated_ref[...] = (pre[:, 0:COLS] * jax.nn.sigmoid(pre[:, COLS:])).astype(bf16)
    unit_ref[...] = jnp.broadcast_to(sum(units), (8, 2 * COLS))
    lane = lax.broadcasted_iota(jnp.int32, (ROWS, 128), 1)
    stat_ref[...] = jnp.where(lane == 0, mean, inv_std)


def act_kernel(place_ref, g0_ref, g1_ref, g2_ref, g3_ref, weight_ref, out_ref):
    total = jnp.zeros((ROWS, QUARTER), f32)
    for j, grad_ref in enumerate((g0_ref, g1_ref, g2_ref, g3_ref)):
        start = pl.multiple_of(place_ref[j] * QUARTER, QUARTER)
        weight = weight_ref[pl.ds(start, QUARTER), 2 * COLS : 3 * COLS]
        total = total + dot(grad_ref[...], weight, 1, 1)
    for i in range(NZ):
        out_ref[i] = total[:, i * COLS : (i + 1) * COLS].astype(bf16)


def sum_kernel(parts_ref, out_ref):
    total = jnp.zeros((ROWS, COLS), f32)
    for i in range(NZ):
        total = total + parts_ref[i].astype(f32)
    out_ref[...] = total.astype(bf16)


CHUNKS = [(-16, 16), (0, 128), (128, 128), (256, 128), (ROWS, 16)]


def same_clip(border, start, count):
    row = lax.broadcasted_iota(jnp.int32, (count + 32, COLS), 0) + (start - 16)
    inside = (row < border).astype(jnp.int32)
    own = jnp.where(start < border, 1, 0)
    return inside == own


def conv_kernel(
    place_ref,
    gated_ref,
    act_ref,
    low_ref,
    high_ref,
    taps_ref,
    pre_ref,
    unit_ref,
    activated_ref,
    message_ref,
    small_ref,
    wide_ref,
    grad_ref,
    glu_ref,
    sums_ref,
    masked_ref,
    masked_grad_ref,
    kernel_ref,
):
    border = place_ref[0]
    total = jnp.zeros((K + 1, COLS), f32)
    for i in range(3):
        total = total + taps_ref[pl.ds(ROWS + i * (K + 1), K + 1), :].astype(f32)
    kernel_ref[...] = total
    wide_ref[0:EDGE, :] = low_ref[0:EDGE, :].astype(f32)
    wide_ref[EDGE : EDGE + ROWS, :] = gated_ref[...].astype(f32)
    wide_ref[EDGE + ROWS :, :] = high_ref[0:EDGE, :].astype(f32)
    sums_ref[...] = jnp.zeros((K + 1, 8, COLS), f32)
    bias = kernel_ref[K : K + 1, :]
    for start, count in CHUNKS:
        here = wide_ref[pl.ds(start - 16 + EDGE, count + 32), :]
        masked_ref[0 : count + 32, :] = jnp.where(same_clip(border, start, count), here, 0.0)
        conv = jnp.broadcast_to(bias, (count, COLS))
        for tap in range(K):
            conv = conv + kernel_ref[tap : tap + 1, :] * masked_ref[1 + tap : 1 + tap + count, :]
        sig = jax.nn.sigmoid(conv)
        if start < 0:
            act = low_ref[EDGE:, :]
        elif start < ROWS:
            act = act_ref[pl.ds(start, count), :]
        else:
            act = high_ref[EDGE:, :]
        grad = (act.astype(f32) * sig * (1.0 + conv * (1.0 - sig))).astype(bf16).astype(f32)
        grad_ref[pl.ds(start + 16, count), :] = grad
        if 0 <= start < ROWS:
            activated_ref[pl.ds(start, count), :] = (conv * sig).astype(bf16)
            for tap in range(K):
                product = grad * masked_ref[1 + tap : 1 + tap + count, :]
                sums_ref[tap] += jnp.sum(product.reshape(count // 8, 8, COLS), axis=0)
            sums_ref[K] += jnp.sum(grad.reshape(count // 8, 8, COLS), axis=0)
    small_ref[...] = jnp.sum(sums_ref[...], axis=1)

    for start, count in CHUNKS[1:4]:
        here = grad_ref[pl.ds(start, count + 32), :]
        masked_grad_ref[...] = jnp.where(same_clip(border, start, count), here, 0.0)
        glu = jnp.zeros((count, COLS), f32)
        for tap in range(K):
            glu = glu + kernel_ref[tap : tap + 1, :] * masked_grad_ref[31 - tap : 31 - tap + count, :]
        glu_ref[pl.ds(start, count), :] = glu

    glu = glu_ref[...]
    value_pre = pre_ref[:, 0:COLS]
    gate_pre = pre_ref[:, COLS:]
    gate_sig = jax.nn.sigmoid(gate_pre)
    value_grad = (glu * gate_sig).astype(bf16)
    gate_grad = (glu * value_pre * gate_sig * (1.0 - gate_sig)).astype(bf16)
    message_ref[0:ROWS, 0:COLS] = value_grad
    message_ref[0:ROWS, COLS:] = gate_grad
    value_wide = value_grad.astype(f32)
    gate_wide = gate_grad.astype(f32)
    first = jnp.sum(
        value_wide * unit_ref[0:1, 0:COLS] + gate_wide * unit_ref[0:1, COLS:],
        axis=1,
        keepdims=True,
    )
    second = jnp.sum(value_wide * value_pre + gate_wide * gate_pre, axis=1, keepdims=True)
    rows = columns_to_rows(first, second).astype(bf16)
    message_ref[ROWS : ROWS + 16, :] = rows[:, 0:256]
    message_ref[ROWS + 16 : ROWS + 32, 0:128] = rows[:, 256:384]
    message_ref[ROWS + 16 : ROWS + 32, 128:256] = jnp.zeros((16, 128), bf16)


def norm_kernel(arrive, send, place_ref, g0_ref, g1_ref, g2_ref, g3_ref, weight_ref, out_ref):
    rows = jnp.zeros((16, ROWS), f32)
    arrive(1)
    grads = (g0_ref, g1_ref, g2_ref, g3_ref)
    for grad_ref in grads:
        here = jnp.concatenate(
            [grad_ref[ROWS : ROWS + 16, :], grad_ref[ROWS + 16 : ROWS + 32, 0:128]], axis=1
        )
        rows = rows + here.astype(f32)
    first = rows[0:1] + rows[1:2] + rows[2:3]
    second = rows[3:4] + rows[4:5] + rows[5:6]
    sums = stacked_rows(split3(first) + split3(second)).astype(bf16)
    step = 2 * COLS
    for part in range(QUARTER // step):
        total = jnp.zeros((ROWS, step), f32)
        for j, grad_ref in enumerate(grads):
            start = pl.multiple_of(place_ref[j] * QUARTER + part * step, step)
            weight = weight_ref[pl.ds(start, step), 0 : 2 * COLS]
            total = total + dot(grad_ref[0:ROWS, :], weight, 1, 1)
        for i in (2 * part, 2 * part + 1):
            cut = (i - 2 * part) * COLS
            out_ref[i, 0:ROWS, :] = total[:, cut : cut + COLS].astype(bf16)
            for j in range(3):
                rows_here = sums[:, j * 128 : (j + 1) * 128]
                out_ref[i, ROWS + 16 * j : ROWS + 16 * j + 16, :] = rows_here
            send(0, i)


def weight_kernel(
    place_ref,
    frames_ref,
    gain_ref,
    stat_ref,
    g0_ref,
    g1_ref,
    g2_ref,
    g3_ref,
    kept_ref,
    given_ref,
    left_ref,
    right_ref,
):
    mean = stat_ref[:, 0:1]
    inv_std = stat_ref[:, 1:2]
    half = QUARTER // NK
    for i in range(NZ):
        cut = pl.ds(i * COLS, COLS)
        scaled = (frames_ref[i].astype(f32) - mean) * inv_std * gain_ref[0:1, cut]
        left_ref[i * COLS // half, :, pl.ds(i * COLS % half, COLS)] = scaled.astype(bf16)
    order_blocks(place_ref, 10, (g0_ref, g1_ref, g2_ref, g3_ref), right_ref, 2 * COLS)
    core = place_ref[9]
    for out_ref, which in ((given_ref, 1 - core), (kept_ref, core)):
        out = dot(left_ref[which], right_ref[...], 0, 0).astype(bf16)
        for i in range(NY):
            out_ref[i] = out[:, i * 2 * COLS : (i + 1) * 2 * COLS]


def order_blocks(place_ref, base, sources, out_ref, lanes):
    for i in range(NY):
        source = place_ref[base + i]
        for j, block_ref in enumerate(sources):

            @pl.when(source == j)
            def _(block_ref=block_ref, i=i):
                out_ref[:, i * lanes : (i + 1) * lanes] = block_ref[0:ROWS, :]


def encode_kernel(arrive, send, place_ref, *refs):
    acts, weight_ref, outs = refs[:NZ], refs[NZ], refs[NZ + 1 :]
    arrive(1)
    for j, enc_ref in enumerate(outs):
        total = jnp.zeros((ROWS, COLS), f32)
        for i, act_ref in enumerate(acts):
            start = place_ref[4 + j] * QUARTER + place_ref[14 + i] * COLS
            weight = weight_ref[pl.ds(pl.multiple_of(start, COLS), COLS), 2 * COLS : 3 * COLS]
            total = total + dot(act_ref[...], weight, 1, 0)
        enc_ref[...] = total.astype(bf16)
        send(j)


def out_kernel(place_ref, *refs):
    acts, grads = refs[:NZ], refs[NZ : NZ + NX]
    kept_ref, given_ref, left_ref, grad_ref = refs[NZ + NX :]
    for i, act_ref in enumerate(acts):
        left_ref[place_ref[14 + i]] = act_ref[...]
    order_blocks(place_ref, 0, grads, grad_ref, COLS)
    core = place_ref[9]
    count = NZ // NK
    for out_ref, which in ((given_ref, 1 - core), (kept_ref, core)):
        for m in range(count):
            out = dot(left_ref[which * count + m], grad_ref[...], 0, 0).astype(bf16)
            for i in range(NY):
                out_ref[i, m * COLS : (m + 1) * COLS, :] = out[:, i * COLS : (i + 1) * COLS]


def input_kernel(
    parts_ref,
    frames_ref,
    grad_ref,
    stat_ref,
    gain_ref,
    e0_ref,
    e1_ref,
    e2_ref,
    e3_ref,
    out_ref,
    small_ref,
):
    normed_grad = jnp.zeros((ROWS, COLS), f32)
    rows = jnp.zeros((16, ROWS), f32)
    for i in range(NZ):
        normed_grad = normed_grad + parts_ref[i, 0:ROWS, :].astype(f32)
        here = [parts_ref[i, ROWS + 16 * j : ROWS + 16 * j + 16, :] for j in range(3)]
        rows = rows + jnp.concatenate(here, axis=1).astype(f32)
    first = rows[0:1] + rows[1:2] + rows[2:3]
    second = rows[3:4] + rows[4:5] + rows[5:6]
    sums = stacked_rows(split3(first) + split3(second)).astype(bf16)
    first, second = rows_to_columns(sums)
    mean = stat_ref[:, 0:1]
    inv_std = stat_ref[:, 1:2]
    centred = (frames_ref[...].astype(f32) - mean) * inv_std
    hat = normed_grad * gain_ref[0:1, :]
    out = grad_ref[...].astype(f32) + inv_std * (hat - first / WIDTH - centred * (second / WIDTH))
    out_ref[:, COLS:] = out.astype(bf16)
    encoded = frames_ref[...].astype(f32)
    for part_ref in (e0_ref, e1_ref, e2_ref, e3_ref):
        encoded = encoded + part_ref[...].astype(f32)
    out_ref[:, 0:COLS] = encoded.astype(bf16)
    gain_term = jnp.sum(normed_grad * centred, axis=0, keepdims=True)
    small_ref[...] = jnp.broadcast_to(gain_term, (8, COLS))


def swap_xy(block):
    return lax.ppermute(
        block, ("x", "y"), [(a * NY + b, b * NY + a) for a in range(NX) for b in range(NY)]
    )


def neighbours(upper, lower):
    place = [k * NY + y for y in range(NY) for k in range(NK)]
    forward = list(zip(place[:-1], place[1:]))
    backward = [(target, source) for source, target in forward]
    low = lax.ppermute(upper, ("k", "y"), forward)
    high = lax.ppermute(lower, ("k", "y"), backward)
    return low, high


def exchange(parts, axis):
    return lax.all_to_all(parts, axis, 0, 0, tiled=True)


def gathered(block, axis, count):
    return exchange(jnp.broadcast_to(block[None], (count,) + block.shape), axis)


def shifted(block, axis, count, shift):
    return lax.ppermute(block, axis, [(i, (i + shift) % count) for i in range(count)])


def spread(block, axis, count):
    return [block] + [shifted(block, axis, count, j) for j in range(1, count)]


def reduced(kept, given):
    other = lax.ppermute(given, "k", [(0, 1), (1, 0)])
    both = [(kept[i].astype(f32) + other[i].astype(f32)) for i in range(NY)]
    sent = [part.astype(bf16) for part in both[1:]]
    total = both[0]
    for i in range(1, NY):
        total = total + shifted(sent[i - 1], "y", NY, i).astype(f32)
    return total, sent


def pieces(value):
    out = []
    for _ in range(3):
        piece = lax.reduce_precision(value, 8, 7)
        out.append(piece.astype(bf16))
        value = value - piece
    return jnp.stack(out)


def after(value, *others):
    return lax.optimization_barrier((value,) + others)[0]


def shards(frames, gain, w_value, w_gate, kernel, bias, w_out, grad_out):
    x_index = lax.axis_index("x")
    k_index = lax.axis_index("k")
    row_start = (lax.axis_index("y") * NK + k_index) * ROWS
    col_start = (x_index * NZ + lax.axis_index("z")) * COLS
    local_gain = lax.dynamic_slice_in_dim(gain, col_start, COLS, 0)[None]
    quarter_gain = lax.dynamic_slice_in_dim(gain, x_index * QUARTER, QUARTER, 0)[None]
    y_index = lax.axis_index("y")
    steps = jnp.arange(NX, dtype=jnp.int32)
    below = (x_index + NX - steps) % NX
    above = (x_index + steps) % NX
    distance = (x_index + 2 * NX - (y_index + steps) % NY) % NX
    edges = jnp.stack([LEN - row_start, k_index]).astype(jnp.int32)
    sources = (lax.axis_index("z") + NZ - jnp.arange(NZ, dtype=jnp.int32)) % NZ
    place = jnp.concatenate([below, above, edges, distance, sources]).astype(jnp.int32)
    border = place[8:9]

    weights = lax.all_gather(
        jnp.concatenate([w_value, w_gate, w_out], axis=1), TIME, axis=0, tiled=True
    )

    frames = swap_xy(frames)
    frames_z = gathered(frames, "z", NZ)
    taps = jnp.concatenate([kernel, bias[None, :]], axis=0)
    packed = jnp.concatenate([grad_out, pieces(taps).reshape(3 * (K + 1), COLS)], axis=0)
    packed = swap_xy(packed)
    grad_out = packed[:ROWS]
    grads = spread(grad_out, "x", NX)

    act_parts = call(
        act_kernel, shape((NZ, ROWS, COLS), bf16), (place, *grads, weights), smem=(0,), near=(1, 2, 3, 4, 5)
    )
    act_moved = exchange(act_parts, "z")
    pre_parts = call(
        project_kernel,
        [shape((ROWS + 48, 2 * COLS), bf16) for _ in range(NX)],
        (place, after(frames_z, act_parts), quarter_gain, weights),
        smem=(0,),
        near=(1, 3),
        late=(2,),
        scratch=[pltpu.VMEM((ROWS, QUARTER), bf16)],
    )
    pre_moved = [pre_parts[0]] + [shifted(pre_parts[j], "x", NX, j) for j in range(1, NX)]
    pre, gated, unit, stat = call(
        gate_kernel,
        [
            shape((ROWS, 2 * COLS), f32),
            shape((ROWS, COLS), bf16),
            shape((8, 2 * COLS), f32),
            shape((ROWS, 128), f32),
        ],
        tuple(pre_moved),
        near=(1, 2, 3),
    )
    act_grad = call(sum_kernel, shape((ROWS, COLS), bf16), (act_moved,), near=(0,))
    low, high = neighbours(
        jnp.concatenate([gated[-EDGE:], act_grad[-16:]], axis=0),
        jnp.concatenate([gated[:EDGE], act_grad[:16]], axis=0),
    )
    activated, message, small = call(
        conv_kernel,
        [
            shape((ROWS, COLS), bf16),
            shape((ROWS + 32, 2 * COLS), bf16),
            shape((K + 1, COLS), f32),
        ],
        (border, gated, act_grad, low, high, packed, pre, unit),
        smem=(0,),
        near=(3, 4),
        scratch=[
            pltpu.VMEM((ROWS + 2 * EDGE, COLS), f32),
            pltpu.VMEM((ROWS + 32, COLS), f32),
            pltpu.VMEM((ROWS, COLS), f32),
            pltpu.VMEM((K + 1, 8, COLS), f32),
            pltpu.VMEM((160, COLS), f32),
            pltpu.VMEM((160, COLS), f32),
            pltpu.VMEM((K + 1, COLS), f32),
        ],
    )
    acts = spread(activated, "z", NZ)

    vg_grads = spread(message, "x", NX)
    norm_parts = call(
        norm_kernel,
        shape((NZ, ROWS + 48, COLS), bf16),
        (place, *vg_grads, weights),
        smem=(0,),
        near=(2, 3, 4, 5),
        late=(1,),
    )
    norm_moved = exchange(norm_parts, "z")
    held = lax.optimization_barrier((vg_grads, norm_parts, acts))[0]
    kept, given = call(
        weight_kernel,
        [shape((NY, QUARTER // NK, 2 * COLS), bf16) for _ in range(2)],
        (place, frames_z, quarter_gain, stat, *held),
        smem=(0,),
        near=(5, 6, 7),
        scratch=[
            pltpu.VMEM((NK, ROWS, QUARTER // NK), bf16),
            pltpu.VMEM((ROWS, NY * 2 * COLS), bf16),
        ],
    )
    in_weight, in_sent = reduced(kept, given)

    enc_parts = call(
        encode_kernel,
        [shape((ROWS, COLS), bf16) for _ in range(NX)],
        (place, *acts, after(weights, in_sent)),
        smem=(0,),
        near=(2, 3, 4, 5, 6, 7, 8, 9),
        late=(1,),
    )
    enc = [enc_parts[0]] + [shifted(enc_parts[j], "x", NX, j) for j in range(1, NX)]
    kept, given = call(
        out_kernel,
        [shape((NY, QUARTER // NK, COLS), bf16) for _ in range(2)],
        (place, *acts, *after(grads, enc_parts)),
        smem=(0,),
        near=(2, 3, 4, 5, 6, 7, 8),
        scratch=[
            pltpu.VMEM((NZ, ROWS, COLS), bf16),
            pltpu.VMEM((ROWS, NY * COLS), bf16),
        ],
    )
    other = lax.ppermute(given, "k", [(0, 1), (1, 0)])
    both = (kept.astype(f32) + other.astype(f32)).astype(bf16)
    grad_out_weight = lax.psum_scatter(
        both.reshape(NY * QUARTER // NK, COLS), "y", scatter_dimension=0, tiled=True
    ).astype(f32)

    results, gain_term = call(
        input_kernel,
        [shape((ROWS, 2 * COLS), bf16), shape((8, COLS), f32)],
        (after(norm_moved, both), frames, grad_out, stat, local_gain, *enc),
        near=(0, 6, 7, 8),
    )
    results = swap_xy(results)
    encoded = results[:, :COLS]
    input_grad = results[:, COLS:]

    small = jnp.concatenate([small, gain_term], axis=0)
    small = small + lax.ppermute(small, "k", [(0, 1), (1, 0)])
    arrived = []
    for shift in range(NX):
        route = [
            (a * NY + b, ((b + shift) % NX) * NY + a) for a in range(NX) for b in range(NY)
        ]
        arrived.append(lax.ppermute(small, ("x", "y"), route))
    small = sum(after(arrived, results))
    return (
        encoded,
        input_grad,
        in_weight[:, :COLS],
        in_weight[:, COLS:],
        small[:K],
        small[K],
        grad_out_weight,
        small[K + 1],
    )


def solution(mesh):
    fine = Mesh(mesh.devices.reshape(NX, NK, NY, NZ), ("x", "k", "y", "z"))
    both = P(ROW, COL)
    return jax.shard_map(
        shards,
        mesh=fine,
        in_specs=(both, P(), both, both, P(None, COL), P(COL), both, both),
        out_specs=(both, both, both, both, P(None, COL), P(COL), both, P(COL)),
        check_vma=False,
    )
```

```python
import jax
import jax.numpy as jnp
from jax import lax
from jax.experimental import pallas as pl
from jax.experimental.pallas import tpu as pltpu
from jax.sharding import Mesh, PartitionSpec as P

K = 31
LEN = 2048
HALF = K // 2
NX, NK, NY, NZ = 4, 2, 4, 8
ROW = ("x", "k")
COL = ("y", "z")
TIME = ("y", "k")
ROWS = 384
COLS = 128
QUARTER = COLS * NZ
WIDTH = QUARTER * NX
EDGE = 32
IN = (0, 2 * COLS)
OUT = (2 * COLS, COLS)

epsilon = 1e-05
f32 = jnp.float32
bf16 = jnp.bfloat16


def dot(left, right, left_dim, right_dim):
    return lax.dot_general(
        left, right, (((left_dim,), (right_dim,)), ((), ())), preferred_element_type=f32
    )


def split3(value):
    high = value.astype(bf16)
    rest = value - high.astype(f32)
    middle = rest.astype(bf16)
    low = (rest - middle.astype(f32)).astype(bf16)
    return high, middle, low


def one_hot():
    lane = lax.broadcasted_iota(jnp.int32, (16, 128), 1)
    row = lax.broadcasted_iota(jnp.int32, (16, 128), 0)
    return jnp.where(lane == row, 1.0, 0.0).astype(bf16)


def columns_to_rows(first, second):
    lane = lax.broadcasted_iota(jnp.int32, (first.shape[0], 128), 1)
    grid = jnp.zeros((first.shape[0], 128), f32)
    for j, piece in enumerate(split3(first) + split3(second)):
        grid = jnp.where(lane == j, piece.astype(f32), grid)
    return dot(one_hot(), grid.astype(bf16), 1, 1)


def rows_to_columns(rows):
    grid = dot(rows, one_hot(), 0, 0)
    first = grid[:, 0:1] + grid[:, 1:2] + grid[:, 2:3]
    second = grid[:, 3:4] + grid[:, 4:5] + grid[:, 5:6]
    return first, second


def stacked_rows(values):
    row = lax.broadcasted_iota(jnp.int32, (16, values[0].shape[1]), 0)
    out = jnp.zeros((16, values[0].shape[1]), f32)
    for j, value in enumerate(values):
        out = jnp.where(row == j, value.astype(f32), out)
    return out


def call(body, out_shape, args, smem=(), near=(), late=(), scratch=(), cuts=()):
    cuts = dict(cuts)
    single = not isinstance(out_shape, (list, tuple))
    outs = [out_shape] if single else list(out_shape)
    count = len(args)
    moved = [i for i in range(count) if i not in smem and i not in near]
    buffers = []
    for i in moved:
        dims = args[i].shape
        if i in cuts:
            dims = (dims[0], cuts[i][1])
        buffers.append(pltpu.VMEM(dims, args[i].dtype))
    for out in outs:
        buffers.append(pltpu.VMEM(out.shape, out.dtype))

    def whole(*refs):
        refs = list(refs)
        inputs, refs = refs[:count], refs[count:]
        results, refs = refs[: len(outs)], refs[len(outs) :]
        held, refs = refs[: len(buffers)], refs[len(buffers) :]
        sems, extra = refs[0], refs[1:]
        copies = {}
        for place, i in enumerate(moved):
            source = inputs[i]
            if i in cuts:
                source = source.at[:, pl.ds(cuts[i][0], cuts[i][1])]
            copies[i] = pltpu.make_async_copy(source, held[place], sems.at[place])
            inputs[i] = held[place]
        for copy in copies.values():
            copy.start()
        for i, copy in copies.items():
            if i not in late:
                copy.wait()
        sent = []

        def send(j, part=None):
            source, target = held[len(moved) + j], results[j]
            if part is not None:
                source, target = source.at[part], target.at[part]
            copy = pltpu.make_async_copy(source, target, sems.at[len(moved) + len(sent)])
            copy.start()
            sent.append((j, copy))

        hooks = (lambda i: copies[i].wait(), send) if late else ()
        body(*hooks, *inputs, *held[len(moved) :], *extra)
        already = {j for j, _ in sent}
        for j in range(len(outs)):
            if j not in already:
                send(j)
        for _, copy in sent:
            copy.wait()

    hbm = pl.BlockSpec(memory_space=pltpu.MemorySpace.HBM)
    spaces = [
        pltpu.MemorySpace.SMEM
        if i in smem
        else (pltpu.MemorySpace.VMEM if i in near else pltpu.MemorySpace.HBM)
        for i in range(count)
    ]
    made = pl.pallas_call(
        whole,
        out_shape=[pltpu.HBM(out.shape, out.dtype) for out in outs],
        in_specs=[pl.BlockSpec(memory_space=space) for space in spaces],
        out_specs=[hbm] * len(outs),
        scratch_shapes=buffers + [pltpu.SemaphoreType.DMA((len(moved) + max(len(outs), NZ),))] + list(scratch),
        compiler_params=pltpu.CompilerParams(vmem_limit_bytes=24 * 1024 * 1024),
        name=body.__name__,
    )(
        *[
            pltpu.with_memory_space_constraint(arg, pltpu.HBM) if i in moved else arg
            for i, arg in enumerate(args)
        ]
    )
    return made[0] if single else made


def shape(dims, kind):
    return jax.ShapeDtypeStruct(dims, kind)


def project_kernel(arrive, send, place_ref, frames_ref, gain_ref, gain_rows_ref, weight_ref, *refs):
    left_ref = refs[NX]
    total = jnp.zeros((ROWS, 1), f32)
    square = jnp.zeros((ROWS, 1), f32)
    for i in range(NZ):
        wide = frames_ref[i].astype(f32)
        total = total + jnp.sum(wide, axis=1, keepdims=True)
        square = square + jnp.sum(wide * wide, axis=1, keepdims=True)
    mean = total / QUARTER
    arrive(2)
    arrive(3)
    for i in range(NZ):
        cut = pl.ds(i * COLS, COLS)
        scaled = (frames_ref[i].astype(f32) - mean) * gain_ref[0:1, cut]
        left_ref[:, cut] = scaled.astype(bf16)
    sums = columns_to_rows(total, square).astype(bf16)
    for j, out_ref in enumerate(refs[:NX]):
        start = pl.multiple_of(place_ref[4 + j] * QUARTER, QUARTER)
        weight = weight_ref[pl.ds(start, QUARTER), 0 : 2 * COLS]
        out_ref[0:ROWS, :] = dot(left_ref[...], weight, 1, 0).astype(bf16)
        unit = jnp.sum(dot(gain_rows_ref[...], weight, 1, 0), axis=0, keepdims=True)
        out_ref[ROWS : ROWS + 16, :] = stacked_rows(split3(unit)).astype(bf16)
        out_ref[ROWS + 16 : ROWS + 32, :] = sums[:, 0:256]
        out_ref[ROWS + 32 : ROWS + 48, 0:128] = sums[:, 256:384]
        out_ref[ROWS + 32 : ROWS + 48, 128:256] = jnp.zeros((16, 128), bf16)
        send(j)


def gate_kernel(p0_ref, p1_ref, p2_ref, p3_ref, pre_ref, gated_ref, unit_ref, stat_ref):
    parts = (p0_ref, p1_ref, p2_ref, p3_ref)
    totals, squares, units = [], [], []
    for part_ref in parts:
        rows = jnp.concatenate(
            [part_ref[ROWS + 16 : ROWS + 32, :], part_ref[ROWS + 32 : ROWS + 48, 0:128]], axis=1
        )
        first, second = rows_to_columns(rows)
        totals.append(first)
        squares.append(second)
        pieces = part_ref[ROWS : ROWS + 16, :].astype(f32)
        units.append(jnp.sum(pieces, axis=0, keepdims=True))
    mean = sum(totals) / WIDTH
    inv_std = lax.rsqrt(sum(squares) / WIDTH - mean * mean + epsilon)
    pre = jnp.zeros((ROWS, 2 * COLS), f32)
    for i, part_ref in enumerate(parts):
        pre = pre + part_ref[0:ROWS, :].astype(f32)
        pre = pre + (totals[i] / QUARTER - mean) * units[i]
    pre = pre * inv_std
    pre_ref[...] = pre
    gated_ref[...] = (pre[:, 0:COLS] * jax.nn.sigmoid(pre[:, COLS:])).astype(bf16)
    unit_ref[...] = jnp.broadcast_to(sum(units), (8, 2 * COLS))
    lane = lax.broadcasted_iota(jnp.int32, (ROWS, 128), 1)
    stat_ref[...] = jnp.where(lane == 0, mean, inv_std)


def act_kernel(place_ref, g0_ref, g1_ref, g2_ref, g3_ref, weight_ref, out_ref):
    total = jnp.zeros((ROWS, QUARTER), f32)
    for j, grad_ref in enumerate((g0_ref, g1_ref, g2_ref, g3_ref)):
        start = pl.multiple_of(place_ref[j] * QUARTER, QUARTER)
        weight = weight_ref[pl.ds(start, QUARTER), 2 * COLS : 3 * COLS]
        total = total + dot(grad_ref[...], weight, 1, 1)
    for i in range(NZ):
        out_ref[i] = total[:, i * COLS : (i + 1) * COLS].astype(bf16)


def sum_kernel(parts_ref, out_ref):
    total = jnp.zeros((ROWS, COLS), f32)
    for i in range(NZ):
        total = total + parts_ref[i].astype(f32)
    out_ref[...] = total.astype(bf16)


CHUNKS = [(-16, 16), (0, 128), (128, 128), (256, 128), (ROWS, 16)]


def same_clip(border, start, count):
    row = lax.broadcasted_iota(jnp.int32, (count + 32, COLS), 0) + (start - 16)
    inside = (row < border).astype(jnp.int32)
    own = jnp.where(start < border, 1, 0)
    return inside == own


def conv_kernel(
    place_ref,
    gated_ref,
    act_ref,
    low_ref,
    high_ref,
    taps_ref,
    pre_ref,
    unit_ref,
    activated_ref,
    message_ref,
    small_ref,
    wide_ref,
    grad_ref,
    glu_ref,
    sums_ref,
    masked_ref,
    masked_grad_ref,
    kernel_ref,
):
    border = place_ref[0]
    total = jnp.zeros((K + 1, COLS), f32)
    for i in range(3):
        total = total + taps_ref[pl.ds(ROWS + i * (K + 1), K + 1), :].astype(f32)
    kernel_ref[...] = total
    wide_ref[0:EDGE, :] = low_ref[0:EDGE, :].astype(f32)
    wide_ref[EDGE : EDGE + ROWS, :] = gated_ref[...].astype(f32)
    wide_ref[EDGE + ROWS :, :] = high_ref[0:EDGE, :].astype(f32)
    sums_ref[...] = jnp.zeros((K + 1, 8, COLS), f32)
    bias = kernel_ref[K : K + 1, :]
    for start, count in CHUNKS:
        here = wide_ref[pl.ds(start - 16 + EDGE, count + 32), :]
        masked_ref[0 : count + 32, :] = jnp.where(same_clip(border, start, count), here, 0.0)
        conv = jnp.broadcast_to(bias, (count, COLS))
        for tap in range(K):
            conv = conv + kernel_ref[tap : tap + 1, :] * masked_ref[1 + tap : 1 + tap + count, :]
        sig = jax.nn.sigmoid(conv)
        if start < 0:
            act = low_ref[EDGE:, :]
        elif start < ROWS:
            act = act_ref[pl.ds(start, count), :]
        else:
            act = high_ref[EDGE:, :]
        grad = (act.astype(f32) * sig * (1.0 + conv * (1.0 - sig))).astype(bf16).astype(f32)
        grad_ref[pl.ds(start + 16, count), :] = grad
        if 0 <= start < ROWS:
            activated = (conv * sig).astype(bf16)
            for i in range(NZ):
                activated_ref[i, pl.ds(start, count), :] = activated
            for tap in range(K):
                product = grad * masked_ref[1 + tap : 1 + tap + count, :]
                sums_ref[tap] += jnp.sum(product.reshape(count // 8, 8, COLS), axis=0)
            sums_ref[K] += jnp.sum(grad.reshape(count // 8, 8, COLS), axis=0)
    small_ref[...] = jnp.sum(sums_ref[...], axis=1)

    for start, count in CHUNKS[1:4]:
        here = grad_ref[pl.ds(start, count + 32), :]
        masked_grad_ref[...] = jnp.where(same_clip(border, start, count), here, 0.0)
        glu = jnp.zeros((count, COLS), f32)
        for tap in range(K):
            glu = glu + kernel_ref[tap : tap + 1, :] * masked_grad_ref[31 - tap : 31 - tap + count, :]
        glu_ref[pl.ds(start, count), :] = glu

    glu = glu_ref[...]
    value_pre = pre_ref[:, 0:COLS]
    gate_pre = pre_ref[:, COLS:]
    gate_sig = jax.nn.sigmoid(gate_pre)
    value_grad = (glu * gate_sig).astype(bf16)
    gate_grad = (glu * value_pre * gate_sig * (1.0 - gate_sig)).astype(bf16)
    message_ref[0:ROWS, 0:COLS] = value_grad
    message_ref[0:ROWS, COLS:] = gate_grad
    value_wide = value_grad.astype(f32)
    gate_wide = gate_grad.astype(f32)
    first = jnp.sum(
        value_wide * unit_ref[0:1, 0:COLS] + gate_wide * unit_ref[0:1, COLS:],
        axis=1,
        keepdims=True,
    )
    second = jnp.sum(value_wide * value_pre + gate_wide * gate_pre, axis=1, keepdims=True)
    rows = columns_to_rows(first, second).astype(bf16)
    message_ref[ROWS : ROWS + 16, :] = rows[:, 0:256]
    message_ref[ROWS + 16 : ROWS + 32, 0:128] = rows[:, 256:384]
    message_ref[ROWS + 16 : ROWS + 32, 128:256] = jnp.zeros((16, 128), bf16)


def norm_kernel(arrive, send, place_ref, g0_ref, g1_ref, g2_ref, g3_ref, weight_ref, out_ref):
    rows = jnp.zeros((16, ROWS), f32)
    arrive(1)
    grads = (g0_ref, g1_ref, g2_ref, g3_ref)
    for grad_ref in grads:
        here = jnp.concatenate(
            [grad_ref[ROWS : ROWS + 16, :], grad_ref[ROWS + 16 : ROWS + 32, 0:128]], axis=1
        )
        rows = rows + here.astype(f32)
    first = rows[0:1] + rows[1:2] + rows[2:3]
    second = rows[3:4] + rows[4:5] + rows[5:6]
    sums = stacked_rows(split3(first) + split3(second)).astype(bf16)
    step = 2 * COLS
    for part in range(QUARTER // step):
        total = jnp.zeros((ROWS, step), f32)
        for j, grad_ref in enumerate(grads):
            start = pl.multiple_of(place_ref[j] * QUARTER + part * step, step)
            weight = weight_ref[pl.ds(start, step), 0 : 2 * COLS]
            total = total + dot(grad_ref[0:ROWS, :], weight, 1, 1)
        for i in (2 * part, 2 * part + 1):
            cut = (i - 2 * part) * COLS
            out_ref[i, 0:ROWS, :] = total[:, cut : cut + COLS].astype(bf16)
            for j in range(3):
                rows_here = sums[:, j * 128 : (j + 1) * 128]
                out_ref[i, ROWS + 16 * j : ROWS + 16 * j + 16, :] = rows_here
            send(0, i)


def weight_kernel(
    place_ref,
    frames_ref,
    gain_ref,
    stat_ref,
    g0_ref,
    g1_ref,
    g2_ref,
    g3_ref,
    out_ref,
    left_ref,
):
    mean = stat_ref[:, 0:1]
    inv_std = stat_ref[:, 1:2]
    for i in range(NZ):
        cut = pl.ds(i * COLS, COLS)
        scaled = (frames_ref[i].astype(f32) - mean) * inv_std * gain_ref[0:1, cut]
        left_ref[:, cut] = scaled.astype(bf16)
    for j, grad_ref in enumerate((g0_ref, g1_ref, g2_ref, g3_ref)):
        start = pl.multiple_of(place_ref[j] * QUARTER, QUARTER)
        out = dot(left_ref[...], grad_ref[0:ROWS, :], 0, 0)
        out_ref[pl.ds(start, QUARTER), :] = out.astype(bf16)


def order_blocks(place_ref, base, sources, out_ref, lanes):
    for i in range(NY):
        source = place_ref[base + i]
        for j, block_ref in enumerate(sources):

            @pl.when(source == j)
            def _(block_ref=block_ref, i=i):
                out_ref[:, i * lanes : (i + 1) * lanes] = block_ref[0:ROWS, :]


def out_kernel(place_ref, act_ref, g0_ref, g1_ref, g2_ref, g3_ref, weight_ref, *refs):
    enc_refs = refs[:NX]
    kept_ref, given_ref, left_ref, grad_ref = refs[NX:]
    half = QUARTER // NK
    for i in range(NZ):
        left_ref[i * COLS // half, :, pl.ds(i * COLS % half, COLS)] = act_ref[i, 0:ROWS, :]
    for j, enc_ref in enumerate(enc_refs):
        total = jnp.zeros((ROWS, COLS), f32)
        for h in range(NK):
            start = pl.multiple_of(place_ref[4 + j] * QUARTER + h * half, half)
            weight = weight_ref[pl.ds(start, half), 2 * COLS : 3 * COLS]
            total = total + dot(left_ref[h], weight, 1, 0)
        enc_ref[...] = total.astype(bf16)
    order_blocks(place_ref, 10, (g0_ref, g1_ref, g2_ref, g3_ref), grad_ref, COLS)
    core = place_ref[9]
    for out_ref, which in ((given_ref, 1 - core), (kept_ref, core)):
        out = dot(left_ref[which], grad_ref[...], 0, 0).astype(bf16)
        for i in range(NY):
            out_ref[i] = out[:, i * COLS : (i + 1) * COLS]


def input_kernel(
    parts_ref,
    frames_ref,
    grad_ref,
    stat_ref,
    gain_ref,
    e0_ref,
    e1_ref,
    e2_ref,
    e3_ref,
    out_ref,
    small_ref,
):
    normed_grad = jnp.zeros((ROWS, COLS), f32)
    rows = jnp.zeros((16, ROWS), f32)
    for i in range(NZ):
        normed_grad = normed_grad + parts_ref[i, 0:ROWS, :].astype(f32)
        here = [parts_ref[i, ROWS + 16 * j : ROWS + 16 * j + 16, :] for j in range(3)]
        rows = rows + jnp.concatenate(here, axis=1).astype(f32)
    first = rows[0:1] + rows[1:2] + rows[2:3]
    second = rows[3:4] + rows[4:5] + rows[5:6]
    sums = stacked_rows(split3(first) + split3(second)).astype(bf16)
    first, second = rows_to_columns(sums)
    mean = stat_ref[:, 0:1]
    inv_std = stat_ref[:, 1:2]
    centred = (frames_ref[...].astype(f32) - mean) * inv_std
    hat = normed_grad * gain_ref[0:1, :]
    out = grad_ref[...].astype(f32) + inv_std * (hat - first / WIDTH - centred * (second / WIDTH))
    out_ref[:, COLS:] = out.astype(bf16)
    encoded = frames_ref[...].astype(f32)
    for part_ref in (e0_ref, e1_ref, e2_ref, e3_ref):
        encoded = encoded + part_ref[...].astype(f32)
    out_ref[:, 0:COLS] = encoded.astype(bf16)
    gain_term = jnp.sum(normed_grad * centred, axis=0, keepdims=True)
    small_ref[...] = jnp.broadcast_to(gain_term, (8, COLS))


def swap_xy(block):
    return lax.ppermute(
        block, ("x", "y"), [(a * NY + b, b * NY + a) for a in range(NX) for b in range(NY)]
    )


def neighbours(upper, lower):
    place = [k * NY + y for y in range(NY) for k in range(NK)]
    forward = list(zip(place[:-1], place[1:]))
    backward = [(target, source) for source, target in forward]
    low = lax.ppermute(upper, ("k", "y"), forward)
    high = lax.ppermute(lower, ("k", "y"), backward)
    return low, high


def exchange(parts, axis):
    return lax.all_to_all(parts, axis, 0, 0, tiled=True)


def gathered(block, axis, count):
    return exchange(jnp.broadcast_to(block[None], (count,) + block.shape), axis)


def shifted(block, axis, count, shift):
    return lax.ppermute(block, axis, [(i, (i + shift) % count) for i in range(count)])


def spread(block, axis, count):
    return [block] + [shifted(block, axis, count, j) for j in range(1, count)]


def reduced(kept, given):
    other = lax.ppermute(given, "k", [(0, 1), (1, 0)])
    both = [(kept[i].astype(f32) + other[i].astype(f32)) for i in range(NY)]
    total = both[0]
    for i in range(1, NY):
        total = total + shifted(both[i].astype(bf16), "y", NY, i).astype(f32)
    return total


def pieces(value):
    out = []
    for _ in range(3):
        piece = lax.reduce_precision(value, 8, 7)
        out.append(piece.astype(bf16))
        value = value - piece
    return jnp.stack(out)


def after(value, *others):
    return lax.optimization_barrier((value,) + others)[0]


def shards(frames, gain, w_value, w_gate, kernel, bias, w_out, grad_out):
    x_index = lax.axis_index("x")
    k_index = lax.axis_index("k")
    row_start = (lax.axis_index("y") * NK + k_index) * ROWS
    col_start = (x_index * NZ + lax.axis_index("z")) * COLS
    local_gain = lax.dynamic_slice_in_dim(gain, col_start, COLS, 0)[None]
    quarter_gain = lax.dynamic_slice_in_dim(gain, x_index * QUARTER, QUARTER, 0)[None]
    gain_rows = jnp.pad(pieces(quarter_gain)[:, 0], ((0, 13), (0, 0)))
    y_index = lax.axis_index("y")
    steps = jnp.arange(NX, dtype=jnp.int32)
    below = (x_index + NX - steps) % NX
    above = (x_index + steps) % NX
    distance = (x_index + 2 * NX - (y_index + steps) % NY) % NX
    edges = jnp.stack([LEN - row_start, k_index]).astype(jnp.int32)
    place = jnp.concatenate([below, above, edges, distance]).astype(jnp.int32)
    border = place[8:9]

    weights = lax.all_gather(
        jnp.concatenate([w_value, w_gate, w_out], axis=1), TIME, axis=0, tiled=True
    )

    frames = swap_xy(frames)
    frames_z = gathered(frames, "z", NZ)
    taps = jnp.concatenate([kernel, bias[None, :]], axis=0)
    packed = jnp.concatenate([grad_out, pieces(taps).reshape(3 * (K + 1), COLS)], axis=0)
    packed = swap_xy(packed)
    grad_out = packed[:ROWS]
    grads = spread(grad_out, "x", NX)

    act_parts = call(
        act_kernel, shape((NZ, ROWS, COLS), bf16), (place, *grads, weights), smem=(0,), near=(1, 2, 3, 4, 5)
    )
    act_moved = exchange(act_parts, "z")
    pre_parts = call(
        project_kernel,
        [shape((ROWS + 48, 2 * COLS), bf16) for _ in range(NX)],
        (place, after(frames_z, act_parts), quarter_gain, gain_rows, weights),
        smem=(0,),
        near=(1, 4),
        late=(2, 3),
        scratch=[pltpu.VMEM((ROWS, QUARTER), bf16)],
    )
    pre_moved = [pre_parts[0]] + [shifted(pre_parts[j], "x", NX, j) for j in range(1, NX)]
    pre, gated, unit, stat = call(
        gate_kernel,
        [
            shape((ROWS, 2 * COLS), f32),
            shape((ROWS, COLS), bf16),
            shape((8, 2 * COLS), f32),
            shape((ROWS, 128), f32),
        ],
        tuple(pre_moved),
        near=(1, 2, 3),
    )
    act_grad = call(sum_kernel, shape((ROWS, COLS), bf16), (act_moved,), near=(0,))
    low, high = neighbours(
        jnp.concatenate([gated[-EDGE:], act_grad[-16:]], axis=0),
        jnp.concatenate([gated[:EDGE], act_grad[:16]], axis=0),
    )
    activated, message, small = call(
        conv_kernel,
        [
            shape((NZ, ROWS, COLS), bf16),
            shape((ROWS + 32, 2 * COLS), bf16),
            shape((K + 1, COLS), f32),
        ],
        (border, gated, act_grad, low, high, packed, pre, unit),
        smem=(0,),
        near=(3, 4),
        scratch=[
            pltpu.VMEM((ROWS + 2 * EDGE, COLS), f32),
            pltpu.VMEM((ROWS + 32, COLS), f32),
            pltpu.VMEM((ROWS, COLS), f32),
            pltpu.VMEM((K + 1, 8, COLS), f32),
            pltpu.VMEM((160, COLS), f32),
            pltpu.VMEM((160, COLS), f32),
            pltpu.VMEM((K + 1, COLS), f32),
        ],
    )
    act_z = exchange(activated, "z")

    vg_grads = spread(message, "x", NX)
    norm_parts = call(
        norm_kernel,
        shape((NZ, ROWS + 48, COLS), bf16),
        (place, *vg_grads, after(weights, act_z)),
        smem=(0,),
        near=(2, 3, 4, 5),
        late=(1,),
    )
    norm_moved = exchange(norm_parts, "z")
    held = lax.optimization_barrier((vg_grads, norm_parts))[0]
    weight_parts = call(
        weight_kernel,
        shape((NY * QUARTER, 2 * COLS), bf16),
        (place, frames_z, quarter_gain, stat, *held),
        smem=(0,),
        near=(5, 6, 7),
        scratch=[pltpu.VMEM((ROWS, QUARTER), bf16)],
    )
    in_weight = lax.psum_scatter(
        weight_parts, TIME, scatter_dimension=0, tiled=True
    ).astype(f32)

    out_parts = call(
        out_kernel,
        [shape((ROWS, COLS), bf16) for _ in range(NX)]
        + [shape((NY, QUARTER // NK, COLS), bf16) for _ in range(2)],
        (place, act_z, *after(grads, norm_parts), weights),
        smem=(0,),
        near=(1, 6),
        scratch=[
            pltpu.VMEM((NK, ROWS, QUARTER // NK), bf16),
            pltpu.VMEM((ROWS, NY * COLS), bf16),
        ],
    )
    grad_out_weight = reduced(*out_parts[NX:])
    enc = [out_parts[0]] + [shifted(out_parts[j], "x", NX, j) for j in range(1, NX)]

    results, gain_term = call(
        input_kernel,
        [shape((ROWS, 2 * COLS), bf16), shape((8, COLS), f32)],
        (norm_moved, frames, grad_out, stat, local_gain, *enc),
        near=(0, 6, 7, 8),
    )
    results = swap_xy(results)
    encoded = results[:, :COLS]
    input_grad = results[:, COLS:]

    small = jnp.concatenate([small, gain_term], axis=0)
    small = small + lax.ppermute(small, "k", [(0, 1), (1, 0)])
    arrived = []
    for shift in range(NX):
        route = [
            (a * NY + b, ((b + shift) % NX) * NY + a) for a in range(NX) for b in range(NY)
        ]
        arrived.append(lax.ppermute(small, ("x", "y"), route))
    small = sum(after(arrived, results))
    return (
        encoded,
        input_grad,
        in_weight[:, :COLS],
        in_weight[:, COLS:],
        small[:K],
        small[K],
        grad_out_weight,
        small[K + 1],
    )


def solution(mesh):
    fine = Mesh(mesh.devices.reshape(NX, NK, NY, NZ), ("x", "k", "y", "z"))
    both = P(ROW, COL)
    return jax.shard_map(
        shards,
        mesh=fine,
        in_specs=(both, P(), both, both, P(None, COL), P(COL), both, both),
        out_specs=(both, both, both, both, P(None, COL), P(COL), both, P(COL)),
        check_vma=False,
    )
```
